32 devices in a mesh: dp: 4 (over y, x), fsdp: 4 (over z), ctx: 2 (over core).
Axes of the slice: x: 2, y: 2, z: 4, core: 2. Of those that a mesh axis runs over, the one named last changes fastest.
Arguments:
- inputs: bfloat16 [16, 1024, 1024], P(('dp', 'fsdp'), 'ctx'), may hold values from -6 to 6
- lengths: int32 [16], P(('dp', 'fsdp')), may hold values from 256 to 1024, as said below
- cotangent: bfloat16 [16, 1024, 1024], P(('dp', 'fsdp'), 'ctx'), may hold values from -6 to 6
- norm_gain1: float32 [1024], replicated, may hold values from 0.5 to 1.5
- w_qkv: bfloat16 [1024, 3072], P('fsdp'), may hold values from -0.1875 to 0.1875
- w_beta: bfloat16 [1024, 8], P('fsdp'), may hold values from -0.1875 to 0.1875
- conv_weight: float32 [4, 3072], replicated, may hold values from -3 to 3
- head_gain: float32 [128], replicated, may hold values from 0.5 to 1.5
- w_out: bfloat16 [1024, 1024], P('fsdp'), may hold values from -0.1875 to 0.1875
- norm_gain2: float32 [1024], replicated, may hold values from 0.5 to 1.5
- w_gateup: bfloat16 [1024, 5632], P('fsdp'), may hold values from -0.1875 to 0.1875
- w_down: bfloat16 [2816, 1024], P('fsdp'), may hold values from -0.109375 to 0.109375
Outputs:
- output: bfloat16 [16, 1024, 1024], P(('dp', 'fsdp'), 'ctx')
- grad_inputs: bfloat16 [16, 1024, 1024], P(('dp', 'fsdp'), 'ctx')
- grad_gain1: float32 [1024], replicated
- grad_qkv: float32 [1024, 3072], P(('fsdp', 'ctx'))
- grad_beta: float32 [1024, 8], P(('fsdp', 'ctx'))
- grad_conv: float32 [4, 3072], replicated
- grad_head_gain: float32 [128], replicated
- grad_out: float32 [1024, 1024], P(('fsdp', 'ctx'))
- grad_gain2: float32 [1024], replicated
- grad_gateup: float32 [1024, 5632], P(('fsdp', 'ctx'))
- grad_down: float32 [2816, 1024], P(('fsdp', 'ctx'))
The draws below stay inside these ranges and needn't reach their ends.
Inputs may be any that keep to these rules, and one draw needn't show every extreme that they name: `lengths`: valid tokens of each sequence; they come first in it. Some sequence has all 1024 positions valid and some sequence has 256.
All inputs are finite; a program needn't handle non-finite values.
Results may differ from the reference program's by a relative error of at most 0.014.
Values may be sent and summed in bfloat16 or wider, within the bound.
No kernel may reach another device: no remote copies, remote signals or barrier semaphores. Data moves between devices by JAX's collectives and lax.ppermute only.
A program may use at most 256 MiB of HBM per device.

```python
import jax
import jax.numpy as jnp
from jax import lax

D = 1024
H = 8
HD = 128
FF = 2816
KERNEL = 4
SPAN = 64
LEN = 1024
SEQS = 16


def draw_lengths(key, part):
    first_key, second_key = jax.random.split(jax.random.fold_in(key, 17))
    values = jax.random.randint(first_key, (SEQS,), LEN // 4, LEN + 1)
    order = jax.random.permutation(second_key, SEQS)
    values = values.at[order[0]].set(LEN)
    values = values.at[order[1]].set(LEN // 4)
    return values.astype(jnp.int32)


def levels(key, dims, shards, low, top_value):
    def one(dim, blocks):
        draws = jax.random.uniform(jax.random.fold_in(jax.random.fold_in(key, 6), dim), (blocks,), jnp.float32, low / len(shards), top_value / len(shards))
        return jnp.repeat(jnp.exp(draws), dims[dim] // blocks).reshape((-1,) + (1,) * (len(dims) - dim - 1))

    level = one(*shards[0])
    for cut in shards[1:]:
        level = level * one(*cut)
    return level


def gaussian(rng, shape, width, limit, pieces=(), held_as=jnp.bfloat16):
    entries = width * jax.random.normal(rng, shape, jnp.float32)
    if pieces:
        entries = entries * levels(rng, shape, pieces, -0.22, 0.18)
    return jnp.clip(entries, -limit, limit).astype(held_as)


def setup_inputs(seed: int = 0) -> dict:
    seeds = jax.random.split(jax.random.key(seed), 13)
    return {
        "inputs": gaussian(seeds[0], (SEQS, LEN, D), 1.0, 6.0, ((0, 16), (1, 2))),
        "lengths": draw_lengths(jax.random.fold_in(seeds[12], 71), 0),
        "cotangent": gaussian(seeds[2], (SEQS, LEN, D), 1.0, 6.0, ((0, 16), (1, 2))),
        "norm_gain1": jnp.clip(1.0 + 0.1 * jax.random.normal(seeds[3], (D,), jnp.float32), 0.5, 1.5),
        "w_qkv": gaussian(seeds[4], (D, 3 * D), D ** -0.5, 0.1875, ((0, 4),)),
        "w_beta": gaussian(seeds[5], (D, H), D ** -0.5, 0.1875, ((0, 4),)),
        "conv_weight": gaussian(seeds[6], (KERNEL, 3 * D), 0.5, 3.0, (), jnp.float32),
        "head_gain": jnp.clip(1.0 + 0.1 * jax.random.normal(seeds[7], (HD,), jnp.float32), 0.5, 1.5),
        "w_out": gaussian(seeds[8], (D, D), D ** -0.5, 0.1875, ((0, 4),)),
        "norm_gain2": jnp.clip(1.0 + 0.1 * jax.random.normal(seeds[9], (D,), jnp.float32), 0.5, 1.5),
        "w_gateup": gaussian(seeds[10], (D, 2 * FF), D ** -0.5, 0.1875, ((0, 4),)),
        "w_down": gaussian(seeds[11], (FF, D), FF ** -0.5, 0.109375, ((0, 4),)),
    }


exact_precision = lax.Precision.HIGHEST

@jax.custom_vjp
def low(v):
    return lax.optimization_barrier(v.astype(jnp.bfloat16)).astype(jnp.float32)

@jax.custom_vjp
def low_back(v):
    return v

def low_keep(v):
    return (low(v), None)

def low_pass(kept, grad):
    return (grad,)

def back_keep(v):
    return (v, None)

def back_low(kept, grad):
    return (low(grad),)
low.defvjp(low_keep, low_pass)
low_back.defvjp(back_keep, back_low)

def span_factors(key_row_block, value_rows, strength):
    block_len = key_row_block.shape[1]
    head_width = key_row_block.shape[2]
    gram_matrix = jnp.einsum('hik,hjk->hij', key_row_block, key_row_block, precision=exact_precision)
    system = jnp.tril(gram_matrix * strength[:, :, None], -1) + jnp.eye(block_len, dtype=key_row_block.dtype)
    right_side = strength[:, :, None] * jnp.concatenate([key_row_block, value_rows], -1)
    solved = jax.scipy.linalg.solve_triangular(system, right_side, lower=True, unit_diagonal=True)
    return (solved[..., :head_width], solved[..., head_width:])

def span_output(memory_matrix, blocks):
    query_rows, key_row_block, value_rows, strength = blocks
    key_blend, value_blend = span_factors(key_row_block, value_rows, strength)
    prediction_error = value_blend - jnp.einsum('ist,itn->isn', key_blend, memory_matrix, precision=exact_precision)
    scores = jnp.tril(jnp.einsum('hik,hjk->hij', query_rows, key_row_block, precision=exact_precision))
    final_result = jnp.einsum('ist,itn->isn', query_rows, memory_matrix, precision=exact_precision)
    final_result = final_result + jnp.einsum('hij,hjv->hiv', scores, prediction_error, precision=exact_precision)
    updated_memory = memory_matrix + jnp.einsum('xzn,xzf->xnf', key_row_block, prediction_error, precision=exact_precision)
    return (updated_memory, final_result)

def to_blocks(tensor):
    shape_now = tensor.shape
    grouped = tensor.reshape((shape_now[0], shape_now[1] // SPAN, SPAN) + shape_now[2:])
    return jnp.moveaxis(grouped, 1, 0)

def from_blocks(tensor):
    moved = jnp.moveaxis(tensor, 0, 1)
    return moved.reshape((moved.shape[0], moved.shape[1] * moved.shape[2]) + moved.shape[3:])

def delta_rule(query_rows, key_row_block, value_rows, strength):
    head_count, length_all, head_width = key_row_block.shape
    memory_matrix = jnp.zeros((head_count, head_width, head_width), key_row_block.dtype)
    blocks = (to_blocks(query_rows), to_blocks(key_row_block), to_blocks(value_rows), to_blocks(strength))
    memory_matrix, outputs = lax.scan(jax.checkpoint(span_output), memory_matrix, blocks)
    return from_blocks(outputs)

def split_heads(tensor):
    return jnp.transpose(tensor.reshape(tensor.shape[0], H, HD), (1, 0, 2))

def join_heads(tensor):
    return jnp.transpose(tensor, (1, 0, 2)).reshape(tensor.shape[1], H * HD)

def sequence_forward(tokens_in, valid, params):
    gain_one, qkv_weight, beta_weight, conv_weight, head_gain, out_weight, gain_two, gateup_weight, down_weight = params
    scale_one = lax.rsqrt(lax.optimization_barrier(jnp.mean(tokens_in * tokens_in, -1, keepdims=True)) + 1e-06)
    normed_one = low(tokens_in * scale_one * gain_one)
    projected = low_back(jnp.dot(normed_one, qkv_weight, precision=exact_precision))
    beta_logits = low_back(jnp.dot(normed_one, beta_weight, precision=exact_precision))
    conv_in = projected * valid[:, None]
    length_all = conv_in.shape[0]
    extended = jnp.concatenate([jnp.zeros((KERNEL - 1, conv_in.shape[1]), conv_in.dtype), conv_in], 0)
    conv_pre = conv_weight[0] * extended[0:length_all]
    for offset in range(1, KERNEL):
        conv_pre = conv_pre + conv_weight[offset] * extended[offset:offset + length_all]
    activated = jax.nn.silu(conv_pre)
    raw_queries = split_heads(activated[:, :D])
    raw_keys = split_heads(activated[:, D:2 * D])
    value_rows = split_heads(activated[:, 2 * D:])
    query_rows = raw_queries * lax.rsqrt(lax.optimization_barrier(jnp.sum(raw_queries * raw_queries, -1, keepdims=True)) + 1e-06) * HD ** (-0.5)
    key_row_block = raw_keys * lax.rsqrt(lax.optimization_barrier(jnp.sum(raw_keys * raw_keys, -1, keepdims=True)) + 1e-06)
    strength = jnp.transpose(jax.nn.sigmoid(beta_logits) * valid[:, None])
    heads_out = delta_rule(query_rows, key_row_block, value_rows, strength)
    head_scale = lax.rsqrt(lax.optimization_barrier(jnp.mean(heads_out * heads_out, -1, keepdims=True)) + 1e-05)
    merged = low(join_heads(heads_out * head_scale * head_gain))
    attention = low_back(jnp.dot(merged, out_weight, precision=exact_precision))
    middle = tokens_in + attention
    scale_two = lax.rsqrt(lax.optimization_barrier(jnp.mean(middle * middle, -1, keepdims=True)) + 1e-06)
    normed_two = low(middle * scale_two * gain_two)
    gate_up = low_back(jnp.dot(normed_two, gateup_weight, precision=exact_precision))
    hidden = low(jax.nn.silu(gate_up[:, :FF]) * gate_up[:, FF:])
    feed_out = low_back(jnp.dot(hidden, down_weight, precision=exact_precision))
    return middle + feed_out

def reference(inputs, lengths, cotangent, norm_gain1, w_qkv, w_beta, conv_weight, head_gain, w_out, norm_gain2, w_gateup, w_down):
    params = tuple((tensor.astype(jnp.float32) for tensor in (norm_gain1, w_qkv, w_beta, conv_weight, head_gain, w_out, norm_gain2, w_gateup, w_down)))
    tokens_all = inputs.astype(jnp.float32)
    positions = jnp.arange(LEN, dtype=jnp.int32)
    valid_all = (positions[None, :] < lengths[:, None].astype(jnp.int32)).astype(jnp.float32)

    def whole_layer(tokens_given, params_given):

        def one_sequence(seq_pair):
            return sequence_forward(seq_pair[0], seq_pair[1], params_given)
        return lax.map(jax.checkpoint(one_sequence), (tokens_given, valid_all))
    final_result, pull_back = jax.vjp(whole_layer, tokens_all, params)
    grad_tokens, weight_grads = pull_back(cotangent.astype(jnp.float32) * valid_all[:, :, None])
    return (final_result.astype(jnp.bfloat16), grad_tokens.astype(jnp.bfloat16), weight_grads[0], weight_grads[1], weight_grads[2], weight_grads[3], weight_grads[4], weight_grads[5], weight_grads[6], weight_grads[7], weight_grads[8])
```

```python
import functools
import jax, jax.numpy as jnp
from jax import lax
from jax.experimental import pallas as pl
from jax.experimental.pallas import tpu as pltpu
from jax.sharding import PartitionSpec as P

HD = 128
KERNEL = 4
CHUNK = 128
bf16 = jnp.bfloat16
f32 = jnp.float32

def dot(a, b):
    return jnp.dot(a, b, preferred_element_type=f32)

def dot_nt(a, b):
    return lax.dot_general(a, b, (((1,), (1,)), ((), ())), preferred_element_type=f32)

def dot_tn(a, b):
    return lax.dot_general(a, b, (((0,), (0,)), ((), ())), preferred_element_type=f32)

def halves(a):
    high = a.astype(bf16)
    return high, (a - high.astype(f32)).astype(bf16)

def fine_dot(a, b):
    n = b[0].shape[1]
    left = jnp.concatenate(a, 1)
    row = jnp.concatenate(b, 1)
    both = dot(left, jnp.concatenate([row, row], 0))
    return both[:, :n] + both[:, n:]

def unit_lower_inverses(lowers, size):
    rows = lax.broadcasted_iota(jnp.int32, (size, size), 0)
    cols = lax.broadcasted_iota(jnp.int32, (size, size), 1)
    eye = jnp.where(rows == cols, 1.0, 0.0)
    def joins(b):
        return (rows // (2 * b) == cols // (2 * b)) & ((rows // b) % 2 == 1) & ((cols // b) % 2 == 0)
    mask = joins(1)
    invs = [eye - jnp.where(mask, t, 0.0) for t in lowers]
    b = 2
    while b < size:
        mask = joins(b)
        parts = [halves(jnp.where(mask, t, 0.0)) for t in lowers]
        splits = [halves(t) for t in invs]
        inner = [halves(fine_dot(p, t)) for p, t in zip(parts, splits)]
        invs = [i - fine_dot(t, n) for i, t, n in zip(invs, splits, inner)]
        b *= 2
    return invs

def conv_rows(ref, weight, length):
    total = weight[0:1] * ref[pl.ds(5, length), :]
    for j in range(1, KERNEL):
        total = total + weight[j:j+1] * ref[pl.ds(5 + j, length), :]
    return total

def fd_kernel(hb, nv_ref, pq, pk, pv, hq, hk, hv, wq, wk, wv, bl_ref,
              q_ref, k_ref, t_ref, x_ref, o_ref, z_ref, ze_ref, ext):
    length = pq.shape[0]
    nv = nv_ref[0]
    valid = lax.broadcasted_iota(jnp.int32, (length, 1), 0) < nv
    rows = lax.broadcasted_iota(jnp.int32, (CHUNK, CHUNK), 0)
    cols = lax.broadcasted_iota(jnp.int32, (CHUNK, CHUNK), 1)
    eye = jnp.where(rows == cols, 1.0, 0.0)
    group = pl.program_id(0)
    lane8 = lax.broadcasted_iota(jnp.int32, bl_ref.shape, 1)
    acts = []
    for i, (p, h, w) in enumerate(((pq, hq, wq), (pk, hk, wk), (pv, hv, wv))):
        ext[i, 0:8, :] = h[...]
        ext[i, 8:, :] = jnp.where(valid, p[...], 0.0)
        c = conv_rows(ext.at[i], w, length)
        acts.append(c * jax.nn.sigmoid(c))
    count = length // CHUNK
    spans = [slice(c * CHUNK, (c + 1) * CHUNK) for c in range(count)]
    heads = []
    for h in range(hb):
        lanes = slice(h * HD, (h + 1) * HD)
        a, b, v = (t[:, lanes] for t in acts)
        q = (a * (lax.rsqrt(jnp.sum(a * a, -1, keepdims=True) + 1e-6) * HD ** -0.5)).astype(bf16)
        k = (b * lax.rsqrt(jnp.sum(b * b, -1, keepdims=True) + 1e-6)).astype(bf16)
        logit = jnp.sum(jnp.where(lane8 == group * hb + h, bl_ref[...], 0.0), -1, keepdims=True)
        beta = jnp.where(valid, jax.nn.sigmoid(logit), 0.0)
        q_ref[:, lanes] = q
        k_ref[:, lanes] = k
        heads.append((q, k, (k.astype(f32) * beta).astype(bf16), (v * beta).astype(bf16)))
    cells = [(h, s) for h in range(hb) for s in spans]
    boths = [dot_nt(jnp.concatenate([heads[h][2][s], heads[h][0][s]], 0), heads[h][1][s]) for h, s in cells]
    invs = unit_lower_inverses([jnp.where(rows > cols, t[:CHUNK], 0.0) for t in boths], CHUNK)
    invs = [t.astype(bf16) for t in invs]
    blends = [dot(t, jnp.concatenate([heads[h][2][s], heads[h][3][s]], 1)) for t, (h, s) in zip(invs, cells)]
    states = [jnp.concatenate([jnp.zeros((HD, HD), f32), eye], 1)] * hb
    for c, s in enumerate(spans):
        for h in range(hb):
            q, k = heads[h][:2]
            cell = h * count + c
            t_ref[h, c] = invs[cell]
            score = jnp.where(rows >= cols, boths[cell][CHUNK:], 0.0).astype(bf16)
            low = states[h].astype(bf16)
            z_ref[h, c] = low
            both = dot(jnp.concatenate([blends[cell][:, :HD].astype(bf16), q[s]], 0), low)
            err = jnp.concatenate([blends[cell][:, HD:] - both[:CHUNK, :HD], -both[:CHUNK, HD:]], 1).astype(bf16)
            wide = slice(2 * h * HD, 2 * (h + 1) * HD)
            x_ref[s, wide] = err
            o_ref[s, wide] = both[CHUNK:] + dot(score, err)
            states[h] = states[h] + dot_tn(k[s], err)
    for h in range(hb):
        ze_ref[h] = states[h]

def fd(proj, halo, conv_w, logits, nv, hb=1):
    length = proj.shape[0]
    heads = proj.shape[1] // (3 * HD)
    nc = length // CHUNK
    g = heads // hb
    w = hb * HD
    col = lambda off: (lambda i, *_: (0, i + off * g))
    in_specs = [pl.BlockSpec((length, w), col(o)) for o in range(3)]
    in_specs += [pl.BlockSpec((8, w), col(o)) for o in range(3)]
    in_specs += [pl.BlockSpec((KERNEL, w), col(o)) for o in range(3)]
    in_specs += [pl.BlockSpec((length, heads), lambda i, *_: (0, 0))]
    out_shape = (
        jax.ShapeDtypeStruct((length, heads * HD), bf16),
        jax.ShapeDtypeStruct((length, heads * HD), bf16),
        jax.ShapeDtypeStruct((heads, nc, CHUNK, CHUNK), bf16),
        jax.ShapeDtypeStruct((length, heads * 2 * HD), bf16),
        jax.ShapeDtypeStruct((length, heads * 2 * HD), f32),
        jax.ShapeDtypeStruct((heads, nc, HD, 2 * HD), bf16),
        jax.ShapeDtypeStruct((heads, HD, 2 * HD), f32),
    )
    out_specs = (
        pl.BlockSpec((length, w), lambda i, *_: (0, i)),
        pl.BlockSpec((length, w), lambda i, *_: (0, i)),
        pl.BlockSpec((hb, nc, CHUNK, CHUNK), lambda i, *_: (i, 0, 0, 0)),
        pl.BlockSpec((length, 2 * w), lambda i, *_: (0, i)),
        pl.BlockSpec((length, 2 * w), lambda i, *_: (0, i)),
        pl.BlockSpec((hb, nc, HD, 2 * HD), lambda i, *_: (i, 0, 0, 0)),
        pl.BlockSpec((hb, HD, 2 * HD), lambda i, *_: (i, 0, 0)),
    )
    return pl.pallas_call(
        functools.partial(fd_kernel, hb), out_shape=out_shape,
        grid_spec=pltpu.PrefetchScalarGridSpec(num_scalar_prefetch=1, grid=(g,), in_specs=in_specs, out_specs=out_specs,
            scratch_shapes=[pltpu.VMEM((3, length + 8, w), f32)]),
        name="delta_forward",
    )(nv, proj, proj, proj, halo, halo, halo, conv_w, conv_w, conv_w, logits)
def fc_kernel(hb, oq, x, z, s_in, gain, o_ref, m_ref, e_ref, s_ref):
    length = oq.shape[0]
    for h in range(hb):
        lanes = slice(h * HD, (h + 1) * HD)
        left = slice(2 * h * HD, (2 * h + 1) * HD)
        right = slice((2 * h + 1) * HD, 2 * (h + 1) * HD)
        enter = s_in[h]
        out = oq[:, left] + dot(oq[:, right].astype(bf16), enter)
        scale = lax.rsqrt(jnp.mean(out * out, -1, keepdims=True) + 1e-05)
        o_ref[:, lanes] = out.astype(bf16)
        m_ref[:, lanes] = (out * scale * gain[...]).astype(bf16)
        e_ref[:, lanes] = (x[:, left].astype(f32) + dot(x[:, right], enter)).astype(bf16)
        for c in range(length // CHUNK):
            s_ref[h, c] = (z[h, c, :, :HD].astype(f32) + dot(z[h, c, :, HD:], enter)).astype(bf16)

def fc(oq, x, z, s_in, gain, hb=2):
    length = oq.shape[0]
    heads, nc = z.shape[:2]
    w = hb * HD
    tok = lambda m: pl.BlockSpec((length, m * w), lambda i: (0, i))
    return pl.pallas_call(
        functools.partial(fc_kernel, hb),
        out_shape=(
            jax.ShapeDtypeStruct((length, heads * HD), bf16),
            jax.ShapeDtypeStruct((length, heads * HD), bf16),
            jax.ShapeDtypeStruct((length, heads * HD), bf16),
            jax.ShapeDtypeStruct((heads, nc, HD, HD), bf16),
        ),
        grid=(heads // hb,),
        in_specs=[tok(2), tok(2), pl.BlockSpec((hb, nc, HD, 2 * HD), lambda i: (i, 0, 0, 0)),
                  pl.BlockSpec((hb, HD, HD), lambda i: (i, 0, 0)), pl.BlockSpec((1, HD), lambda i: (0, 0))],
        out_specs=(tok(1), tok(1), tok(1), pl.BlockSpec((hb, nc, HD, HD), lambda i: (i, 0, 0, 0))),
        name="heads_out",
    )(oq, x, z, s_in, gain)

def head_beta(logits, head, valid):
    lane = lax.broadcasted_iota(jnp.int32, logits.shape, 1)
    logit = jnp.sum(jnp.where(lane == head, logits, 0.0), -1, keepdims=True)
    return jnp.where(valid, jax.nn.sigmoid(logit), 0.0)

def bd_kernel(hb, nv_ref, gm, o, q, k, t, bl, gain, g_ref, d_ref, de_ref, do_ref, hg_ref):
    length = gm.shape[0]
    count = length // CHUNK
    group = pl.program_id(0)
    valid = lax.broadcasted_iota(jnp.int32, (length, 1), 0) < nv_ref[0]
    rows = lax.broadcasted_iota(jnp.int32, (CHUNK, CHUNK), 0)
    cols = lax.broadcasted_iota(jnp.int32, (CHUNK, CHUNK), 1)
    eye = jnp.where(rows == cols, 1.0, 0.0)
    spans = [slice(c * CHUNK, (c + 1) * CHUNK) for c in range(count)]
    @pl.when(group == 0)
    def _():
        hg_ref[...] = jnp.zeros_like(hg_ref)
    heads = []
    for h in range(hb):
        lanes = slice(h * HD, (h + 1) * HD)
        grad, out = gm[:, lanes].astype(f32), o[:, lanes].astype(f32)
        scale = lax.rsqrt(jnp.mean(out * out, -1, keepdims=True) + 1e-05)
        hg_ref[0:1, :] += jnp.sum(grad * out * scale, 0, keepdims=True)
        scaled = grad * gain[...]
        down = (scale * scaled - scale * scale * scale * out * jnp.mean(scaled * out, -1, keepdims=True)).astype(bf16)
        do_ref[:, lanes] = down
        heads.append((q[:, lanes], k[:, lanes], down, head_beta(bl[...], group * hb + h, valid)))
    cells = [(h, c) for h in range(hb) for c in range(count)]
    scores = [jnp.where(rows >= cols, dot_nt(heads[h][0][spans[c]], heads[h][1][spans[c]]), 0.0).astype(bf16) for h, c in cells]
    errs = [dot_tn(m, heads[h][2][spans[c]]).astype(bf16) for m, (h, c) in zip(scores, cells)]
    firsts = [dot_tn(t[h, c], jnp.concatenate([e, heads[h][1][spans[c]]], 1)) for e, (h, c) in zip(errs, cells)]
    adds = [dot_tn(heads[h][0][spans[c]], heads[h][2][spans[c]]) for h, c in cells]
    states = [jnp.concatenate([jnp.zeros((HD, HD), f32), eye], 1)] * hb
    for c in reversed(range(count)):
        s = spans[c]
        for h in range(hb):
            cell = h * count + c
            low = states[h].astype(bf16)
            d_ref[h, c] = low
            both = dot(firsts[cell][:, HD:].astype(bf16), low)
            full = jnp.concatenate([both[:, :HD] + firsts[cell][:, :HD], both[:, HD:]], 1)
            g_ref[s, 2 * h * HD:2 * (h + 1) * HD] = full.astype(bf16)
            back = (full * heads[h][3][s]).astype(bf16)
            change = dot_tn(heads[h][1][s], back)
            states[h] = states[h] - change + jnp.concatenate([adds[cell], jnp.zeros((HD, HD), f32)], 1)
    for h in range(hb):
        de_ref[h] = states[h]

def bd(gm, o, q, k, t, logits, gain, nv, hb=2):
    length = gm.shape[0]
    heads, nc = t.shape[:2]
    w = hb * HD
    tok = lambda m: pl.BlockSpec((length, m * w), lambda i, *_: (0, i))
    sq = lambda m: pl.BlockSpec((hb, nc, HD, m * HD), lambda i, *_: (i, 0, 0, 0))
    return pl.pallas_call(
        functools.partial(bd_kernel, hb),
        out_shape=(
            jax.ShapeDtypeStruct((length, heads * 2 * HD), bf16),
            jax.ShapeDtypeStruct((heads, nc, HD, 2 * HD), bf16),
            jax.ShapeDtypeStruct((heads, HD, 2 * HD), f32),
            jax.ShapeDtypeStruct((length, heads * HD), bf16),
            jax.ShapeDtypeStruct((8, HD), f32),
        ),
        grid_spec=pltpu.PrefetchScalarGridSpec(
            num_scalar_prefetch=1, grid=(heads // hb,),
            in_specs=[tok(1), tok(1), tok(1), tok(1), sq(1),
                      pl.BlockSpec((length, heads), lambda i, *_: (0, 0)), pl.BlockSpec((1, HD), lambda i, *_: (0, 0))],
            out_specs=(tok(2), sq(2), pl.BlockSpec((hb, HD, 2 * HD), lambda i, *_: (i, 0, 0)), tok(1),
                       pl.BlockSpec((8, HD), lambda i, *_: (0, 0)))),
        name="delta_backward",
    )(nv, gm, o, q, k, t, logits, gain)

TAIL = 16

def bg_kernel(hb, nv_ref, g, d, ds, do, q, k, e, s_c, bl, pq, pk, pv, hq, hk, hv, wq, wk, wv,
              gp_ref, tail_ref, back_ref, conv_ref, gl_ref, ext, gext):
    length = pq.shape[0]
    count = length // CHUNK
    group = pl.program_id(0)
    valid = lax.broadcasted_iota(jnp.int32, (length, 1), 0) < nv_ref[0]
    rows = lax.broadcasted_iota(jnp.int32, (CHUNK, CHUNK), 0)
    cols = lax.broadcasted_iota(jnp.int32, (CHUNK, CHUNK), 1)
    spans = [slice(c * CHUNK, (c + 1) * CHUNK) for c in range(count)]
    weights = (wq, wk, wv)
    pres = []
    for i, (p, h, w) in enumerate(((pq, hq, wq), (pk, hk, wk), (pv, hv, wv))):
        ext[i, 0:8, :] = h[...]
        ext[i, 8:, :] = jnp.where(valid, p[...], 0.0)
        pres.append(conv_rows(ext.at[i], w, length))
    @pl.when(group == 0)
    def _():
        gl_ref[...] = jnp.zeros_like(gl_ref)
    lane8 = lax.broadcasted_iota(jnp.int32, (length, bl.shape[1]), 1)
    grads = ([], [], [])
    for h in range(hb):
        lanes = slice(h * HD, (h + 1) * HD)
        wide = slice(2 * h * HD, (2 * h + 1) * HD)
        wider = slice((2 * h + 1) * HD, 2 * (h + 1) * HD)
        beta = head_beta(bl[...], group * hb + h, valid)
        enter = ds[h]
        full = g[:, wide].astype(f32) + dot(g[:, wider], enter)
        back32 = full * beta
        grads[2].append(back32)
        err = e[:, lanes]
        gl = jnp.sum(full * err.astype(f32), -1, keepdims=True) * (1.0 - beta)
        gl_ref[...] += jnp.where((lane8 == group * hb + h) & valid, gl, 0.0)
        back = back32.astype(bf16)
        nback = (-back32).astype(bf16)
        qh, kh, dh = q[:, lanes], k[:, lanes], do[:, lanes]
        outs = [(d[h, c, :, :HD].astype(f32) + dot(d[h, c, :, HD:], enter)).astype(bf16) for c in range(count)]
        pairs = [dot_nt(jnp.concatenate([dh[s], nback[s]], 0), err[s]) for s in spans]
        pairs = [jnp.concatenate([jnp.where(rows >= cols, p[:CHUNK], 0.0), jnp.where(rows > cols, p[CHUNK:], 0.0)], 0).astype(bf16) for p in pairs]
        first = [dot_nt(jnp.concatenate([dh[s], nback[s]], 0), s_c[h, c]) for c, s in enumerate(spans)]
        second = [dot(p, kh[s]) for p, s in zip(pairs, spans)]
        third = [dot_nt(err[s], o) for o, s in zip(outs, spans)]
        fourth = [dot_tn(p, jnp.concatenate([qh[s], kh[s]], 0)) for p, s in zip(pairs, spans)]
        grads[0].append(jnp.concatenate([a[:CHUNK] + b[:CHUNK] for a, b in zip(first, second)], 0))
        grads[1].append(jnp.concatenate([a[CHUNK:] + b[CHUNK:] + t + f for a, b, t, f in zip(first, second, third, fourth)], 0))
    for i in range(3):
        pre = pres[i]
        sig = jax.nn.sigmoid(pre)
        pieces = []
        for h in range(hb):
            grad = grads[i][h]
            if i < 2:
                raw = (pre * sig)[:, h * HD:(h + 1) * HD]
                scale = lax.rsqrt(jnp.sum(raw * raw, -1, keepdims=True) + 1e-06)
                grad = scale * (grad - scale * scale * raw * jnp.sum(raw * grad, -1, keepdims=True))
                if i == 0:
                    grad = grad * HD ** -0.5
            pieces.append(grad)
        grad = jnp.concatenate(pieces, 1) if hb > 1 else pieces[0]
        grad = grad * sig * (1.0 + pre * (1.0 - sig))
        gext[i, 0:8, :] = jnp.zeros((8, gext.shape[2]), f32)
        gext[i, 8:8 + length, :] = grad
        gext[i, 8 + length:, :] = jnp.zeros((8, gext.shape[2]), f32)
        w = weights[i]
        for j in range(KERNEL):
            conv_ref[i, j:j + 1, :] = jnp.sum(grad * ext[i, 5 + j:5 + j + length, :], 0, keepdims=True)
        total = w[0:1] * gext[i, 3:3 + length + 8, :]
        for j in range(1, KERNEL):
            total = total + w[j:j + 1] * gext[i, 3 - j:3 - j + length + 8, :]
        back_ref[i] = total[:8]
        tail_ref[i] = total[8 + length - TAIL:]
        gp_ref[i] = jnp.where(valid, total[8:], 0.0).astype(bf16)

def bg(g, d, ds, do, q, k, e, s_c, logits, proj, halo, conv_w, nv, hb=2):
    length = do.shape[0]
    heads, nc = d.shape[:2]
    w = hb * HD
    groups = heads // hb
    tok = lambda m: pl.BlockSpec((length, m * w), lambda i, *_: (0, i))
    sq = lambda m: pl.BlockSpec((hb, nc, HD, m * HD), lambda i, *_: (i, 0, 0, 0))
    col = lambda off: (lambda i, *_: (0, i + off * groups))
    three = lambda n: pl.BlockSpec((3, n, w), lambda i, *_: (0, 0, i))
    in_specs = [tok(2), sq(2), pl.BlockSpec((hb, HD, HD), lambda i, *_: (i, 0, 0)), tok(1), tok(1), tok(1), tok(1), sq(1),
                pl.BlockSpec((length, heads), lambda i, *_: (0, 0))]
    in_specs += [pl.BlockSpec((length, w), col(o)) for o in range(3)]
    in_specs += [pl.BlockSpec((8, w), col(o)) for o in range(3)]
    in_specs += [pl.BlockSpec((KERNEL, w), col(o)) for o in range(3)]
    width = heads * HD
    return pl.pallas_call(
        functools.partial(bg_kernel, hb),
        out_shape=(
            jax.ShapeDtypeStruct((3, length, width), bf16),
            jax.ShapeDtypeStruct((3, TAIL, width), f32),
            jax.ShapeDtypeStruct((3, 8, width), f32),
            jax.ShapeDtypeStruct((3, KERNEL, width), f32),
            jax.ShapeDtypeStruct((length, heads), f32),
        ),
        grid_spec=pltpu.PrefetchScalarGridSpec(
            num_scalar_prefetch=1, grid=(groups,), in_specs=in_specs,
            out_specs=(three(length), three(TAIL), three(8), three(KERNEL), pl.BlockSpec((length, heads), lambda i, *_: (0, 0))),
            scratch_shapes=[pltpu.VMEM((3, length + 8, w), f32), pltpu.VMEM((3, length + 16, w), f32)]),
        name="mixer_gradients",
    )(nv, g, d, ds, do, q, k, e, s_c, logits, proj, proj, proj, halo, halo, halo, conv_w, conv_w, conv_w)


def passed_along(value, axis, steps):
    count = lax.axis_size(axis)
    first, last = (max(0, -steps), min(count, count - steps))
    return lax.ppermute(value, axis, [(source, source + steps) for source in range(first, last)])


def apply_map(matrix, tensor):
    return jnp.einsum("hij,hjk->hik", matrix, tensor, precision=lax.Precision.HIGHEST)


def gathered(shard):
    rows = shard.shape[0] // lax.axis_size("ctx")
    mine = lax.dynamic_slice_in_dim(shard, lax.axis_index("ctx") * rows, rows, 0)
    return lax.all_gather(mine, ("fsdp", "ctx"), axis=0, tiled=True)


def summed(partial):
    share = lax.psum_scatter(partial.astype(bf16), ("fsdp", "ctx"), scatter_dimension=0, tiled=True)
    return lax.psum(share, "dp").astype(f32)


def local(
    inputs,
    lengths,
    cotangent,
    norm_gain1,
    w_qkv,
    w_beta,
    conv_weight,
    head_gain,
    w_out,
    norm_gain2,
    w_gateup,
    w_down,
):
    tokens_in = inputs[0].astype(f32)
    piece_len, model_width = tokens_in.shape
    heads = w_beta.shape[1]
    width = heads * HD
    start = lax.axis_index("ctx") * piece_len
    left_valid = lengths - start
    positions = start + jnp.arange(piece_len, dtype=jnp.int32)
    valid = (positions < lengths[0]).astype(f32)
    mixed = jnp.concatenate([w_qkv, jnp.pad(w_beta, ((0, 0), (0, HD - heads)))], 1)
    mixed_full = gathered(mixed)
    out_full = gathered(w_out)
    gateup_full = gathered(w_gateup)
    down_full = gathered(w_down)
    qkv_full, beta_full = mixed_full[:, : 3 * width], mixed_full[:, 3 * width :]
    scale_one = lax.rsqrt(jnp.mean(tokens_in * tokens_in, -1, keepdims=True) + 1e-06)
    normed_one = (tokens_in * scale_one * norm_gain1).astype(bf16)
    projected = jnp.dot(normed_one, qkv_full, preferred_element_type=f32)
    beta_logits = jnp.dot(normed_one, beta_full, preferred_element_type=f32)[:, :heads]
    last_rows = jnp.where(valid[piece_len - 8 :, None] > 0, projected[piece_len - 8 :], 0.0)
    halo = passed_along(last_rows.astype(bf16), "ctx", 1).astype(f32)
    queries, keys, inverse, errors, outs, states, ends = fd(
        projected, halo, conv_weight, beta_logits, left_valid, hb=2
    )
    local_end, transition = ends[:, :, :HD], ends[:, :, HD:]
    zero_memory = jnp.zeros((heads, HD, HD), f32)

    def relay_forward(step_index, memory):
        return passed_along(
            (apply_map(transition, memory) + local_end).astype(bf16), "ctx", 1
        ).astype(f32)

    memory_in = passed_along(local_end.astype(bf16), "ctx", 1)
    memory_in = lax.fori_loop(
        0, lax.axis_size("ctx") - 2, relay_forward, memory_in.astype(f32)
    ).astype(bf16)
    heads_out, merged, errors, states = fc(outs, errors, states, memory_in, head_gain[None])
    attention = jnp.dot(merged, out_full, preferred_element_type=f32)
    middle = tokens_in + attention
    scale_two = lax.rsqrt(jnp.mean(middle * middle, -1, keepdims=True) + 1e-06)
    normed_two = (middle * scale_two * norm_gain2).astype(bf16)
    gate_up = jnp.dot(normed_two, gateup_full, preferred_element_type=f32)
    ff_width = gate_up.shape[1] // 2
    gate_part = gate_up[:, :ff_width]
    up_part = gate_up[:, ff_width:]
    gate_sig = jax.nn.sigmoid(gate_part)
    hidden = (gate_part * gate_sig * up_part).astype(bf16)
    feed_out = jnp.dot(hidden, down_full, preferred_element_type=f32)
    output = (middle + feed_out).astype(bf16)
    contract_cols = (((1,), (1,)), ((), ()))
    contract_rows = (((0,), (0,)), ((), ()))
    masked_cotangent = cotangent[0].astype(f32) * valid[:, None]
    grad_feed = masked_cotangent.astype(bf16)
    grad_hidden = lax.dot_general(grad_feed, down_full, contract_cols, preferred_element_type=f32)
    grad_gate = grad_hidden * up_part * gate_sig * (1.0 + gate_part * (1.0 - gate_sig))
    grad_up = grad_hidden * gate_part * gate_sig
    grad_gate_up = jnp.concatenate([grad_gate, grad_up], 1).astype(bf16)
    down_total = summed(
        lax.dot_general(hidden, grad_feed, contract_rows, preferred_element_type=f32)
    )
    gateup_total = summed(
        lax.dot_general(normed_two, grad_gate_up, contract_rows, preferred_element_type=f32)
    )
    grad_normed_two = lax.dot_general(
        grad_gate_up, gateup_full, contract_cols, preferred_element_type=f32
    )
    gain_two_term = jnp.sum(grad_normed_two * middle * scale_two, 0)
    scaled_two = grad_normed_two * norm_gain2
    grad_middle = (
        masked_cotangent
        + scale_two * scaled_two
        - scale_two
        * scale_two
        * scale_two
        * middle
        * jnp.mean(scaled_two * middle, -1, keepdims=True)
    )
    grad_attention = grad_middle.astype(bf16)
    out_total = summed(
        lax.dot_general(merged, grad_attention, contract_rows, preferred_element_type=f32)
    )
    grad_merged = lax.dot_general(
        grad_attention, out_full, contract_cols, preferred_element_type=f32
    )
    grads, pulls, ends, grad_outs, gain_rows = bd(
        grad_merged, heads_out, queries, keys, inverse, beta_logits, head_gain[None], left_valid
    )
    head_gain_term = gain_rows[0]
    local_part, transposed = ends[:, :, :HD], ends[:, :, HD:]

    def relay_backward(step_index, memory_grad):
        return passed_along(
            (apply_map(transposed, memory_grad) + local_part).astype(bf16), "ctx", -1
        ).astype(f32)

    grad_memory = passed_along(local_part.astype(bf16), "ctx", -1)
    grad_memory = lax.fori_loop(
        0, lax.axis_size("ctx") - 2, relay_backward, grad_memory.astype(f32)
    ).astype(bf16)
    grad_three, tails, returns, conv_terms, grad_logits = bg(
        grads, pulls, grad_memory, grad_outs, queries, keys, errors, states, beta_logits,
        projected, halo, conv_weight, left_valid,
    )
    returned = passed_along(returns.astype(bf16), "ctx", -1).astype(f32)
    ending = jnp.where(
        valid[None, piece_len - 8 :, None] > 0, tails[:, TAIL - 8 :] + returned, 0.0
    ).astype(bf16)
    grad_three = lax.dynamic_update_slice(grad_three, ending, (0, piece_len - 8, 0))
    grad_projected = jnp.concatenate([grad_three[0], grad_three[1], grad_three[2]], 1)
    grad_logits = jnp.pad(grad_logits, ((0, 0), (0, HD - heads))).astype(bf16)
    grad_mixed = jnp.concatenate([grad_projected, grad_logits], 1)
    grad_normed_one = lax.dot_general(
        grad_mixed, mixed_full, contract_cols, preferred_element_type=f32
    )
    gain_one_term = jnp.sum(grad_normed_one * tokens_in * scale_one, 0)
    scaled_one = grad_normed_one * norm_gain1
    grad_tokens = (
        grad_middle
        + scale_one * scaled_one
        - scale_one
        * scale_one
        * scale_one
        * tokens_in
        * jnp.mean(scaled_one * tokens_in, -1, keepdims=True)
    )
    mixed_total = summed(
        lax.dot_general(normed_one, grad_mixed, contract_rows, preferred_element_type=f32)
    )
    conv_terms = jnp.concatenate([conv_terms[0], conv_terms[1], conv_terms[2]], 1)
    small = jnp.concatenate(
        [gain_one_term, gain_two_term, head_gain_term, conv_terms.reshape(-1)], 0
    )
    small = lax.psum(small, ("dp", "fsdp", "ctx"))
    cuts = [model_width, 2 * model_width, 2 * model_width + HD]
    gain_one, gain_two, gain_head, conv_total = jnp.split(small, cuts)
    return (
        output[None],
        grad_tokens.astype(bf16)[None],
        gain_one,
        mixed_total[:, : 3 * width],
        mixed_total[:, 3 * width : 3 * width + heads],
        conv_total.reshape(conv_weight.shape),
        gain_head,
        out_total,
        gain_two,
        gateup_total,
        down_total,
    )


def solution(mesh):
    placed = (
        P(("dp", "fsdp"), "ctx", None),
        P(("dp", "fsdp")),
        P(("dp", "fsdp"), "ctx", None),
        P(),
        P("fsdp", None),
        P("fsdp", None),
        P(),
        P(),
        P("fsdp", None),
        P(),
        P("fsdp", None),
        P("fsdp", None),
    )
    return jax.shard_map(
        local,
        mesh=mesh,
        in_specs=placed,
        out_specs=(
            P(("dp", "fsdp"), "ctx", None),
            P(("dp", "fsdp"), "ctx", None),
            P(),
            P(("fsdp", "ctx"), None),
            P(("fsdp", "ctx"), None),
            P(),
            P(),
            P(("fsdp", "ctx"), None),
            P(),
            P(("fsdp", "ctx"), None),
            P(("fsdp", "ctx"), None),
        ),
        check_vma=False,
    )
```

```python
import functools
import jax, jax.numpy as jnp
from jax import lax
from jax.experimental import pallas as pl
from jax.experimental.pallas import tpu as pltpu
from jax.sharding import PartitionSpec as P

HD = 128
KERNEL = 4
CHUNK = 128
bf16 = jnp.bfloat16
f32 = jnp.float32

def dot(a, b):
    return jnp.dot(a, b, preferred_element_type=f32)

def dot_nt(a, b):
    return lax.dot_general(a, b, (((1,), (1,)), ((), ())), preferred_element_type=f32)

def dot_tn(a, b):
    return lax.dot_general(a, b, (((0,), (0,)), ((), ())), preferred_element_type=f32)

def halves(a):
    high = a.astype(bf16)
    return high, (a - high.astype(f32)).astype(bf16)

def fine_dot(a, b):
    n = b[0].shape[1]
    left = jnp.concatenate(a, 1)
    row = jnp.concatenate(b, 1)
    both = dot(left, jnp.concatenate([row, row], 0))
    return both[:, :n] + both[:, n:]

def unit_lower_inverses(lowers, size):
    rows = lax.broadcasted_iota(jnp.int32, (size, size), 0)
    cols = lax.broadcasted_iota(jnp.int32, (size, size), 1)
    eye = jnp.where(rows == cols, 1.0, 0.0)
    def joins(b):
        return (rows // (2 * b) == cols // (2 * b)) & ((rows // b) % 2 == 1) & ((cols // b) % 2 == 0)
    mask = joins(1)
    invs = [eye - jnp.where(mask, t, 0.0) for t in lowers]
    b = 2
    while b < size:
        mask = joins(b)
        parts = [halves(jnp.where(mask, t, 0.0)) for t in lowers]
        splits = [halves(t) for t in invs]
        inner = [halves(fine_dot(p, t)) for p, t in zip(parts, splits)]
        invs = [i - fine_dot(t, n) for i, t, n in zip(invs, splits, inner)]
        b *= 2
    return invs

def conv_rows(ref, weight, length):
    total = weight[0:1] * ref[pl.ds(5, length), :]
    for j in range(1, KERNEL):
        total = total + weight[j:j+1] * ref[pl.ds(5 + j, length), :]
    return total


def head_beta(logits, head, valid):
    lane = lax.broadcasted_iota(jnp.int32, logits.shape, 1)
    logit = jnp.sum(jnp.where(lane == head, logits, 0.0), -1, keepdims=True)
    return jnp.where(valid, jax.nn.sigmoid(logit), 0.0)


def mixer_forward_kernel(hb, nv_ref, pq, pk, pv, wq, wk, wv, bl, gain,
                         q_ref, k_ref, t_ref, e_ref, s_ref, o_ref, m_ref, ext):
    length = pq.shape[0]
    valid = lax.broadcasted_iota(jnp.int32, (length, 1), 0) < nv_ref[0]
    rows = lax.broadcasted_iota(jnp.int32, (CHUNK, CHUNK), 0)
    cols = lax.broadcasted_iota(jnp.int32, (CHUNK, CHUNK), 1)
    group = pl.program_id(0)
    acts = []
    for i, (p, w) in enumerate(((pq, wq), (pk, wk), (pv, wv))):
        ext[i, 0:8, :] = jnp.zeros((8, ext.shape[2]), f32)
        ext[i, 8:, :] = jnp.where(valid, p[...], 0.0)
        c = conv_rows(ext.at[i], w, length)
        acts.append(c * jax.nn.sigmoid(c))
    count = length // CHUNK
    spans = [slice(c * CHUNK, (c + 1) * CHUNK) for c in range(count)]
    heads = []
    for h in range(hb):
        lanes = slice(h * HD, (h + 1) * HD)
        a, b, v = (t[:, lanes] for t in acts)
        q = (a * (lax.rsqrt(jnp.sum(a * a, -1, keepdims=True) + 1e-6) * HD ** -0.5)).astype(bf16)
        k = (b * lax.rsqrt(jnp.sum(b * b, -1, keepdims=True) + 1e-6)).astype(bf16)
        beta = head_beta(bl[...], group * hb + h, valid)
        q_ref[:, lanes] = q
        k_ref[:, lanes] = k
        heads.append((q, k, (k.astype(f32) * beta).astype(bf16), (v * beta).astype(bf16)))
    cells = [(h, s) for h in range(hb) for s in spans]
    boths = [dot_nt(jnp.concatenate([heads[h][2][s], heads[h][0][s]], 0), heads[h][1][s]) for h, s in cells]
    invs = unit_lower_inverses([jnp.where(rows > cols, t[:CHUNK], 0.0) for t in boths], CHUNK)
    invs = [t.astype(bf16) for t in invs]
    blends = [dot(t, jnp.concatenate([heads[h][2][s], heads[h][3][s]], 1)) for t, (h, s) in zip(invs, cells)]
    states = [jnp.zeros((HD, HD), f32)] * hb
    for c, s in enumerate(spans):
        for h in range(hb):
            lanes = slice(h * HD, (h + 1) * HD)
            q, k = heads[h][:2]
            cell = h * count + c
            t_ref[h, c] = invs[cell]
            score = jnp.where(rows >= cols, boths[cell][CHUNK:], 0.0).astype(bf16)
            low = states[h].astype(bf16)
            s_ref[h, c] = low
            both = dot(jnp.concatenate([blends[cell][:, :HD].astype(bf16), q[s]], 0), low)
            err = (blends[cell][:, HD:] - both[:CHUNK]).astype(bf16)
            e_ref[s, lanes] = err
            states[h] = states[h] + dot_tn(k[s], err)
            out = both[CHUNK:] + dot(score, err)
            scale = lax.rsqrt(jnp.mean(out * out, -1, keepdims=True) + 1e-05)
            o_ref[s, lanes] = out.astype(bf16)
            m_ref[s, lanes] = (out * scale * gain[...]).astype(bf16)


def heads_per_step(heads):
    return 2 if heads % 2 == 0 else 1


def mixer_forward(projected, conv_w, gain, nv, heads):
    length = projected.shape[0]
    nc = length // CHUNK
    hb = heads_per_step(heads)
    groups = heads // hb
    w = hb * HD
    col = lambda off: (lambda i, *_: (0, i + off * groups))
    tok = pl.BlockSpec((length, w), lambda i, *_: (0, i))
    sq = pl.BlockSpec((hb, nc, HD, HD), lambda i, *_: (i, 0, 0, 0))
    in_specs = [pl.BlockSpec((length, w), col(o)) for o in range(3)]
    in_specs += [pl.BlockSpec((KERNEL, w), col(o)) for o in range(3)]
    in_specs += [pl.BlockSpec((length, HD), lambda i, *_: (0, 3 * heads)), pl.BlockSpec((1, HD), lambda i, *_: (0, 0))]
    flat = jax.ShapeDtypeStruct((length, heads * HD), bf16)
    square = jax.ShapeDtypeStruct((heads, nc, HD, HD), bf16)
    return pl.pallas_call(
        functools.partial(mixer_forward_kernel, hb),
        out_shape=(flat, flat, square, flat, square, flat, flat),
        grid_spec=pltpu.PrefetchScalarGridSpec(
            num_scalar_prefetch=1, grid=(groups,), in_specs=in_specs,
            out_specs=(tok, tok, sq, tok, sq, tok, tok),
            scratch_shapes=[pltpu.VMEM((3, length + 8, w), f32)]),
        name="mixer_forward",
    )(nv, projected, projected, projected, conv_w, conv_w, conv_w, projected, gain)


def mixer_backward_kernel(hb, heads_all, nv_ref, gm, o, q, k, t, e, s_c, bl, pq, pk, pv, wq, wk, wv, gain,
                          gp_ref, conv_ref, hg_ref, ext, gext):
    length = gm.shape[0]
    count = length // CHUNK
    group = pl.program_id(0)
    width = hb * HD
    valid = lax.broadcasted_iota(jnp.int32, (length, 1), 0) < nv_ref[0]
    rows = lax.broadcasted_iota(jnp.int32, (CHUNK, CHUNK), 0)
    cols = lax.broadcasted_iota(jnp.int32, (CHUNK, CHUNK), 1)
    spans = [slice(c * CHUNK, (c + 1) * CHUNK) for c in range(count)]
    logits_at = slice(3 * heads_all * HD, (3 * heads_all + 1) * HD)
    @pl.when(group == 0)
    def _():
        hg_ref[...] = jnp.zeros_like(hg_ref)
        gp_ref[:, logits_at] = jnp.zeros((length, HD), bf16)
    heads = []
    for h in range(hb):
        lanes = slice(h * HD, (h + 1) * HD)
        grad, out = gm[:, lanes].astype(f32), o[:, lanes].astype(f32)
        scale = lax.rsqrt(jnp.mean(out * out, -1, keepdims=True) + 1e-05)
        hg_ref[0:1, :] += jnp.sum(grad * out * scale, 0, keepdims=True)
        scaled = grad * gain[...]
        down = (scale * scaled - scale * scale * scale * out * jnp.mean(scaled * out, -1, keepdims=True)).astype(bf16)
        heads.append((q[:, lanes], k[:, lanes], down, head_beta(bl[...], group * hb + h, valid), e[:, lanes]))
    cells = [(h, c) for h in range(hb) for c in range(count)]
    scores = [jnp.where(rows >= cols, dot_nt(heads[h][0][spans[c]], heads[h][1][spans[c]]), 0.0).astype(bf16) for h, c in cells]
    errs = [dot_tn(m, heads[h][2][spans[c]]).astype(bf16) for m, (h, c) in zip(scores, cells)]
    firsts = [dot_tn(t[h, c], jnp.concatenate([r, heads[h][1][spans[c]]], 1)) for r, (h, c) in zip(errs, cells)]
    adds = [dot_tn(heads[h][0][spans[c]], heads[h][2][spans[c]]) for h, c in cells]
    states = [jnp.zeros((HD, HD), f32)] * hb
    backs, outs, gls = {}, {}, {}
    for c in reversed(range(count)):
        s = spans[c]
        for h in range(hb):
            cell = h * count + c
            low = states[h].astype(bf16)
            outs[h, c] = low
            full = firsts[cell][:, :HD] + dot(firsts[cell][:, HD:].astype(bf16), low)
            beta = heads[h][3][s]
            gls[h, c] = jnp.sum(full * heads[h][4][s].astype(f32), -1, keepdims=True) * (1.0 - beta)
            backs[h, c] = full * beta
            states[h] = states[h] + adds[cell] - dot_tn(heads[h][1][s], backs[h, c].astype(bf16))
    lane = lax.broadcasted_iota(jnp.int32, (length, HD), 1)
    total = jnp.zeros((length, HD), f32)
    grads = ([], [], [])
    for h in range(hb):
        gl = jnp.concatenate([gls[h, c] for c in range(count)], 0)
        total = jnp.where((lane == group * hb + h) & valid, gl, total)
        qh, kh, dh, _, err = heads[h]
        grads[2].append(jnp.concatenate([backs[h, c] for c in range(count)], 0))
        left = [jnp.concatenate([dh[s], (-backs[h, c]).astype(bf16)], 0) for c, s in enumerate(spans)]
        pairs = [dot_nt(p, err[s]) for p, s in zip(left, spans)]
        pairs = [jnp.concatenate([jnp.where(rows >= cols, p[:CHUNK], 0.0), jnp.where(rows > cols, p[CHUNK:], 0.0)], 0).astype(bf16) for p in pairs]
        first = [dot_nt(p, s_c[h, c]) for c, p in enumerate(left)]
        second = [dot(p, kh[s]) for p, s in zip(pairs, spans)]
        third = [dot_nt(err[s], outs[h, c]) for c, s in enumerate(spans)]
        fourth = [dot_tn(p, jnp.concatenate([qh[s], kh[s]], 0)) for p, s in zip(pairs, spans)]
        grads[0].append(jnp.concatenate([a[:CHUNK] + b[:CHUNK] for a, b in zip(first, second)], 0))
        grads[1].append(jnp.concatenate([a[CHUNK:] + b[CHUNK:] + x + y for a, b, x, y in zip(first, second, third, fourth)], 0))
    gp_ref[:, logits_at] = gp_ref[:, logits_at] + total.astype(bf16)
    for i, (p, w) in enumerate(((pq, wq), (pk, wk), (pv, wv))):
        ext[0:8, :] = jnp.zeros((8, width), f32)
        ext[8:, :] = jnp.where(valid, p[...], 0.0)
        pre = conv_rows(ext, w, length)
        sig = jax.nn.sigmoid(pre)
        pieces = []
        for h in range(hb):
            grad = grads[i][h]
            if i < 2:
                raw = (pre * sig)[:, h * HD:(h + 1) * HD]
                scale = lax.rsqrt(jnp.sum(raw * raw, -1, keepdims=True) + 1e-06)
                grad = scale * (grad - scale * scale * raw * jnp.sum(raw * grad, -1, keepdims=True))
                if i == 0:
                    grad = grad * HD ** -0.5
            pieces.append(grad)
        grad = jnp.concatenate(pieces, 1) if hb > 1 else pieces[0]
        grad = grad * sig * (1.0 + pre * (1.0 - sig))
        gext[0:length, :] = grad
        gext[length:, :] = jnp.zeros((8, width), f32)
        at = pl.ds(pl.multiple_of(i * heads_all * HD + group * width, HD), width)
        for j in range(KERNEL):
            conv_ref[j:j + 1, at] = jnp.sum(grad * ext[5 + j:5 + j + length, :], 0, keepdims=True)
        back = w[3:4] * grad
        for j in range(KERNEL - 1):
            back = back + w[j:j + 1] * gext[3 - j:3 - j + length, :]
        gp_ref[:, at] = jnp.where(valid, back, 0.0).astype(bf16)


def mixer_backward(gm, o, q, k, t, e, s_c, projected, conv_w, gain, nv):
    length = gm.shape[0]
    heads, nc = t.shape[:2]
    hb = heads_per_step(heads)
    groups = heads // hb
    w = hb * HD
    tok = pl.BlockSpec((length, w), lambda i, *_: (0, i))
    sq = pl.BlockSpec((hb, nc, HD, HD), lambda i, *_: (i, 0, 0, 0))
    col = lambda off: (lambda i, *_: (0, i + off * groups))
    fixed = lambda shape: pl.BlockSpec(shape, lambda i, *_: (0, 0))
    in_specs = [tok, tok, tok, tok, sq, tok, sq, pl.BlockSpec((length, HD), lambda i, *_: (0, 3 * heads))]
    in_specs += [pl.BlockSpec((length, w), col(n)) for n in range(3)]
    in_specs += [pl.BlockSpec((KERNEL, w), col(n)) for n in range(3)]
    in_specs += [fixed((1, HD))]
    wide = (length, (3 * heads + 1) * HD)
    return pl.pallas_call(
        functools.partial(mixer_backward_kernel, hb, heads),
        out_shape=(
            jax.ShapeDtypeStruct(wide, bf16),
            jax.ShapeDtypeStruct((KERNEL, 3 * heads * HD), f32),
            jax.ShapeDtypeStruct((8, HD), f32),
        ),
        grid_spec=pltpu.PrefetchScalarGridSpec(
            num_scalar_prefetch=1, grid=(groups,), in_specs=in_specs,
            out_specs=(fixed(wide), fixed((KERNEL, 3 * heads * HD)), fixed((8, HD))),
            scratch_shapes=[pltpu.VMEM((length + 8, w), f32), pltpu.VMEM((length + 8, w), f32)]),
        name="mixer_backward",
    )(nv, gm, o, q, k, t, e, s_c, projected, projected, projected, projected, conv_w, conv_w, conv_w, gain)


def xor(value, axis, step):
    return lax.ppermute(value, axis, [(i, i ^ step) for i in range(lax.axis_size(axis))])


def pick(tensor, index, axis=0):
    return lax.dynamic_index_in_dim(tensor, index, axis, keepdims=False)


def added(a, b):
    return (a.astype(f32) + b.astype(f32)).astype(bf16)


def direct():
    return (lax.axis_size("dp"), lax.axis_size("fsdp"), lax.axis_size("ctx")) == (4, 4, 2)


def mixer_columns(weight, heads):
    n = lax.axis_size("ctx")
    view = weight.reshape(weight.shape[0], 3, heads // n, n, HD)
    return pick(view, lax.axis_index("ctx"), 3).reshape(weight.shape[0], -1)


def beta_columns(weight, heads):
    n = lax.axis_size("ctx")
    view = weight.reshape(weight.shape[0], heads // n, n)
    return jnp.pad(pick(view, lax.axis_index("ctx"), 2), ((0, 0), (0, HD - heads // n)))


def feed_columns(weight):
    n = lax.axis_size("ctx")
    view = weight.reshape(weight.shape[0], 2, n, weight.shape[1] // (2 * n))
    return pick(view, lax.axis_index("ctx"), 2).reshape(weight.shape[0], -1)


def after(value, *others):
    return lax.optimization_barrier((value,) + others)


def start_pieces(tags, places, sources, outs, sems, z, d):
    copies = []
    for tag in tags:
        source, at_first, row_step, same, other = tag
        for at, index, row, col in places(tag, z ^ row_step, other if same else d ^ other):
            rows, width = (s.stop - s.start for s in at)
            target = outs[index].at[pl.ds(row, rows), pl.ds(col, width)]
            copy = pltpu.make_async_copy(
                sources[source].at[at_first + at], target, sems.at[len(copies)]
            )
            copy.start()
            copies.append(copy)
    return copies


def positions():
    return jnp.stack([lax.axis_index(a) for a in ("fsdp", "dp", "ctx")]).astype(jnp.int32)


def project_kernel(tags, places, count, where_ref, x_own, x_far, gain, *refs):
    sources = refs[:count]
    normed_ref, out_ref, full_ref, weight, sems, out_sem = refs[count:]
    step, steps = pl.program_id(0), pl.num_programs(0)
    z, d, c = where_ref[0], where_ref[1], where_ref[2]
    kept = pltpu.make_async_copy(weight, full_ref, out_sem)

    @pl.when(step == 0)
    def _():
        for copy in start_pieces(tags, places, sources, (weight,), sems, z, d):
            copy.wait()
        kept.start()

    x = jnp.where(step // (steps // 2) == c, x_own[...], x_far[...]).astype(f32)
    scale = lax.rsqrt(jnp.mean(x * x, -1, keepdims=True) + 1e-06)
    normed = (x * scale * gain[...]).astype(bf16)
    normed_ref[...] = normed
    out_ref[...] = dot(normed, weight[...])

    @pl.when(step == steps - 1)
    def _():
        kept.wait()


def project(x_own, x_far, gain, pieces, width):
    arrays, tags, places = pieces
    rows, depth = x_own.shape
    block = rows // 2
    half = pl.BlockSpec((block, depth), lambda i, *_: (i % 2, 0))
    each = lambda w: pl.BlockSpec((block, w), lambda i, *_: (i, 0))
    anywhere = pl.BlockSpec(memory_space=pl.ANY)
    return pl.pallas_call(
        functools.partial(project_kernel, tags, places, len(arrays)),
        out_shape=(
            jax.ShapeDtypeStruct((2 * rows, depth), bf16),
            jax.ShapeDtypeStruct((2 * rows, width), f32),
            jax.ShapeDtypeStruct((depth, width), bf16),
        ),
        grid_spec=pltpu.PrefetchScalarGridSpec(
            num_scalar_prefetch=1,
            grid=(4,),
            in_specs=[half, half, pl.BlockSpec((1, depth), lambda i, *_: (0, 0))]
            + [anywhere] * len(arrays),
            out_specs=(each(depth), each(width), anywhere),
            scratch_shapes=[
                pltpu.VMEM((depth, width), bf16),
                pltpu.SemaphoreType.DMA((len(tags),)),
                pltpu.SemaphoreType.DMA,
            ],
        ),
        name="projections",
    )(positions(), x_own, x_far, gain, *arrays)


def near_first(i, where):
    return ((where[2] * 2 + i) % 4, 0)


def attend_kernel(tags, places, count, where_ref, merged, *refs):
    sources = refs[:count]
    near, far, full_ref, weight, sems, out_sem = refs[count:]
    step, steps = pl.program_id(0), pl.num_programs(0)
    z, d = where_ref[0], where_ref[1]
    kept = pltpu.make_async_copy(weight, full_ref, out_sem)

    @pl.when(step == 0)
    def _():
        for copy in start_pieces(tags, places, sources, (weight,), sems, z, d):
            copy.wait()
        kept.start()

    total = dot(merged[...], weight[...])

    @pl.when(step < 2)
    def _():
        near[...] = total

    @pl.when(step >= 2)
    def _():
        far[...] = total.astype(bf16)

    @pl.when(step == steps - 1)
    def _():
        kept.wait()


def near_spec(block, width):
    return pl.BlockSpec((block, width), lambda i, *_: (jnp.minimum(i, 1), 0))


def far_spec(block, width):
    return pl.BlockSpec((block, width), lambda i, *_: (jnp.maximum(i - 2, 0), 0))


def attend(merged, pieces, width):
    arrays, tags, places = pieces
    rows, depth = merged.shape
    block = rows // 4
    anywhere = pl.BlockSpec(memory_space=pl.ANY)
    return pl.pallas_call(
        functools.partial(attend_kernel, tags, places, len(arrays)),
        out_shape=(
            jax.ShapeDtypeStruct((rows // 2, width), f32),
            jax.ShapeDtypeStruct((rows // 2, width), bf16),
            jax.ShapeDtypeStruct((depth, width), bf16),
        ),
        grid_spec=pltpu.PrefetchScalarGridSpec(
            num_scalar_prefetch=1,
            grid=(4,),
            in_specs=[pl.BlockSpec((block, depth), near_first)] + [anywhere] * len(arrays),
            out_specs=(near_spec(block, width), far_spec(block, width), anywhere),
            scratch_shapes=[
                pltpu.VMEM((depth, width), bf16),
                pltpu.SemaphoreType.DMA((2 * len(tags),)),
                pltpu.SemaphoreType.DMA,
            ],
        ),
        name="mixer_out",
    )(positions(), merged, *arrays)


def merged_grad_kernel(where_ref, own, far, weight, out):
    grad = jnp.where(pl.program_id(0) < 2, own[...], far[...])
    out[...] = dot_nt(grad, weight[...])


def merged_grad(own, far, weight):
    rows, width = own.shape
    depth = weight.shape[0]
    block = rows // 2
    return pl.pallas_call(
        merged_grad_kernel,
        out_shape=jax.ShapeDtypeStruct((2 * rows, depth), f32),
        grid_spec=pltpu.PrefetchScalarGridSpec(
            num_scalar_prefetch=1,
            grid=(4,),
            in_specs=[
                near_spec(block, width),
                far_spec(block, width),
                pl.BlockSpec((depth, width), lambda i, *_: (0, 0)),
            ],
            out_specs=pl.BlockSpec((block, depth), near_first),
        ),
        name="merged_gradient",
    )(positions(), own, far, weight)


def normed_grad_kernel(where_ref, grad, weight, near, far):
    total = dot_nt(grad[...], weight[...])

    @pl.when(pl.program_id(0) < 2)
    def _():
        near[...] = total

    @pl.when(pl.program_id(0) >= 2)
    def _():
        far[...] = total.astype(bf16)


def normed_grad(grad, weight):
    rows, width = grad.shape
    depth = weight.shape[0]
    block = rows // 4
    return pl.pallas_call(
        normed_grad_kernel,
        out_shape=(
            jax.ShapeDtypeStruct((rows // 2, depth), f32),
            jax.ShapeDtypeStruct((rows // 2, depth), bf16),
        ),
        grid_spec=pltpu.PrefetchScalarGridSpec(
            num_scalar_prefetch=1,
            grid=(4,),
            in_specs=[
                pl.BlockSpec((block, width), near_first),
                pl.BlockSpec((depth, width), lambda i, *_: (0, 0)),
            ],
            out_specs=(near_spec(block, depth), far_spec(block, depth)),
        ),
        name="normed_gradient",
    )(positions(), grad, weight)


def weight_grad_kernel(parts, with_out, where_ref, *refs):
    lefts, grad = refs[:parts], refs[parts]
    z = pl.program_id(0)
    d, c = where_ref[1], where_ref[2]
    first_low, first_high = d % 2 == 0, d // 2 == 0
    total, at = 0.0, 0
    for left in lefts:
        rows = left.shape[0]
        total = total + dot_tn(left[...], grad[at : at + rows, :])
        at += rows
    total = total.astype(bf16)
    short = total.shape[0] // 8
    blocks = [total[i * short : (i + 1) * short] for i in range(8)]
    if with_out:
        merged, own, far = refs[parts + 1 : parts + 4]
        rows, half = own.shape[0], own.shape[1] // 2
        mine = merged[pl.ds(pl.multiple_of(c * rows, rows), rows), :]
        theirs = merged[pl.ds(pl.multiple_of((1 - c) * rows, rows), rows), :]
        out = (dot_tn(mine, own[...]) + dot_tn(theirs, far[...])).astype(bf16)
        lines = short // 2
        for i in range(8):
            part = out[i * lines : (i + 1) * lines]
            part = jnp.concatenate([part[:, :half], part[:, half:]], 0)
            blocks[i] = jnp.concatenate([blocks[i], part], 1)
    low_keep, low_send, high_keep, high_send = refs[-4:]

    @pl.when(z < 2)
    def _():
        for i in range(4):
            a, b = blocks[2 * i], blocks[2 * i + 1]
            low_keep[0, i // 2, i % 2] = jnp.where(first_low, a, b)
            low_send[0, i // 2, i % 2] = jnp.where(first_low, b, a)

    @pl.when(z >= 2)
    def _():
        for i in range(4):
            k = (i // 2) * 4 + i % 2
            a, b = blocks[k], blocks[k + 2]
            high_keep[0, i // 2, i % 2] = jnp.where(first_high, a, b)
            high_send[0, i // 2, i % 2] = jnp.where(first_high, b, a)


def weight_grad(lefts, grad, out=()):
    depth = lefts[0].shape[1] // 4
    width = grad.shape[1] + (out[1].shape[1] // 2 if out else 0)
    short = depth // 8
    shape = jax.ShapeDtypeStruct((2, 2, 2, short, width), bf16)
    low = pl.BlockSpec((1, 2, 2, short, width), lambda i, *_: (jnp.minimum(i, 1), 0, 0, 0, 0))
    high = pl.BlockSpec((1, 2, 2, short, width), lambda i, *_: (jnp.maximum(i - 2, 0), 0, 0, 0, 0))
    whole = lambda a: pl.BlockSpec(a.shape, lambda i, *_: (0, 0))
    column = lambda a: pl.BlockSpec((a.shape[0], a.shape[1] // 4), lambda i, *_: (0, i))
    specs = [column(a) for a in lefts] + [whole(grad)]
    if out:
        specs += [column(out[0]), whole(out[1]), whole(out[2])]
    return pl.pallas_call(
        functools.partial(weight_grad_kernel, len(lefts), bool(out)),
        out_shape=(shape,) * 4,
        grid_spec=pltpu.PrefetchScalarGridSpec(
            num_scalar_prefetch=1, grid=(4,), in_specs=specs, out_specs=(low, low, high, high)
        ),
        name="weight_gradient",
    )(positions(), *lefts, grad, *out)


def down_grad_kernel(hidden, own, far, out):
    rows = own.shape[0]
    total = dot_tn(hidden[:rows, :], own[...]) + dot_tn(hidden[rows:, :], far[...])
    out[...] = total.astype(bf16)


def down_gradient(hidden, own, far):
    rows, width = own.shape
    half = hidden.shape[1]
    return pl.pallas_call(
        down_grad_kernel,
        out_shape=jax.ShapeDtypeStruct((half, width), bf16),
        grid=(half // HD,),
        in_specs=[
            pl.BlockSpec((2 * rows, HD), lambda i: (0, i)),
            pl.BlockSpec((rows, width), lambda i: (0, 0)),
            pl.BlockSpec((rows, width), lambda i: (0, 0)),
        ],
        out_specs=pl.BlockSpec((HD, width), lambda i: (i, 0)),
        name="down_gradient",
    )(hidden, own, far)


def whole_rows(weight):
    return lax.all_gather(weight, "fsdp", axis=0, tiled=True)


def exchange(blocks, axis):
    return lax.all_to_all(blocks, axis, 0, 0, tiled=True)


def to_all(piece, axis):
    return exchange(jnp.broadcast_to(piece, (lax.axis_size(axis),) + piece.shape), axis)


def bounds(total, step):
    return [slice(i, min(i + step, total)) for i in range(0, total, step)]


def feed_kernel(tags, places, count_down, own, where_ref, x_own, x_other, e_own, e_other, *refs):
    count = 1 + max(t[0] for t in tags)
    sources, downs = refs[:count], refs[count : count + count_down]
    hidden_ref, grad_ref, near_out, far_out, near_grad, far_grad = refs[count + count_down : -3]
    gateup, down, sems = refs[-3:]
    step = pl.program_id(0)
    z, d, c = where_ref[0], where_ref[1], where_ref[2]

    @pl.when(step == 0)
    def _():
        copies = start_pieces(tags, places, sources, (gateup,), sems, z, d)
        rows, cols = downs[1].shape[1:]
        for j in range(2):
            for source, at, first in ((downs[0], 2 * c + j, c), (downs[1], j, 1 - c)):
                col = pl.multiple_of(first * cols, HD)
                copy = pltpu.make_async_copy(
                    source.at[at],
                    down.at[pl.ds(j * rows, rows), pl.ds(col, cols)],
                    sems.at[len(copies)],
                )
                copy.start()
                copies.append(copy)
        for copy in copies:
            copy.wait()

    near = step < own
    x = jnp.where(near, x_own[...], x_other[...])
    e = jnp.where(near, e_own[...], e_other[...])
    half = down.shape[0]
    for j in bounds(half, 256):
        up_j = slice(half + j.start, half + j.stop)
        gate = dot(x, gateup[:, j])
        up = dot(x, gateup[:, up_j])
        grad = dot_nt(e, down[j, :])
        sig = jax.nn.sigmoid(gate)
        act = gate * sig
        hidden_ref[:, j] = (act * up).astype(bf16)
        grad_ref[:, j] = (grad * up * sig * (1.0 + gate * (1.0 - sig))).astype(bf16)
        grad_ref[:, up_j] = (grad * act).astype(bf16)
    out = dot(hidden_ref[...], down[...])
    back = dot_nt(grad_ref[...], gateup[...])

    @pl.when(near)
    def _():
        near_out[...] = out
        near_grad[...] = back

    @pl.when(jnp.logical_not(near))
    def _():
        far_out[...] = out.astype(bf16)
        far_grad[...] = back.astype(bf16)


def feed(x_own, x_other, e_own, e_other, wide, down):
    arrays, tags, places = wide
    rows, width = x_own.shape
    others = x_other.shape[0]
    half = 2 * down[1].shape[1]
    block = min(256, rows)
    own, steps = rows // block, (rows + others) // block
    near = lambda w: pl.BlockSpec((block, w), lambda i, *_: (jnp.minimum(i, own - 1), 0))
    far = lambda w: pl.BlockSpec((block, w), lambda i, *_: (jnp.maximum(i - own, 0), 0))
    each = lambda w: pl.BlockSpec((block, w), lambda i, *_: (i, 0))
    anywhere = pl.BlockSpec(memory_space=pl.ANY)
    return pl.pallas_call(
        functools.partial(feed_kernel, tags, places, len(down), own),
        out_shape=(
            jax.ShapeDtypeStruct((rows + others, half), bf16),
            jax.ShapeDtypeStruct((rows + others, 2 * half), bf16),
            jax.ShapeDtypeStruct((rows, width), f32),
            jax.ShapeDtypeStruct((others, width), bf16),
            jax.ShapeDtypeStruct((rows, width), f32),
            jax.ShapeDtypeStruct((others, width), bf16),
        ),
        grid_spec=pltpu.PrefetchScalarGridSpec(
            num_scalar_prefetch=1,
            grid=(steps,),
            in_specs=[near(width), far(width), near(width), far(width)]
            + [anywhere] * (len(arrays) + len(down)),
            out_specs=(each(half), each(2 * half), near(width), far(width), near(width), far(width)),
            scratch_shapes=[
                pltpu.VMEM((width, 2 * half), bf16),
                pltpu.VMEM((half, width), bf16),
                pltpu.SemaphoreType.DMA((4 + len(tags),)),
            ],
        ),
        name="feed_forward",
    )(positions(), x_own, x_other, e_own, e_other, *arrays, *down)


def pack_kernel(heads, where_ref, qkv, beta, out, gateup, all_ref, mixed_ref, wide_ref):
    rows = qkv.shape[0]
    strips = qkv.shape[1] // (2 * HD)
    mixed = (strips + 1) * HD
    width = gateup.shape[1] // 4
    half = out.shape[1] // 2
    short = out.shape[0]
    for c in range(2):

        @pl.when(where_ref[1] == c)
        def _():
            for i in range(strips):
                at = (2 * i + c) * HD
                all_ref[:, i * HD : (i + 1) * HD] = qkv[:, at : at + HD]
            source = lax.broadcasted_iota(jnp.int32, (heads, HD), 0)
            lane = lax.broadcasted_iota(jnp.int32, (heads, HD), 1)
            chosen = (source == 2 * lane + c).astype(f32).astype(bf16)
            all_ref[:, strips * HD : mixed] = dot(beta[...], chosen).astype(bf16)
            for i in range(2):
                at = (2 * i + c) * width
                to = mixed + i * width
                all_ref[:, to : to + width] = gateup[:, at : at + width]

    last = mixed + 2 * width
    all_ref[:short, last:] = out[:, :half]
    all_ref[short:, last:] = out[:, half:]
    for i in range(4):
        mixed_ref[i] = all_ref[:, :mixed]
    wide_ref[...] = all_ref[:, mixed:]


def pack(w_qkv, w_beta, w_out, w_gateup):
    rows, short = w_qkv.shape[0] // 4, HD // 4
    heads = w_beta.shape[1]
    here = jnp.stack([lax.axis_index("dp"), lax.axis_index("ctx")]).astype(jnp.int32)
    mixed = w_qkv.shape[1] // 2 + HD
    wide = w_gateup.shape[1] // 2 + w_out.shape[1] // 2
    fixed = lambda *shape: pl.BlockSpec(shape, lambda i, *_: (0,) * len(shape))
    mine = lambda width: pl.BlockSpec((rows, width), lambda i, at: (at[0], 0))
    shapes = ((rows, mixed + wide), (4, rows, mixed), (rows, wide))
    return pl.pallas_call(
        functools.partial(pack_kernel, heads),
        out_shape=tuple(jax.ShapeDtypeStruct(s, bf16) for s in shapes),
        grid_spec=pltpu.PrefetchScalarGridSpec(
            num_scalar_prefetch=1,
            grid=(1,),
            in_specs=[
                mine(w_qkv.shape[1]),
                mine(heads),
                pl.BlockSpec((short, w_out.shape[1]), lambda i, at: (at[1] * 4 + at[0], 0)),
                mine(w_gateup.shape[1]),
            ],
            out_specs=tuple(fixed(*s) for s in shapes),
        ),
        name="weight_pieces",
    )(here, w_qkv, w_beta, w_out, w_gateup)


def gather_direct(pieces, mixed_piece, wide_piece, down_shard):
    z, c = lax.axis_index("fsdp"), lax.axis_index("ctx")
    own = [pieces] + [xor(pieces, "dp", k) for k in (1, 2, 3)]
    rows = exchange(mixed_piece, "fsdp")
    wide_piece, rows = after(wide_piece, rows)
    wide_rows = [xor(wide_piece, "fsdp", k) for k in (1, 2, 3)]
    rows, *own[1:] = after(rows, *own[1:])
    rest = to_all(jnp.stack([pick(rows, z ^ k) for k in (1, 2, 3)]), "dp")
    half = down_shard.shape[1] // 2
    mine = lax.dynamic_slice_in_dim(down_shard, c * half, half, 1)
    rest, mine, *wide_rows = after(rest, mine, *wide_rows)
    down = to_all(mine, "fsdp")
    half = pieces.shape[1] // 3
    low = jnp.stack([w[:, :half] for w in wide_rows])
    high = jnp.stack([w[:, half:] for w in wide_rows])
    low, high = [low, xor(low, "dp", 1)], [high, xor(high, "dp", 2)]
    own_tags = [(k, (), 0, False, k) for k in range(4)]
    mixed_tags = own_tags + [(4, (i, k - 1), k, True, i) for i in range(4) for k in (1, 2, 3)]
    return own, rest, low, high, mixed_tags, down


def spread_further(own, low, high):
    low = low + [xor(low[0], "dp", 2), xor(low[1], "dp", 2)]
    high = [high[0], xor(high[0], "dp", 1), high[1], xor(high[1], "dp", 1)]
    tags = [(k, (), 0, False, k) for k in range(4)]
    tags += [(4 + i, (k - 1,), k, False, i) for i in range(4) for k in (1, 2, 3)]
    tags += [(8 + i, (k - 1,), k, False, i) for i in range(4) for k in (1, 2, 3)]
    return own + low + high, tags


def gather_weights(w_qkv, w_beta, w_out, w_gateup, w_down, heads):
    n, c = lax.axis_size("ctx"), lax.axis_index("ctx")
    if not direct():
        mixed = jnp.concatenate([mixer_columns(w_qkv, heads), beta_columns(w_beta, heads)], 1)
        out = whole_rows(w_out).reshape(heads // n, n, HD, -1)
        down = whole_rows(w_down)
        return (
            whole_rows(mixed),
            whole_rows(feed_columns(w_gateup)),
            pick(out, c, 1).reshape(-1, w_out.shape[1]),
            pick(down.reshape(n, -1, down.shape[1]), c),
        )
    rows, short = w_qkv.shape[0] // 4, HD // 4
    pieces, mixed_piece, wide_piece = pack(w_qkv, w_beta, w_out, w_gateup)
    mixed, width, half = mixed_piece.shape[2], w_gateup.shape[1] // 2, w_out.shape[1] // 2
    own, rest, low, high, mixed_tags, down = gather_direct(
        pieces, mixed_piece, wide_piece, w_down
    )
    cut = low[0].shape[2]

    def mixed_places(tag, z, d):
        row = pl.multiple_of(z * (4 * rows) + d * rows, rows)
        return [((slice(0, rows), slice(0, mixed)), 0, row, 0)]

    def out_places(tag, z, d):
        row = pl.multiple_of(z * HD + d * short, short)
        if tag[0] < 4:
            at = slice(mixed + width, mixed + width + half)
        else:
            at = slice(width - cut, width - cut + half)
        return [
            ((slice(0, short), at), 0, row, 0),
            ((slice(short, 2 * short), at), 0, row, half),
        ]

    def feed_places(tag, z, d):
        row = pl.multiple_of(z * (4 * rows) + d * rows, rows)
        if tag[0] < 4:
            at, col = slice(mixed, mixed + width), 0
        elif tag[0] < 8:
            at, col = slice(0, cut), 0
        else:
            at, col = slice(0, width - cut), cut
        return [((slice(0, rows), at), 0, row, col)]

    def further(full):
        full, low[1], high[1] = after(full, low[1], high[1])
        wide_all, wide_tags = spread_further(own, low, high)
        out_tags = [t for t in wide_tags if not 4 <= t[0] < 8]
        return full, (wide_all, wide_tags, feed_places), (wide_all, out_tags, out_places)

    return (own + [rest], mixed_tags, mixed_places), further, down


def feed_both(normed, grad_feed, gateup, down):
    if direct():
        normed_far, grad_far = xor(normed, "ctx", 1), xor(grad_feed, "ctx", 1)
        theirs = pick(down.reshape((2, 2) + down.shape[1:]), 1 - lax.axis_index("ctx"))
        down = [down, xor(theirs, "ctx", 1)]
        hidden, grad, out, out_far, back, back_far = feed(
            normed, normed_far, grad_feed, grad_far, gateup, down
        )
        out = out + xor(out_far, "ctx", 1).astype(f32)
        back = back + xor(back_far, "ctx", 1).astype(f32)
        return (normed, normed_far), (grad_feed, grad_far), hidden, grad, out, back
    normed, grad_feed = both_pieces(normed), both_pieces(grad_feed)
    gate_up = jnp.dot(normed, gateup, preferred_element_type=f32)
    ff_width = gate_up.shape[1] // 2
    gate_part = gate_up[:, :ff_width]
    up_part = gate_up[:, ff_width:]
    gate_sig = jax.nn.sigmoid(gate_part)
    hidden = (gate_part * gate_sig * up_part).astype(bf16)
    contract_cols = (((1,), (1,)), ((), ()))
    grad_hidden = lax.dot_general(grad_feed, down, contract_cols, preferred_element_type=f32)
    grad_gate = grad_hidden * up_part * gate_sig * (1.0 + gate_part * (1.0 - gate_sig))
    grad = jnp.concatenate([grad_gate, grad_hidden * gate_part * gate_sig], 1).astype(bf16)
    out = own_piece(jnp.dot(hidden, down, preferred_element_type=f32))
    back = own_piece(lax.dot_general(grad, gateup, contract_cols, preferred_element_type=f32))
    return normed, grad_feed, hidden, grad, out, back


def both_pieces(mine):
    n = lax.axis_size("ctx")
    if n != 2:
        return lax.all_gather(mine, "ctx", axis=0, tiled=True)
    other = xor(mine, "ctx", 1)
    first = lax.axis_index("ctx") == 0
    return jnp.concatenate([jnp.where(first, mine, other), jnp.where(first, other, mine)], 0)


def own_piece(partial):
    n = lax.axis_size("ctx")
    rows = partial.shape[0] // n
    if n != 2:
        return lax.psum_scatter(
            partial.astype(bf16), "ctx", scatter_dimension=0, tiled=True
        ).astype(f32)
    here = lax.axis_index("ctx")
    theirs = lax.dynamic_slice_in_dim(partial, (1 - here) * rows, rows, 0).astype(bf16)
    mine = lax.dynamic_slice_in_dim(partial, here * rows, rows, 0)
    return mine.astype(f32) + xor(theirs, "ctx", 1).astype(f32)


def replicas_first(part):
    d = lax.axis_index("dp")
    high, low = d // 2, d % 2
    a, b = part[:2], part[2:]
    got = xor(pick(a, 1 - low, 3), "dp", 1), xor(pick(b, 1 - high, 2), "dp", 2)
    return (pick(a, low, 3), pick(b, high, 2)), got


def replicas_second(kept, got):
    d = lax.axis_index("dp")
    high, low = d // 2, d % 2
    a, b = added(kept[0], got[0]), added(kept[1], got[1])
    got = xor(pick(a, 1 - high, 2), "dp", 2), xor(pick(b, 1 - low, 2), "dp", 1)
    return (pick(a, high, 2), pick(b, low, 2)), got


def rows_sent(kept, got):
    z = lax.axis_index("fsdp")
    part = jnp.concatenate([added(kept[0], got[0]), added(kept[1], got[1])], 0)
    return pick(part, z), [xor(pick(part, z ^ k), "fsdp", k) for k in (1, 2, 3)]


def summed_rows(own, got):
    total = own.astype(f32)
    for part in got:
        total = total + part.astype(f32)
    return total.astype(bf16)


def both_columns(part):
    c = lax.axis_index("ctx")
    other = xor(pick(part, 1 - c), "ctx", 1)
    mine = pick(part, c)
    first = c == 0
    return jnp.stack([jnp.where(first, mine, other), jnp.where(first, other, mine)])


def finish_kernel(moves, source, *outs):
    for at, index, to in moves:
        outs[index][to] = source[at].astype(f32)


def finish(source, moves, shapes, name):
    return pl.pallas_call(
        functools.partial(finish_kernel, moves),
        out_shape=tuple(jax.ShapeDtypeStruct(s, f32) for s in shapes),
        name=name,
    )(source)


def blocks_of(grad, n, z):
    return grad.reshape(z, n, 2, 2, grad.shape[0] // (4 * z * n), grad.shape[1])


def scattered(full):
    share = lax.psum_scatter(full.astype(bf16), ("fsdp", "ctx"), scatter_dimension=0, tiled=True)
    return lax.psum(share, "dp").astype(f32)


def placed_at_ctx(part, axis):
    n = lax.axis_size("ctx")
    shape = [1] * (part.ndim + 1)
    shape[axis] = n
    here = (jnp.arange(n) == lax.axis_index("ctx")).reshape(shape)
    return jnp.where(here, jnp.expand_dims(part, axis), 0)


def sum_columns(grad, views, widths):
    outs, start = [], 0
    for shape, size in zip(views, widths):
        part = grad[:, start : start + size].reshape((grad.shape[0],) + shape)
        full = placed_at_ctx(part, part.ndim - 1)
        outs.append(scattered(full.reshape(grad.shape[0], -1)))
        start += size
    return outs


def added_up(parts):
    total = parts[0].astype(f32)
    for i in range(1, parts.shape[0]):
        total = total + parts[i].astype(f32)
    return total.astype(bf16)


def down_summed(got):
    part = added_up(got)
    rows, cols = part.shape[0], part.shape[1] // 4
    part = added_up(exchange(jnp.transpose(part.reshape(rows, 4, cols), (1, 0, 2)), "dp"))
    pairs = [(z * 2 + c, (2 * c + z // 2) * 2 + z % 2) for z in range(4) for c in range(2)]
    every = to_all(lax.ppermute(part, ("fsdp", "ctx"), pairs), "dp")
    moves = [((i,), 0, (slice(None), slice(i * cols, (i + 1) * cols))) for i in range(4)]
    return finish(every, moves, [(rows, 4 * cols)], "down_total")[0]


def sum_small(vector):
    if not direct():
        return lax.psum(vector, ("dp", "fsdp", "ctx"))
    for axis, step in (("ctx", 1), ("dp", 1), ("dp", 2), ("fsdp", 1), ("fsdp", 2)):
        vector = vector + xor(vector, axis, step)
    return vector


def local(
    inputs,
    lengths,
    cotangent,
    norm_gain1,
    w_qkv,
    w_beta,
    conv_weight,
    head_gain,
    w_out,
    norm_gain2,
    w_gateup,
    w_down,
):
    n = lax.axis_size("ctx")
    heads_all = w_beta.shape[1]
    heads = heads_all // n
    tokens_in = inputs[0].astype(f32)
    piece_len, model_width = tokens_in.shape
    length = piece_len * n
    conv_mine = mixer_columns(conv_weight, heads_all)
    positions_here = jnp.arange(length, dtype=jnp.int32)
    start = lax.axis_index("ctx") * piece_len
    valid = ((start + positions_here[:piece_len]) < lengths[0]).astype(f32)[:, None]
    grad_feed = (cotangent[0].astype(f32) * valid).astype(bf16)
    if direct():
        pieces, further, down = gather_weights(w_qkv, w_beta, w_out, w_gateup, w_down, heads_all)
        far_rows = xor(inputs[0], "ctx", 1)
        normed_one, projected, mixed = project(
            inputs[0], far_rows, norm_gain1[None], pieces, (3 * heads + 1) * HD
        )
        projected, gateup, out = further(projected)
    else:
        mixed, gateup, out, down = gather_weights(
            w_qkv, w_beta, w_out, w_gateup, w_down, heads_all
        )
        tokens_all = both_pieces(inputs[0]).astype(f32)
        scale_all = lax.rsqrt(jnp.mean(tokens_all * tokens_all, -1, keepdims=True) + 1e-06)
        normed_one = (tokens_all * scale_all * norm_gain1).astype(bf16)
        projected = jnp.dot(normed_one, mixed, preferred_element_type=f32)
    queries, keys, inverse, errors, states, heads_out, merged = mixer_forward(
        projected, conv_mine, head_gain[None], lengths, heads
    )
    if direct():
        near, far, out = attend(merged, out, model_width)
        attention = near + xor(far, "ctx", 1).astype(f32)
    else:
        attention = own_piece(jnp.dot(merged, out, preferred_element_type=f32))
    middle = tokens_in + attention
    scale_two = lax.rsqrt(jnp.mean(middle * middle, -1, keepdims=True) + 1e-06)
    normed_two = (middle * scale_two * norm_gain2).astype(bf16)
    normed_two, feed_all, hidden, grad_gate_up, feed_out, grad_normed_two = feed_both(
        normed_two, grad_feed, gateup, down
    )
    output = (middle + feed_out).astype(bf16)
    contract_cols = (((1,), (1,)), ((), ()))
    contract_rows = (((0,), (0,)), ((), ()))
    ff_width = hidden.shape[1]
    if direct():
        down_grad = down_gradient(hidden, *feed_all)
        grad_normed_two, down_grad = after(grad_normed_two, down_grad)
        down_got = exchange(down_grad.reshape(4, down_grad.shape[0] // 4, -1), "fsdp")
    else:
        down_grad = lax.dot_general(
            hidden, feed_all, contract_rows, preferred_element_type=f32
        ).astype(bf16)
        gateup_grad = lax.dot_general(
            normed_two, grad_gate_up, contract_rows, preferred_element_type=f32
        ).astype(bf16)
    gain_two_term = jnp.sum(grad_normed_two * middle * scale_two, 0)
    scaled_two = grad_normed_two * norm_gain2
    grad_middle = (
        grad_feed.astype(f32)
        + scale_two * scaled_two
        - scale_two
        * scale_two
        * scale_two
        * middle
        * jnp.mean(scaled_two * middle, -1, keepdims=True)
    )
    grad_attention = grad_middle.astype(bf16)
    if direct():
        grad_far = xor(grad_attention, "ctx", 1)
        low_kept, low_sent, high_kept, high_sent = weight_grad(
            normed_two, grad_gate_up, (merged, grad_attention, grad_far)
        )
        wide_kept = low_kept, high_kept
        wide_got = xor(low_sent, "dp", 1), xor(high_sent, "dp", 2)
        grad_merged = merged_grad(grad_attention, grad_far, out)
    else:
        grad_attention = both_pieces(grad_attention)
        out_grad = lax.dot_general(
            merged, grad_attention, contract_rows, preferred_element_type=f32
        ).astype(bf16)
        grad_merged = lax.dot_general(
            grad_attention, out, contract_cols, preferred_element_type=f32
        )
    grad_mixed, conv_term, gain_rows = mixer_backward(
        grad_merged, heads_out, queries, keys, inverse, errors, states,
        projected, conv_mine, head_gain[None], lengths,
    )
    if direct():
        grad_mixed, *wide_got = after(grad_mixed, *wide_got)
        wide_kept, wide_got = replicas_second(wide_kept, wide_got)
        low_kept, low_sent, high_kept, high_sent = weight_grad((normed_one,), grad_mixed)
        mixed_kept = low_kept, high_kept
        mixed_got = xor(low_sent, "dp", 1), xor(high_sent, "dp", 2)
        wide_own, wide_got = rows_sent(wide_kept, wide_got)
        near, far = normed_grad(grad_mixed, mixed)
        grad_normed_one = near + xor(far, "ctx", 1).astype(f32)
        mixed_kept, mixed_got = replicas_second(mixed_kept, mixed_got)
        down_total = down_summed(down_got)
        mixed = summed_rows(*rows_sent(mixed_kept, mixed_got))
        wide = summed_rows(wide_own, wide_got)
        feed_part = both_columns(wide[..., : 2 * ff_width])
        wide = to_all(jnp.concatenate([feed_part, wide[..., 2 * ff_width :]], 2), "dp")
        short, rows, half = wide.shape[2], HD // (4 * n), model_width // 2
        moves = []
        for i in range(4):
            for j in range(n):
                lines = slice(i * short, (i + 1) * short)
                for k in range(2):
                    at = slice(k * ff_width, (k + 1) * ff_width)
                    to = (k * n + j) * ff_width
                    moves.append(((i, j, slice(None), at), 0, (lines, slice(to, to + ff_width))))
                for k in range(2):
                    at = slice(k * rows, (k + 1) * rows), slice(2 * ff_width, None)
                    low = j * 4 * rows + i * rows
                    to = slice(low, low + rows), slice(k * half, (k + 1) * half)
                    moves.append(((i, j) + at, 1, to))
        shapes = [(4 * short, 2 * n * ff_width), (4 * n * rows, model_width)]
        gateup_total, out_total = finish(wide, moves, shapes, "wide_totals")
        both = to_all(both_columns(mixed), "dp")
        moves = []
        for i in range(4):
            for j in range(n):
                for k in range(3 * heads):
                    at = (i, j, slice(None), slice(k * HD, (k + 1) * HD))
                    to = (k * n + j) * HD
                    lines = slice(i * short, (i + 1) * short)
                    moves.append((at, 0, (lines, slice(to, to + HD))))
        (qkv_total,) = finish(both, moves, [(4 * short, 3 * heads_all * HD)], "mixed_totals")
        beta_total = both[..., 3 * heads * HD : 3 * heads * HD + heads].astype(f32)
        beta_total = jnp.transpose(beta_total, (0, 2, 3, 1)).reshape(4 * short, heads_all)
    else:
        mixed_grad = lax.dot_general(
            normed_one, grad_mixed, contract_rows, preferred_element_type=f32
        ).astype(bf16)
        grad_normed_one = own_piece(
            lax.dot_general(grad_mixed, mixed, contract_cols, preferred_element_type=f32)
        )
        (gateup_total,) = sum_columns(gateup_grad, [(2, ff_width)], [2 * ff_width])
        down_total = scattered(placed_at_ctx(down_grad, 0).reshape(-1, model_width))
        view = placed_at_ctx(out_grad.reshape(heads, HD, model_width), 1)
        out_total = scattered(view.reshape(-1, model_width))
        views, widths = [(3, heads, HD), (1, heads, 1)], [3 * heads * HD, heads]
        qkv_total, beta_total = sum_columns(mixed_grad, views, widths)
    scale_one = lax.rsqrt(jnp.mean(tokens_in * tokens_in, -1, keepdims=True) + 1e-06)
    gain_one_term = jnp.sum(grad_normed_one * tokens_in * scale_one, 0)
    scaled_one = grad_normed_one * norm_gain1
    grad_tokens = (
        grad_middle
        + scale_one * scaled_one
        - scale_one
        * scale_one
        * scale_one
        * tokens_in
        * jnp.mean(scaled_one * tokens_in, -1, keepdims=True)
    )
    conv_term = placed_at_ctx(conv_term.reshape(KERNEL, 3, heads, HD), 3)
    small = jnp.concatenate([gain_one_term, gain_two_term, gain_rows[0], conv_term.reshape(-1)], 0)
    cuts = [model_width, 2 * model_width, 2 * model_width + HD]
    gain_one, gain_two, gain_head, conv_total = jnp.split(sum_small(small), cuts)
    return (
        output[None],
        grad_tokens.astype(bf16)[None],
        gain_one,
        qkv_total,
        beta_total,
        conv_total.reshape(conv_weight.shape),
        gain_head,
        out_total,
        gain_two,
        gateup_total,
        down_total,
    )


def solution(mesh):
    placed = (
        P(("dp", "fsdp"), "ctx", None),
        P(("dp", "fsdp")),
        P(("dp", "fsdp"), "ctx", None),
        P(),
        P("fsdp", None),
        P("fsdp", None),
        P(),
        P(),
        P("fsdp", None),
        P(),
        P("fsdp", None),
        P("fsdp", None),
    )
    return jax.shard_map(
        local,
        mesh=mesh,
        in_specs=placed,
        out_specs=(
            P(("dp", "fsdp"), "ctx", None),
            P(("dp", "fsdp"), "ctx", None),
            P(),
            P(("fsdp", "ctx"), None),
            P(("fsdp", "ctx"), None),
            P(),
            P(),
            P(("fsdp", "ctx"), None),
            P(),
            P(("fsdp", "ctx"), None),
            P(("fsdp", "ctx"), None),
        ),
        check_vma=False,
    )
```

```python
import functools
import jax, jax.numpy as jnp
from jax import lax
from jax.experimental import pallas as pl
from jax.experimental.pallas import tpu as pltpu
from jax.sharding import PartitionSpec as P

HD = 128
KERNEL = 4
CHUNK = 128
bf16 = jnp.bfloat16
f32 = jnp.float32

def dot(a, b):
    return jnp.dot(a, b, preferred_element_type=f32)

def dot_nt(a, b):
    return lax.dot_general(a, b, (((1,), (1,)), ((), ())), preferred_element_type=f32)

def dot_tn(a, b):
    return lax.dot_general(a, b, (((0,), (0,)), ((), ())), preferred_element_type=f32)

def halves(a):
    high = a.astype(bf16)
    return high, (a - high.astype(f32)).astype(bf16)

def fine_dot(a, b):
    n = b[0].shape[1]
    left = jnp.concatenate(a, 1)
    row = jnp.concatenate(b, 1)
    both = dot(left, jnp.concatenate([row, row], 0))
    return both[:, :n] + both[:, n:]

def unit_lower_inverses(lowers, size):
    rows = lax.broadcasted_iota(jnp.int32, (size, size), 0)
    cols = lax.broadcasted_iota(jnp.int32, (size, size), 1)
    eye = jnp.where(rows == cols, 1.0, 0.0)
    def joins(b):
        return (rows // (2 * b) == cols // (2 * b)) & ((rows // b) % 2 == 1) & ((cols // b) % 2 == 0)
    mask = joins(1)
    invs = [eye - jnp.where(mask, t, 0.0) for t in lowers]
    b = 2
    while b < size:
        mask = joins(b)
        parts = [halves(jnp.where(mask, t, 0.0)) for t in lowers]
        splits = [halves(t) for t in invs]
        inner = [halves(fine_dot(p, t)) for p, t in zip(parts, splits)]
        invs = [i - fine_dot(t, n) for i, t, n in zip(invs, splits, inner)]
        b *= 2
    return invs

def conv_rows(ref, weight, length):
    total = weight[0:1] * ref[pl.ds(5, length), :]
    for j in range(1, KERNEL):
        total = total + weight[j:j+1] * ref[pl.ds(5 + j, length), :]
    return total


def head_beta(logits, head, valid):
    lane = lax.broadcasted_iota(jnp.int32, logits.shape, 1)
    logit = jnp.sum(jnp.where(lane == head, logits, 0.0), -1, keepdims=True)
    return jnp.where(valid, jax.nn.sigmoid(logit), 0.0)


def mixer_forward_kernel(hb, nv_ref, pq, pk, pv, wq, wk, wv, bl, gain,
                         q_ref, k_ref, t_ref, e_ref, s_ref, o_ref, m_ref, ext):
    length = pq.shape[0]
    valid = lax.broadcasted_iota(jnp.int32, (length, 1), 0) < nv_ref[0]
    rows = lax.broadcasted_iota(jnp.int32, (CHUNK, CHUNK), 0)
    cols = lax.broadcasted_iota(jnp.int32, (CHUNK, CHUNK), 1)
    group = pl.program_id(0)
    acts = []
    for i, (p, w) in enumerate(((pq, wq), (pk, wk), (pv, wv))):
        ext[i, 0:8, :] = jnp.zeros((8, ext.shape[2]), f32)
        ext[i, 8:, :] = jnp.where(valid, p[...], 0.0)
        c = conv_rows(ext.at[i], w, length)
        acts.append(c * jax.nn.sigmoid(c))
    count = length // CHUNK
    spans = [slice(c * CHUNK, (c + 1) * CHUNK) for c in range(count)]
    heads = []
    for h in range(hb):
        lanes = slice(h * HD, (h + 1) * HD)
        a, b, v = (t[:, lanes] for t in acts)
        q = (a * (lax.rsqrt(jnp.sum(a * a, -1, keepdims=True) + 1e-6) * HD ** -0.5)).astype(bf16)
        k = (b * lax.rsqrt(jnp.sum(b * b, -1, keepdims=True) + 1e-6)).astype(bf16)
        beta = head_beta(bl[...], group * hb + h, valid)
        q_ref[:, lanes] = q
        k_ref[:, lanes] = k
        heads.append((q, k, (k.astype(f32) * beta).astype(bf16), (v * beta).astype(bf16)))
    cells = [(h, s) for h in range(hb) for s in spans]
    boths = [dot_nt(jnp.concatenate([heads[h][2][s], heads[h][0][s]], 0), heads[h][1][s]) for h, s in cells]
    invs = unit_lower_inverses([jnp.where(rows > cols, t[:CHUNK], 0.0) for t in boths], CHUNK)
    invs = [t.astype(bf16) for t in invs]
    blends = [dot(t, jnp.concatenate([heads[h][2][s], heads[h][3][s]], 1)) for t, (h, s) in zip(invs, cells)]
    states = [jnp.zeros((HD, HD), f32)] * hb
    for c, s in enumerate(spans):
        for h in range(hb):
            lanes = slice(h * HD, (h + 1) * HD)
            q, k = heads[h][:2]
            cell = h * count + c
            t_ref[h, c] = invs[cell]
            score = jnp.where(rows >= cols, boths[cell][CHUNK:], 0.0).astype(bf16)
            low = states[h].astype(bf16)
            s_ref[h, c] = low
            both = dot(jnp.concatenate([blends[cell][:, :HD].astype(bf16), q[s]], 0), low)
            err = (blends[cell][:, HD:] - both[:CHUNK]).astype(bf16)
            e_ref[s, lanes] = err
            states[h] = states[h] + dot_tn(k[s], err)
            out = both[CHUNK:] + dot(score, err)
            scale = lax.rsqrt(jnp.mean(out * out, -1, keepdims=True) + 1e-05)
            o_ref[s, lanes] = out.astype(bf16)
            m_ref[s, lanes] = (out * scale * gain[...]).astype(bf16)


def heads_per_step(heads):
    return 2 if heads % 2 == 0 else 1


def mixer_forward(projected, conv_w, gain, nv, heads):
    length = projected.shape[0]
    nc = length // CHUNK
    hb = heads_per_step(heads)
    groups = heads // hb
    w = hb * HD
    col = lambda off: (lambda i, *_: (0, i + off * groups))
    tok = pl.BlockSpec((length, w), lambda i, *_: (0, i))
    sq = pl.BlockSpec((hb, nc, HD, HD), lambda i, *_: (i, 0, 0, 0))
    in_specs = [pl.BlockSpec((length, w), col(o)) for o in range(3)]
    in_specs += [pl.BlockSpec((KERNEL, w), col(o)) for o in range(3)]
    in_specs += [pl.BlockSpec((length, HD), lambda i, *_: (0, 3 * heads)), pl.BlockSpec((1, HD), lambda i, *_: (0, 0))]
    flat = jax.ShapeDtypeStruct((length, heads * HD), bf16)
    square = jax.ShapeDtypeStruct((heads, nc, HD, HD), bf16)
    return pl.pallas_call(
        functools.partial(mixer_forward_kernel, hb),
        out_shape=(flat, flat, square, flat, square, flat, flat),
        grid_spec=pltpu.PrefetchScalarGridSpec(
            num_scalar_prefetch=1, grid=(groups,), in_specs=in_specs,
            out_specs=(tok, tok, sq, tok, sq, tok, tok),
            scratch_shapes=[pltpu.VMEM((3, length + 8, w), f32)]),
        name="mixer_forward",
    )(nv, projected, projected, projected, conv_w, conv_w, conv_w, projected, gain)


def mixer_backward_kernel(hb, heads_all, nv_ref, gm, o, q, k, t, e, s_c, bl, pq, pk, pv, wq, wk, wv, gain,
                          gp_ref, conv_ref, hg_ref, ext, gext):
    length = gm.shape[0]
    count = length // CHUNK
    group = pl.program_id(0)
    width = hb * HD
    valid = lax.broadcasted_iota(jnp.int32, (length, 1), 0) < nv_ref[0]
    rows = lax.broadcasted_iota(jnp.int32, (CHUNK, CHUNK), 0)
    cols = lax.broadcasted_iota(jnp.int32, (CHUNK, CHUNK), 1)
    spans = [slice(c * CHUNK, (c + 1) * CHUNK) for c in range(count)]
    logits_at = slice(3 * heads_all * HD, (3 * heads_all + 1) * HD)
    @pl.when(group == 0)
    def _():
        hg_ref[...] = jnp.zeros_like(hg_ref)
        gp_ref[:, logits_at] = jnp.zeros((length, HD), bf16)
    heads = []
    for h in range(hb):
        lanes = slice(h * HD, (h + 1) * HD)
        grad, out = gm[:, lanes].astype(f32), o[:, lanes].astype(f32)
        scale = lax.rsqrt(jnp.mean(out * out, -1, keepdims=True) + 1e-05)
        hg_ref[0:1, :] += jnp.sum(grad * out * scale, 0, keepdims=True)
        scaled = grad * gain[...]
        down = (scale * scaled - scale * scale * scale * out * jnp.mean(scaled * out, -1, keepdims=True)).astype(bf16)
        heads.append((q[:, lanes], k[:, lanes], down, head_beta(bl[...], group * hb + h, valid), e[:, lanes]))
    cells = [(h, c) for h in range(hb) for c in range(count)]
    scores = [jnp.where(rows >= cols, dot_nt(heads[h][0][spans[c]], heads[h][1][spans[c]]), 0.0).astype(bf16) for h, c in cells]
    errs = [dot_tn(m, heads[h][2][spans[c]]).astype(bf16) for m, (h, c) in zip(scores, cells)]
    firsts = [dot_tn(t[h, c], jnp.concatenate([r, heads[h][1][spans[c]]], 1)) for r, (h, c) in zip(errs, cells)]
    adds = [dot_tn(heads[h][0][spans[c]], heads[h][2][spans[c]]) for h, c in cells]
    states = [jnp.zeros((HD, HD), f32)] * hb
    backs, outs, gls = {}, {}, {}
    for c in reversed(range(count)):
        s = spans[c]
        for h in range(hb):
            cell = h * count + c
            low = states[h].astype(bf16)
            outs[h, c] = low
            full = firsts[cell][:, :HD] + dot(firsts[cell][:, HD:].astype(bf16), low)
            beta = heads[h][3][s]
            gls[h, c] = jnp.sum(full * heads[h][4][s].astype(f32), -1, keepdims=True) * (1.0 - beta)
            backs[h, c] = full * beta
            states[h] = states[h] + adds[cell] - dot_tn(heads[h][1][s], backs[h, c].astype(bf16))
    lane = lax.broadcasted_iota(jnp.int32, (length, HD), 1)
    total = jnp.zeros((length, HD), f32)
    grads = ([], [], [])
    for h in range(hb):
        gl = jnp.concatenate([gls[h, c] for c in range(count)], 0)
        total = jnp.where((lane == group * hb + h) & valid, gl, total)
        qh, kh, dh, _, err = heads[h]
        grads[2].append(jnp.concatenate([backs[h, c] for c in range(count)], 0))
        left = [jnp.concatenate([dh[s], (-backs[h, c]).astype(bf16)], 0) for c, s in enumerate(spans)]
        pairs = [dot_nt(p, err[s]) for p, s in zip(left, spans)]
        pairs = [jnp.concatenate([jnp.where(rows >= cols, p[:CHUNK], 0.0), jnp.where(rows > cols, p[CHUNK:], 0.0)], 0).astype(bf16) for p in pairs]
        first = [dot_nt(p, s_c[h, c]) for c, p in enumerate(left)]
        second = [dot(p, kh[s]) for p, s in zip(pairs, spans)]
        third = [dot_nt(err[s], outs[h, c]) for c, s in enumerate(spans)]
        fourth = [dot_tn(p, jnp.concatenate([qh[s], kh[s]], 0)) for p, s in zip(pairs, spans)]
        grads[0].append(jnp.concatenate([a[:CHUNK] + b[:CHUNK] for a, b in zip(first, second)], 0))
        grads[1].append(jnp.concatenate([a[CHUNK:] + b[CHUNK:] + x + y for a, b, x, y in zip(first, second, third, fourth)], 0))
    gp_ref[:, logits_at] = gp_ref[:, logits_at] + total.astype(bf16)
    for i, (p, w) in enumerate(((pq, wq), (pk, wk), (pv, wv))):
        ext[0:8, :] = jnp.zeros((8, width), f32)
        ext[8:, :] = jnp.where(valid, p[...], 0.0)
        pre = conv_rows(ext, w, length)
        sig = jax.nn.sigmoid(pre)
        pieces = []
        for h in range(hb):
            grad = grads[i][h]
            if i < 2:
                raw = (pre * sig)[:, h * HD:(h + 1) * HD]
                scale = lax.rsqrt(jnp.sum(raw * raw, -1, keepdims=True) + 1e-06)
                grad = scale * (grad - scale * scale * raw * jnp.sum(raw * grad, -1, keepdims=True))
                if i == 0:
                    grad = grad * HD ** -0.5
            pieces.append(grad)
        grad = jnp.concatenate(pieces, 1) if hb > 1 else pieces[0]
        grad = grad * sig * (1.0 + pre * (1.0 - sig))
        gext[0:length, :] = grad
        gext[length:, :] = jnp.zeros((8, width), f32)
        at = pl.ds(pl.multiple_of(i * heads_all * HD + group * width, HD), width)
        for j in range(KERNEL):
            conv_ref[j:j + 1, at] = jnp.sum(grad * ext[5 + j:5 + j + length, :], 0, keepdims=True)
        back = w[3:4] * grad
        for j in range(KERNEL - 1):
            back = back + w[j:j + 1] * gext[3 - j:3 - j + length, :]
        gp_ref[:, at] = jnp.where(valid, back, 0.0).astype(bf16)


def mixer_backward(gm, o, q, k, t, e, s_c, projected, conv_w, gain, nv):
    length = gm.shape[0]
    heads, nc = t.shape[:2]
    hb = heads_per_step(heads)
    groups = heads // hb
    w = hb * HD
    tok = pl.BlockSpec((length, w), lambda i, *_: (0, i))
    sq = pl.BlockSpec((hb, nc, HD, HD), lambda i, *_: (i, 0, 0, 0))
    col = lambda off: (lambda i, *_: (0, i + off * groups))
    fixed = lambda shape: pl.BlockSpec(shape, lambda i, *_: (0, 0))
    in_specs = [tok, tok, tok, tok, sq, tok, sq, pl.BlockSpec((length, HD), lambda i, *_: (0, 3 * heads))]
    in_specs += [pl.BlockSpec((length, w), col(n)) for n in range(3)]
    in_specs += [pl.BlockSpec((KERNEL, w), col(n)) for n in range(3)]
    in_specs += [fixed((1, HD))]
    wide = (length, (3 * heads + 1) * HD)
    return pl.pallas_call(
        functools.partial(mixer_backward_kernel, hb, heads),
        out_shape=(
            jax.ShapeDtypeStruct(wide, bf16),
            jax.ShapeDtypeStruct((KERNEL, 3 * heads * HD), f32),
            jax.ShapeDtypeStruct((8, HD), f32),
        ),
        grid_spec=pltpu.PrefetchScalarGridSpec(
            num_scalar_prefetch=1, grid=(groups,), in_specs=in_specs,
            out_specs=(fixed(wide), fixed((KERNEL, 3 * heads * HD)), fixed((8, HD))),
            scratch_shapes=[pltpu.VMEM((length + 8, w), f32), pltpu.VMEM((length + 8, w), f32)]),
        name="mixer_backward",
    )(nv, gm, o, q, k, t, e, s_c, projected, projected, projected, projected, conv_w, conv_w, conv_w, gain)


def xor(value, axis, step):
    return lax.ppermute(value, axis, [(i, i ^ step) for i in range(lax.axis_size(axis))])


def pick(tensor, index, axis=0):
    return lax.dynamic_index_in_dim(tensor, index, axis, keepdims=False)


def added(a, b):
    return (a.astype(f32) + b.astype(f32)).astype(bf16)


def direct():
    return (lax.axis_size("dp"), lax.axis_size("fsdp"), lax.axis_size("ctx")) == (4, 4, 2)


def mixer_columns(weight, heads):
    n = lax.axis_size("ctx")
    view = weight.reshape(weight.shape[0], 3, heads // n, n, HD)
    return pick(view, lax.axis_index("ctx"), 3).reshape(weight.shape[0], -1)


def beta_columns(weight, heads):
    n = lax.axis_size("ctx")
    view = weight.reshape(weight.shape[0], heads // n, n)
    return jnp.pad(pick(view, lax.axis_index("ctx"), 2), ((0, 0), (0, HD - heads // n)))


def feed_columns(weight):
    n = lax.axis_size("ctx")
    view = weight.reshape(weight.shape[0], 2, n, weight.shape[1] // (2 * n))
    return pick(view, lax.axis_index("ctx"), 2).reshape(weight.shape[0], -1)


def after(value, *others):
    return lax.optimization_barrier((value,) + others)


def start_pieces(tags, places, sources, outs, sems, z, d):
    copies = []
    for tag in tags:
        source, at_first, row_step, same, other = tag
        for at, index, row, col in places(tag, z ^ row_step, other if same else d ^ other):
            rows, width = (s.stop - s.start for s in at)
            target = outs[index].at[pl.ds(row, rows), pl.ds(col, width)]
            copy = pltpu.make_async_copy(
                sources[source].at[at_first + at], target, sems.at[len(copies)]
            )
            copy.start()
            copies.append(copy)
    return copies


def positions():
    return jnp.stack([lax.axis_index(a) for a in ("fsdp", "dp", "ctx")]).astype(jnp.int32)


def project_kernel(tags, places, count, where_ref, x_own, x_far, gain, *refs):
    sources = refs[:count]
    normed_ref, out_ref, full_ref, weight, sems, out_sem = refs[count:]
    step, steps = pl.program_id(0), pl.num_programs(0)
    z, d, c = where_ref[0], where_ref[1], where_ref[2]
    kept = pltpu.make_async_copy(weight, full_ref, out_sem)

    @pl.when(step == 0)
    def _():
        for copy in start_pieces(tags, places, sources, (weight,), sems, z, d):
            copy.wait()
        kept.start()

    x = jnp.where(step == c, x_own[...], x_far[...]).astype(f32)
    scale = lax.rsqrt(jnp.mean(x * x, -1, keepdims=True) + 1e-06)
    normed = (x * scale * gain[...]).astype(bf16)
    normed_ref[...] = normed
    out_ref[...] = dot(normed, weight[...])

    @pl.when(step == steps - 1)
    def _():
        kept.wait()


def project(x_own, x_far, gain, pieces, width):
    arrays, tags, places = pieces
    rows, depth = x_own.shape
    half = pl.BlockSpec((rows, depth), lambda i, *_: (0, 0))
    each = lambda w: pl.BlockSpec((rows, w), lambda i, *_: (i, 0))
    anywhere = pl.BlockSpec(memory_space=pl.ANY)
    return pl.pallas_call(
        functools.partial(project_kernel, tags, places, len(arrays)),
        out_shape=(
            jax.ShapeDtypeStruct((2 * rows, depth), bf16),
            jax.ShapeDtypeStruct((2 * rows, width), f32),
            jax.ShapeDtypeStruct((depth, width), bf16),
        ),
        grid_spec=pltpu.PrefetchScalarGridSpec(
            num_scalar_prefetch=1,
            grid=(2,),
            in_specs=[half, half, pl.BlockSpec((1, depth), lambda i, *_: (0, 0))]
            + [anywhere] * len(arrays),
            out_specs=(each(depth), each(width), anywhere),
            scratch_shapes=[
                pltpu.VMEM((depth, width), bf16),
                pltpu.SemaphoreType.DMA((len(tags),)),
                pltpu.SemaphoreType.DMA,
            ],
        ),
        name="projections",
    )(positions(), x_own, x_far, gain, *arrays)


def near_first(i, where):
    return ((where[2] + i) % 2, 0)


def attend_kernel(tags, places, count, where_ref, merged, *refs):
    sources = refs[:count]
    near, far, full_ref, weight, sems, out_sem = refs[count:]
    step, steps = pl.program_id(0), pl.num_programs(0)
    z, d = where_ref[0], where_ref[1]
    kept = pltpu.make_async_copy(weight, full_ref, out_sem)

    @pl.when(step == 0)
    def _():
        for copy in start_pieces(tags, places, sources, (weight,), sems, z, d):
            copy.wait()
        kept.start()

    total = dot(merged[...], weight[...])

    @pl.when(step == 0)
    def _():
        near[...] = total

    @pl.when(step == 1)
    def _():
        far[...] = total.astype(bf16)

    @pl.when(step == steps - 1)
    def _():
        kept.wait()


def near_spec(block, width):
    return pl.BlockSpec((block, width), lambda i, *_: (0, 0))


def far_spec(block, width):
    return pl.BlockSpec((block, width), lambda i, *_: (0, 0))


def attend(merged, pieces, width):
    arrays, tags, places = pieces
    rows, depth = merged.shape
    block = rows // 2
    anywhere = pl.BlockSpec(memory_space=pl.ANY)
    return pl.pallas_call(
        functools.partial(attend_kernel, tags, places, len(arrays)),
        out_shape=(
            jax.ShapeDtypeStruct((rows // 2, width), f32),
            jax.ShapeDtypeStruct((rows // 2, width), bf16),
            jax.ShapeDtypeStruct((depth, width), bf16),
        ),
        grid_spec=pltpu.PrefetchScalarGridSpec(
            num_scalar_prefetch=1,
            grid=(2,),
            in_specs=[pl.BlockSpec((block, depth), near_first)] + [anywhere] * len(arrays),
            out_specs=(near_spec(block, width), far_spec(block, width), anywhere),
            scratch_shapes=[
                pltpu.VMEM((depth, width), bf16),
                pltpu.SemaphoreType.DMA((2 * len(tags),)),
                pltpu.SemaphoreType.DMA,
            ],
        ),
        name="mixer_out",
    )(positions(), merged, *arrays)


def merged_grad_kernel(where_ref, own, far, weight, out):
    grad = jnp.where(pl.program_id(0) == 0, own[...], far[...])
    out[...] = dot_nt(grad, weight[...])


def merged_grad(own, far, weight):
    rows, width = own.shape
    depth = weight.shape[0]
    block = rows
    return pl.pallas_call(
        merged_grad_kernel,
        out_shape=jax.ShapeDtypeStruct((2 * rows, depth), f32),
        grid_spec=pltpu.PrefetchScalarGridSpec(
            num_scalar_prefetch=1,
            grid=(2,),
            in_specs=[
                near_spec(block, width),
                far_spec(block, width),
                pl.BlockSpec((depth, width), lambda i, *_: (0, 0)),
            ],
            out_specs=pl.BlockSpec((block, depth), near_first),
        ),
        name="merged_gradient",
    )(positions(), own, far, weight)


def normed_grad_kernel(where_ref, grad, weight, near, far):
    total = dot_nt(grad[...], weight[...])

    @pl.when(pl.program_id(0) == 0)
    def _():
        near[...] = total

    @pl.when(pl.program_id(0) == 1)
    def _():
        far[...] = total.astype(bf16)


def normed_grad(grad, weight):
    rows, width = grad.shape
    depth = weight.shape[0]
    block = rows // 2
    return pl.pallas_call(
        normed_grad_kernel,
        out_shape=(
            jax.ShapeDtypeStruct((rows // 2, depth), f32),
            jax.ShapeDtypeStruct((rows // 2, depth), bf16),
        ),
        grid_spec=pltpu.PrefetchScalarGridSpec(
            num_scalar_prefetch=1,
            grid=(2,),
            in_specs=[
                pl.BlockSpec((block, width), near_first),
                pl.BlockSpec((depth, width), lambda i, *_: (0, 0)),
            ],
            out_specs=(near_spec(block, depth), far_spec(block, depth)),
        ),
        name="normed_gradient",
    )(positions(), grad, weight)


def keep_and_send(total, where_ref, refs, col):
    low_keep, low_send, high_keep, high_send = refs
    first_low, first_high = where_ref[1] % 2 == 0, where_ref[1] // 2 == 0
    short = total.shape[0] // 32
    block = lambda i: total[i * short : (i + 1) * short]
    for z in range(2):
        for i in range(4):
            a, b = block(8 * z + 2 * i), block(8 * z + 2 * i + 1)
            low_keep[z, i // 2, i % 2, col, :] = jnp.where(first_low, a, b)
            low_send[z, i // 2, i % 2, col, :] = jnp.where(first_low, b, a)
            k = 16 + 8 * z + (i // 2) * 4 + i % 2
            a, b = block(k), block(k + 2)
            high_keep[z, i // 2, i % 2, col, :] = jnp.where(first_high, a, b)
            high_send[z, i // 2, i % 2, col, :] = jnp.where(first_high, b, a)


def weight_grad_kernel(parts, steps, where_ref, *refs):
    lefts, grad = refs[:parts], refs[parts]
    turned = refs[-1]
    step = pl.program_id(0)
    c = where_ref[2]

    @pl.when(step == 0)
    def _():
        at = 0
        for left in lefts:
            rows = left.shape[0]
            turned[:, at : at + rows] = left[...].T
            at += rows

    if len(refs) == parts + 6:
        every = slice(None)
        keep_and_send(dot(turned[...], grad[...]).astype(bf16), where_ref, refs[-5:-1], every)
        return

    merged, own, far = refs[parts + 1 : parts + 4]
    outs = refs[-5:-1]

    @pl.when(step < steps)
    def _():
        keep_and_send(dot(turned[...], grad[...]).astype(bf16), where_ref, outs, slice(None))

    @pl.when(step >= steps)
    def _():
        rows, half = own.shape[0], own.shape[1] // 2
        mine = merged[pl.ds(pl.multiple_of(c * rows, rows), rows), :]
        theirs = merged[pl.ds(pl.multiple_of((1 - c) * rows, rows), rows), :]
        width = outs[0].shape[-1]
        for k in range(2):
            at = pl.ds(pl.multiple_of(k * half + (step - steps) * width, width), width)
            part = (dot_tn(mine, own[:, at]) + dot_tn(theirs, far[:, at])).astype(bf16)
            lines = part.shape[0] // 32
            keep_and_send(part, where_ref, outs, slice(k * lines, (k + 1) * lines))


def weight_grad(lefts, grad, out=()):
    depth = lefts[0].shape[1]
    rows = sum(a.shape[0] for a in lefts)
    block = 256
    steps = pl.cdiv(grad.shape[1], block)
    more = out[1].shape[1] // 2 if out else 0
    shape = jax.ShapeDtypeStruct((2, 2, 2, depth // 32, grad.shape[1] + more), bf16)
    each = pl.BlockSpec((2, 2, 2, depth // 32, block), lambda i, *_: (0, 0, 0, 0, i))
    whole = lambda a: pl.BlockSpec(a.shape, lambda i, *_: (0, 0))
    specs = [whole(a) for a in lefts]
    specs += [pl.BlockSpec((rows, block), lambda i, *_: (0, jnp.minimum(i, steps - 1)))]
    specs += [whole(a) for a in out]
    return pl.pallas_call(
        functools.partial(weight_grad_kernel, len(lefts), steps),
        out_shape=(shape,) * 4,
        grid_spec=pltpu.PrefetchScalarGridSpec(
            num_scalar_prefetch=1,
            grid=(steps + more // block,),
            in_specs=specs,
            out_specs=(each,) * 4,
            scratch_shapes=[pltpu.VMEM((depth, rows), bf16)],
        ),
        name="weight_gradient",
    )(positions(), *lefts, grad, *out)


def down_grad_kernel(hidden, own, far, out, turned):
    rows = own.shape[0]

    @pl.when(pl.program_id(0) == 0)
    def _():
        turned[...] = hidden[...].T

    total = dot(turned[:, :rows], own[...]) + dot(turned[:, rows:], far[...])
    out[...] = total.astype(bf16)


def down_gradient(hidden, own, far):
    rows, width = own.shape
    half = hidden.shape[1]
    block = 256
    return pl.pallas_call(
        down_grad_kernel,
        out_shape=jax.ShapeDtypeStruct((half, width), bf16),
        grid=(width // block,),
        in_specs=[
            pl.BlockSpec((2 * rows, half), lambda i: (0, 0)),
            pl.BlockSpec((rows, block), lambda i: (0, i)),
            pl.BlockSpec((rows, block), lambda i: (0, i)),
        ],
        out_specs=pl.BlockSpec((half, block), lambda i: (0, i)),
        scratch_shapes=[pltpu.VMEM((half, 2 * rows), bf16)],
        name="down_gradient",
    )(hidden, own, far)


def whole_rows(weight):
    return lax.all_gather(weight, "fsdp", axis=0, tiled=True)


def exchange(blocks, axis):
    return lax.all_to_all(blocks, axis, 0, 0, tiled=True)


def to_all(piece, axis):
    return exchange(jnp.broadcast_to(piece, (lax.axis_size(axis),) + piece.shape), axis)


def bounds(total, step):
    return [slice(i, min(i + step, total)) for i in range(0, total, step)]


def feed_kernel(tags, places, count_down, own, where_ref, x_own, x_other, e_own, e_other, *refs):
    count = 1 + max(t[0] for t in tags)
    sources, downs = refs[:count], refs[count : count + count_down]
    hidden_ref, grad_ref, near_out, far_out, near_grad, far_grad = refs[count + count_down : -3]
    gateup, down, sems = refs[-3:]
    step = pl.program_id(0)
    z, d, c = where_ref[0], where_ref[1], where_ref[2]

    @pl.when(step == 0)
    def _():
        copies = start_pieces(tags, places, sources, (gateup,), sems, z, d)
        rows, cols = downs[1].shape[1:]
        for j in range(2):
            for source, at, first in ((downs[0], 2 * c + j, c), (downs[1], j, 1 - c)):
                col = pl.multiple_of(first * cols, HD)
                copy = pltpu.make_async_copy(
                    source.at[at],
                    down.at[pl.ds(j * rows, rows), pl.ds(col, cols)],
                    sems.at[len(copies)],
                )
                copy.start()
                copies.append(copy)
        for copy in copies:
            copy.wait()

    near = step < own
    x = jnp.where(near, x_own[...], x_other[...])
    e = jnp.where(near, e_own[...], e_other[...])
    half = down.shape[0]
    for j in bounds(half, 256):
        up_j = slice(half + j.start, half + j.stop)
        gate = dot(x, gateup[:, j])
        up = dot(x, gateup[:, up_j])
        grad = dot_nt(e, down[j, :])
        sig = jax.nn.sigmoid(gate)
        act = gate * sig
        hidden_ref[:, j] = (act * up).astype(bf16)
        grad_ref[:, j] = (grad * up * sig * (1.0 + gate * (1.0 - sig))).astype(bf16)
        grad_ref[:, up_j] = (grad * act).astype(bf16)
    out = dot(hidden_ref[...], down[...])
    back = dot_nt(grad_ref[...], gateup[...])

    @pl.when(near)
    def _():
        near_out[...] = out
        near_grad[...] = back

    @pl.when(jnp.logical_not(near))
    def _():
        far_out[...] = out.astype(bf16)
        far_grad[...] = back.astype(bf16)


def feed(x_own, x_other, e_own, e_other, wide, down):
    arrays, tags, places = wide
    rows, width = x_own.shape
    others = x_other.shape[0]
    half = 2 * down[1].shape[1]
    block = rows
    own, steps = rows // block, (rows + others) // block
    near = lambda w: pl.BlockSpec((block, w), lambda i, *_: (jnp.minimum(i, own - 1), 0))
    far = lambda w: pl.BlockSpec((block, w), lambda i, *_: (jnp.maximum(i - own, 0), 0))
    each = lambda w: pl.BlockSpec((block, w), lambda i, *_: (i, 0))
    anywhere = pl.BlockSpec(memory_space=pl.ANY)
    return pl.pallas_call(
        functools.partial(feed_kernel, tags, places, len(down), own),
        out_shape=(
            jax.ShapeDtypeStruct((rows + others, half), bf16),
            jax.ShapeDtypeStruct((rows + others, 2 * half), bf16),
            jax.ShapeDtypeStruct((rows, width), f32),
            jax.ShapeDtypeStruct((others, width), bf16),
            jax.ShapeDtypeStruct((rows, width), f32),
            jax.ShapeDtypeStruct((others, width), bf16),
        ),
        grid_spec=pltpu.PrefetchScalarGridSpec(
            num_scalar_prefetch=1,
            grid=(steps,),
            in_specs=[near(width), far(width), near(width), far(width)]
            + [anywhere] * (len(arrays) + len(down)),
            out_specs=(each(half), each(2 * half), near(width), far(width), near(width), far(width)),
            scratch_shapes=[
                pltpu.VMEM((width, 2 * half), bf16),
                pltpu.VMEM((half, width), bf16),
                pltpu.SemaphoreType.DMA((4 + len(tags),)),
            ],
        ),
        name="feed_forward",
    )(positions(), x_own, x_other, e_own, e_other, *arrays, *down)


def pack_kernel(heads, where_ref, qkv, beta, out, gateup, mixed_ref, wide_ref, every):
    rows = qkv.shape[0]
    strips = qkv.shape[1] // (2 * HD)
    mixed = (strips + 1) * HD
    width = gateup.shape[1] // 4
    half = out.shape[1] // 2
    short = out.shape[0]
    for c in range(2):

        @pl.when(where_ref[1] == c)
        def _():
            for i in range(strips):
                at = (2 * i + c) * HD
                mixed_ref[:, i * HD : (i + 1) * HD] = qkv[:, at : at + HD]
            source = lax.broadcasted_iota(jnp.int32, (heads, HD), 0)
            lane = lax.broadcasted_iota(jnp.int32, (heads, HD), 1)
            chosen = (source == 2 * lane + c).astype(f32).astype(bf16)
            every[...] = dot_tn(beta[...], chosen)
            here = pl.ds(pl.multiple_of(where_ref[0] * rows, rows), rows)
            mixed_ref[:, strips * HD : mixed] = every[here, :].astype(bf16)
            for i in range(2):
                at = (2 * i + c) * width
                wide_ref[0, :, i * width : (i + 1) * width] = gateup[:, at : at + width]

    wide_ref[0, :short, 2 * width :] = out[:, :half]
    wide_ref[0, short:, 2 * width :] = out[:, half:]
    for i in range(1, 4):
        wide_ref[i] = wide_ref[0]


def pack(w_qkv, w_beta, w_out, w_gateup):
    rows, short = w_qkv.shape[0] // 4, HD // 4
    heads = w_beta.shape[1]
    here = jnp.stack([lax.axis_index("dp"), lax.axis_index("ctx")]).astype(jnp.int32)
    mixed = w_qkv.shape[1] // 2 + HD
    wide = w_gateup.shape[1] // 2 + w_out.shape[1] // 2
    fixed = lambda *shape: pl.BlockSpec(shape, lambda i, *_: (0,) * len(shape))
    mine = lambda width: pl.BlockSpec((rows, width), lambda i, at: (at[0], 0))
    shapes = ((rows, mixed), (4, rows, wide))
    return pl.pallas_call(
        functools.partial(pack_kernel, heads),
        out_shape=tuple(jax.ShapeDtypeStruct(s, bf16) for s in shapes),
        grid_spec=pltpu.PrefetchScalarGridSpec(
            num_scalar_prefetch=1,
            grid=(1,),
            in_specs=[
                mine(w_qkv.shape[1]),
                pl.BlockSpec(w_beta.shape[::-1], lambda i, *_: (0, 0)),
                pl.BlockSpec((short, w_out.shape[1]), lambda i, at: (at[1] * 4 + at[0], 0)),
                mine(w_gateup.shape[1]),
            ],
            out_specs=tuple(fixed(*s) for s in shapes),
            scratch_shapes=[pltpu.VMEM((w_beta.shape[0], HD), f32)],
        ),
        name="weight_pieces",
    )(here, w_qkv, w_beta.T, w_out, w_gateup)


def gather_direct(mixed_piece, wide_piece, down_shard):
    z, c = lax.axis_index("fsdp"), lax.axis_index("ctx")
    own = [mixed_piece] + [xor(mixed_piece, "dp", k) for k in (1, 2, 3)]
    rows = [xor(mixed_piece, "fsdp", k) for k in (1, 2, 3)]
    wide_own, *own[1:] = after(wide_piece[0], *own[1:])
    wide_own = [wide_own] + [xor(wide_own, "dp", k) for k in (1, 2, 3)]
    wide_piece, *rows = after(wide_piece, *rows)
    wide_rows = exchange(wide_piece, "fsdp")
    rows, *wide_own[1:] = after(jnp.stack(rows), *wide_own[1:])
    rest = [rows] + [xor(rows, "dp", k) for k in (1, 2, 3)]
    half = down_shard.shape[1] // 2
    mine = lax.dynamic_slice_in_dim(down_shard, c * half, half, 1)
    tags = [(k, (), 0, False, k) for k in range(4)]
    tags += [(4 + i, (k - 1,), k, False, i) for i in range(4) for k in (1, 2, 3)]
    return own + rest, tags, wide_own, wide_rows, mine


def spread_first(own, wide_rows, mine):
    z = lax.axis_index("fsdp")
    half = wide_rows.shape[2] // 2
    low = jnp.stack([pick(wide_rows, z ^ k)[:, :half] for k in (1, 2, 3)])
    high = jnp.stack([pick(wide_rows, z ^ k)[:, half:] for k in (1, 2, 3)])
    low, high = [low, xor(low, "dp", 1)], [high, xor(high, "dp", 2)]
    mine, wide_rows = after(mine, wide_rows)
    return own, low, high, to_all(mine, "fsdp")


def spread_second(full, own, low, high):
    full, low[1], high[1] = after(full, low[1], high[1])
    low = low + [xor(low[0], "dp", 2), xor(low[1], "dp", 2)]
    high = [high[0], xor(high[0], "dp", 1), high[1], xor(high[1], "dp", 1)]
    tags = [(k, (), 0, False, k) for k in range(4)]
    tags += [(4 + i, (k - 1,), k, False, i) for i in range(4) for k in (1, 2, 3)]
    tags += [(8 + i, (k - 1,), k, False, i) for i in range(4) for k in (1, 2, 3)]
    return full, own + low + high, tags


def gather_weights(w_qkv, w_beta, w_out, w_gateup, w_down, heads):
    n, c = lax.axis_size("ctx"), lax.axis_index("ctx")
    if not direct():
        mixed = jnp.concatenate([mixer_columns(w_qkv, heads), beta_columns(w_beta, heads)], 1)
        out = whole_rows(w_out).reshape(heads // n, n, HD, -1)
        down = whole_rows(w_down)
        return (
            whole_rows(mixed),
            whole_rows(feed_columns(w_gateup)),
            pick(out, c, 1).reshape(-1, w_out.shape[1]),
            pick(down.reshape(n, -1, down.shape[1]), c),
        )
    rows, short = w_qkv.shape[0] // 4, HD // 4
    mixed_piece, wide_piece = pack(w_qkv, w_beta, w_out, w_gateup)
    mixed, width, half = mixed_piece.shape[1], w_gateup.shape[1] // 2, w_out.shape[1] // 2
    mixed_all, mixed_tags, own, wide_rows, mine = gather_direct(mixed_piece, wide_piece, w_down)
    cut = (width + half) // 2

    def mixed_places(tag, z, d):
        row = pl.multiple_of(z * (4 * rows) + d * rows, rows)
        return [((slice(0, rows), slice(0, mixed)), 0, row, 0)]

    def out_places(tag, z, d):
        row = pl.multiple_of(z * HD + d * short, short)
        first = width if tag[0] < 4 else width - cut
        at = slice(first, first + half)
        return [
            ((slice(0, short), at), 0, row, 0),
            ((slice(short, 2 * short), at), 0, row, half),
        ]

    def feed_places(tag, z, d):
        row = pl.multiple_of(z * (4 * rows) + d * rows, rows)
        if tag[0] < 4:
            at, col = slice(0, width), 0
        elif tag[0] < 8:
            at, col = slice(0, cut), 0
        else:
            at, col = slice(0, width - cut), cut
        return [((slice(0, rows), at), 0, row, col)]

    spread = spread_first(own, wide_rows, mine)

    def further(full):
        full, wide_all, wide_tags = spread_second(full, *spread[:3])
        out_tags = [t for t in wide_tags if not 4 <= t[0] < 8]
        wide = wide_all, wide_tags, feed_places
        return full, wide, (wide_all, out_tags, out_places), spread[3]

    return (mixed_all, mixed_tags, mixed_places), further


def feed_both(normed, grad_feed, gateup, down):
    if direct():
        normed_far, grad_far = xor(normed, "ctx", 1), xor(grad_feed, "ctx", 1)
        theirs = pick(down.reshape((2, 2) + down.shape[1:]), 1 - lax.axis_index("ctx"))
        down = [down, xor(theirs, "ctx", 1)]
        hidden, grad, out, out_far, back, back_far = feed(
            normed, normed_far, grad_feed, grad_far, gateup, down
        )
        out = out + xor(out_far, "ctx", 1).astype(f32)
        back = back + xor(back_far, "ctx", 1).astype(f32)
        return (normed, normed_far), (grad_feed, grad_far), hidden, grad, out, back
    normed, grad_feed = both_pieces(normed), both_pieces(grad_feed)
    gate_up = jnp.dot(normed, gateup, preferred_element_type=f32)
    ff_width = gate_up.shape[1] // 2
    gate_part = gate_up[:, :ff_width]
    up_part = gate_up[:, ff_width:]
    gate_sig = jax.nn.sigmoid(gate_part)
    hidden = (gate_part * gate_sig * up_part).astype(bf16)
    contract_cols = (((1,), (1,)), ((), ()))
    grad_hidden = lax.dot_general(grad_feed, down, contract_cols, preferred_element_type=f32)
    grad_gate = grad_hidden * up_part * gate_sig * (1.0 + gate_part * (1.0 - gate_sig))
    grad = jnp.concatenate([grad_gate, grad_hidden * gate_part * gate_sig], 1).astype(bf16)
    out = own_piece(jnp.dot(hidden, down, preferred_element_type=f32))
    back = own_piece(lax.dot_general(grad, gateup, contract_cols, preferred_element_type=f32))
    return normed, grad_feed, hidden, grad, out, back


def both_pieces(mine):
    n = lax.axis_size("ctx")
    if n != 2:
        return lax.all_gather(mine, "ctx", axis=0, tiled=True)
    other = xor(mine, "ctx", 1)
    first = lax.axis_index("ctx") == 0
    return jnp.concatenate([jnp.where(first, mine, other), jnp.where(first, other, mine)], 0)


def own_piece(partial):
    n = lax.axis_size("ctx")
    rows = partial.shape[0] // n
    if n != 2:
        return lax.psum_scatter(
            partial.astype(bf16), "ctx", scatter_dimension=0, tiled=True
        ).astype(f32)
    here = lax.axis_index("ctx")
    theirs = lax.dynamic_slice_in_dim(partial, (1 - here) * rows, rows, 0).astype(bf16)
    mine = lax.dynamic_slice_in_dim(partial, here * rows, rows, 0)
    return mine.astype(f32) + xor(theirs, "ctx", 1).astype(f32)


def replicas_first(part):
    d = lax.axis_index("dp")
    high, low = d // 2, d % 2
    a, b = part[:2], part[2:]
    got = xor(pick(a, 1 - low, 3), "dp", 1), xor(pick(b, 1 - high, 2), "dp", 2)
    return (pick(a, low, 3), pick(b, high, 2)), got


def replicas_second(kept, got):
    d = lax.axis_index("dp")
    high, low = d // 2, d % 2
    a, b = added(kept[0], got[0]), added(kept[1], got[1])
    sent = pick(a, 1 - high, 2), pick(b, 1 - low, 2)
    return (pick(a, high, 2), pick(b, low, 2)), sent


def over_replicas(kept, got):
    return jnp.concatenate([added(kept[0], got[0]), added(kept[1], got[1])], 0)


def summed_rows(own, got):
    total = own.astype(f32)
    for part in got:
        total = total + part.astype(f32)
    return total.astype(bf16)


def both_columns(part):
    c = lax.axis_index("ctx")
    other = xor(pick(part, 1 - c), "ctx", 1)
    mine = pick(part, c)
    first = c == 0
    return jnp.stack([jnp.where(first, mine, other), jnp.where(first, other, mine)])


def finish_kernel(moves, count, where_ref, *refs):
    sources, outs = refs[:count], refs[count:]
    d = where_ref[1]
    for source, at, index, to in moves:
        if len(to) == 3:
            if isinstance(to[0], int):
                to = (pl.ds(pl.multiple_of((d ^ to[0]) * to[1], to[1]), to[1]), to[2])
            else:
                to = (to[0], pl.ds(pl.multiple_of((d ^ to[1]) * to[2], HD), to[2]))
        outs[index][to] = sources[source][at].astype(f32)


def finish(sources, moves, shapes, name):
    whole = lambda shape: pl.BlockSpec(shape, lambda i, *_: (0,) * len(shape))
    return pl.pallas_call(
        functools.partial(finish_kernel, moves, len(sources)),
        out_shape=tuple(jax.ShapeDtypeStruct(s, f32) for s in shapes),
        grid_spec=pltpu.PrefetchScalarGridSpec(
            num_scalar_prefetch=1,
            grid=(1,),
            in_specs=[whole(s.shape) for s in sources],
            out_specs=tuple(whole(s) for s in shapes),
        ),
        name=name,
    )(positions(), *sources)


def blocks_of(grad, n, z):
    return grad.reshape(z, n, 2, 2, grad.shape[0] // (4 * z * n), grad.shape[1])


def scattered(full):
    share = lax.psum_scatter(full.astype(bf16), ("fsdp", "ctx"), scatter_dimension=0, tiled=True)
    return lax.psum(share, "dp").astype(f32)


def placed_at_ctx(part, axis):
    n = lax.axis_size("ctx")
    shape = [1] * (part.ndim + 1)
    shape[axis] = n
    here = (jnp.arange(n) == lax.axis_index("ctx")).reshape(shape)
    return jnp.where(here, jnp.expand_dims(part, axis), 0)


def sum_columns(grad, views, widths):
    outs, start = [], 0
    for shape, size in zip(views, widths):
        part = grad[:, start : start + size].reshape((grad.shape[0],) + shape)
        full = placed_at_ctx(part, part.ndim - 1)
        outs.append(scattered(full.reshape(grad.shape[0], -1)))
        start += size
    return outs


def added_up(parts):
    total = parts[0].astype(f32)
    for i in range(1, parts.shape[0]):
        total = total + parts[i].astype(f32)
    return total.astype(bf16)


def quarter(part, k):
    cols = part.shape[1] // 4
    return lax.dynamic_slice_in_dim(part, (lax.axis_index("dp") ^ k) * cols, cols, 1)


def down_to_owners(part):
    pairs = [(z * 2 + c, (2 * c + z // 2) * 2 + z % 2) for z in range(4) for c in range(2)]
    return lax.ppermute(part, ("fsdp", "ctx"), pairs)


def sum_over(vector, axis):
    got = [xor(vector, axis, k) for k in (1, 2, 3)]
    return (vector + got[0]) + (got[1] + got[2])


def local(
    inputs,
    lengths,
    cotangent,
    norm_gain1,
    w_qkv,
    w_beta,
    conv_weight,
    head_gain,
    w_out,
    norm_gain2,
    w_gateup,
    w_down,
):
    n = lax.axis_size("ctx")
    heads_all = w_beta.shape[1]
    heads = heads_all // n
    tokens_in = inputs[0].astype(f32)
    piece_len, model_width = tokens_in.shape
    length = piece_len * n
    conv_mine = mixer_columns(conv_weight, heads_all)
    positions_here = jnp.arange(length, dtype=jnp.int32)
    start = lax.axis_index("ctx") * piece_len
    valid = ((start + positions_here[:piece_len]) < lengths[0]).astype(f32)[:, None]
    grad_feed = (cotangent[0].astype(f32) * valid).astype(bf16)
    if direct():
        pieces, further = gather_weights(w_qkv, w_beta, w_out, w_gateup, w_down, heads_all)
        far_rows = xor(inputs[0], "ctx", 1)
        normed_one, projected, mixed = project(
            inputs[0], far_rows, norm_gain1[None], pieces, (3 * heads + 1) * HD
        )
        projected, gateup, out, down = further(projected)
    else:
        mixed, gateup, out, down = gather_weights(
            w_qkv, w_beta, w_out, w_gateup, w_down, heads_all
        )
        tokens_all = both_pieces(inputs[0]).astype(f32)
        scale_all = lax.rsqrt(jnp.mean(tokens_all * tokens_all, -1, keepdims=True) + 1e-06)
        normed_one = (tokens_all * scale_all * norm_gain1).astype(bf16)
        projected = jnp.dot(normed_one, mixed, preferred_element_type=f32)
    queries, keys, inverse, errors, states, heads_out, merged = mixer_forward(
        projected, conv_mine, head_gain[None], lengths, heads
    )
    if direct():
        near, far, out = attend(merged, out, model_width)
        attention = near + xor(far, "ctx", 1).astype(f32)
    else:
        attention = own_piece(jnp.dot(merged, out, preferred_element_type=f32))
    middle = tokens_in + attention
    scale_two = lax.rsqrt(jnp.mean(middle * middle, -1, keepdims=True) + 1e-06)
    normed_two = (middle * scale_two * norm_gain2).astype(bf16)
    normed_two, feed_all, hidden, grad_gate_up, feed_out, grad_normed_two = feed_both(
        normed_two, grad_feed, gateup, down
    )
    output = (middle + feed_out).astype(bf16)
    contract_cols = (((1,), (1,)), ((), ()))
    contract_rows = (((0,), (0,)), ((), ()))
    ff_width = hidden.shape[1]
    if direct():
        down_grad = down_gradient(hidden, *feed_all)
        grad_normed_two, down_grad = after(grad_normed_two, down_grad)
        down_got = exchange(down_grad.reshape(4, down_grad.shape[0] // 4, -1), "fsdp")
    else:
        down_grad = lax.dot_general(
            hidden, feed_all, contract_rows, preferred_element_type=f32
        ).astype(bf16)
        gateup_grad = lax.dot_general(
            normed_two, grad_gate_up, contract_rows, preferred_element_type=f32
        ).astype(bf16)
    gain_two_term = jnp.sum(grad_normed_two * middle * scale_two, 0)
    scaled_two = grad_normed_two * norm_gain2
    grad_middle = (
        grad_feed.astype(f32)
        + scale_two * scaled_two
        - scale_two
        * scale_two
        * scale_two
        * middle
        * jnp.mean(scaled_two * middle, -1, keepdims=True)
    )
    grad_attention = grad_middle.astype(bf16)
    if direct():
        grad_far = xor(grad_attention, "ctx", 1)
        low_kept, low_sent, high_kept, high_sent = weight_grad(
            normed_two, grad_gate_up, (merged, grad_attention, grad_far)
        )
        wide_kept = low_kept, high_kept
        wide_got = xor(low_sent, "dp", 1), xor(high_sent, "dp", 2)
        grad_merged = merged_grad(grad_attention, grad_far, out)
    else:
        grad_attention = both_pieces(grad_attention)
        out_grad = lax.dot_general(
            merged, grad_attention, contract_rows, preferred_element_type=f32
        ).astype(bf16)
        grad_merged = lax.dot_general(
            grad_attention, out, contract_cols, preferred_element_type=f32
        )
    grad_mixed, conv_term, gain_rows = mixer_backward(
        grad_merged, heads_out, queries, keys, inverse, errors, states,
        projected, conv_mine, head_gain[None], lengths,
    )
    if direct():
        grad_mixed, *wide_got = after(grad_mixed, *wide_got)
        wide_kept, wide_sent = replicas_second(wide_kept, wide_got)
        grad_mixed, *wide_sent = after(grad_mixed, *wide_sent)
        wide_got = xor(wide_sent[0], "dp", 2), xor(wide_sent[1], "dp", 1)
        low_kept, low_sent, high_kept, high_sent = weight_grad((normed_one,), grad_mixed)
        mixed_kept = low_kept, high_kept
        mixed_got = xor(low_sent, "dp", 1), xor(high_sent, "dp", 2)
        low_sent, *wide_got = after(low_sent, *wide_got)
        wide = over_replicas(wide_kept, wide_got)
        grad_mixed, down_got, wide = after(grad_mixed, down_got, wide)
        wide = exchange(wide, "fsdp")
        near, far = normed_grad(grad_mixed, mixed)
        down_part = added_up(down_got)
        near, *mixed_got = after(near, *mixed_got)
        grad_normed_one = near + xor(far, "ctx", 1).astype(f32)
        mixed_kept, mixed_sent = replicas_second(mixed_kept, mixed_got)
        mixed_got = xor(mixed_sent[0], "dp", 2), xor(mixed_sent[1], "dp", 1)
        down_got = [xor(quarter(down_part, k), "dp", k) for k in (1, 2, 3)]
    else:
        mixed_grad = lax.dot_general(
            normed_one, grad_mixed, contract_rows, preferred_element_type=f32
        ).astype(bf16)
        grad_normed_one = own_piece(
            lax.dot_general(grad_mixed, mixed, contract_cols, preferred_element_type=f32)
        )
        (gateup_total,) = sum_columns(gateup_grad, [(2, ff_width)], [2 * ff_width])
        down_total = scattered(placed_at_ctx(down_grad, 0).reshape(-1, model_width))
        view = placed_at_ctx(out_grad.reshape(heads, HD, model_width), 1)
        out_total = scattered(view.reshape(-1, model_width))
        views, widths = [(3, heads, HD), (1, heads, 1)], [3 * heads * HD, heads]
        qkv_total, beta_total = sum_columns(mixed_grad, views, widths)
    scale_one = lax.rsqrt(jnp.mean(tokens_in * tokens_in, -1, keepdims=True) + 1e-06)
    gain_one_term = jnp.sum(grad_normed_one * tokens_in * scale_one, 0)
    scaled_one = grad_normed_one * norm_gain1
    grad_tokens = (
        grad_middle
        + scale_one * scaled_one
        - scale_one
        * scale_one
        * scale_one
        * tokens_in
        * jnp.mean(scaled_one * tokens_in, -1, keepdims=True)
    ).astype(bf16)
    conv_term = placed_at_ctx(conv_term.reshape(KERNEL, 3, heads, HD), 3)
    small = jnp.concatenate([gain_one_term, gain_two_term, gain_rows[0], conv_term.reshape(-1)], 0)
    cuts = [model_width, 2 * model_width, 2 * model_width + HD]
    if direct():
        small = small + xor(small, "ctx", 1)
        small, wide, *got = after(small, wide, *mixed_got, *down_got)
        mixed_got, down_got = got[:2], got[2:]
        mixed_part = over_replicas(mixed_kept, mixed_got)
        z = lax.axis_index("fsdp")
        mixed_sent = [pick(mixed_part, z ^ k) for k in (1, 2, 3)]
        small, wide, *mixed_sent = after(small, wide, *mixed_sent)
        mixed_got = [xor(s, "fsdp", k + 1) for k, s in enumerate(mixed_sent)]
        down_mine = down_to_owners(summed_rows(quarter(down_part, 0), down_got))
        wide = added_up(wide)
        feed_part = both_columns(wide[..., : 2 * ff_width])
        lines, cols = wide.shape[1], down_mine.shape[1]
        count = down_mine.shape[0] // lines
        each = pl.cdiv(count, n)
        down_part = jnp.pad(down_mine, ((0, (n * each - count) * lines), (0, 0)))
        down_part = jnp.transpose(down_part.reshape(n, each, lines, cols), (0, 2, 1, 3))
        down_part = down_part.reshape(n, lines, each * cols)
        wide = jnp.concatenate([feed_part, wide[..., 2 * ff_width :], down_part], 2)
        small, wide = after(small, wide)
        small = sum_over(small, "dp")
        wide = to_all(wide, "dp")
        mixed_mine = pick(mixed_part, z)
        ready = after(mixed_mine, small, grad_tokens, *mixed_got)
        mixed_mine, small, grad_tokens = ready[:3]
        mixed_got = ready[3:]
        both = both_columns(summed_rows(mixed_mine, mixed_got))
        both = [both] + [xor(both, "dp", k) for k in (1, 2, 3)]
        small_total = sum_over(small, "fsdp")
        short, rows, half = wide.shape[2], HD // (4 * n), model_width // 2
        moves = []
        for i in range(4):
            for j in range(n):
                lines = slice(i * short, (i + 1) * short)
                for k in range(2):
                    at = slice(k * ff_width, (k + 1) * ff_width)
                    to = (k * n + j) * ff_width
                    moves.append((0, (i, j, slice(None), at), 0, (lines, slice(to, to + ff_width))))
                for k in range(2):
                    at = slice(2 * ff_width, 2 * ff_width + half)
                    at = slice(k * rows, (k + 1) * rows), at
                    low = j * 4 * rows + i * rows
                    to = slice(low, low + rows), slice(k * half, (k + 1) * half)
                    moves.append((0, (i, j) + at, 1, to))
            first = 2 * ff_width + half
            for m in range(count):
                at = slice(first + (m % each) * cols, first + (m % each + 1) * cols)
                to = slice(m * short, (m + 1) * short), slice(i * cols, (i + 1) * cols)
                moves.append((0, (i, m // each, slice(None), at), 2, to))
        shapes = [(4 * short, 2 * n * ff_width), (4 * n * rows, model_width)]
        shapes += [(down_mine.shape[0], 4 * cols)]
        gateup_total, out_total, down_total = finish([wide], moves, shapes, "wide_totals")
        ready = after(both[0], *both[1:], gateup_total, out_total, down_total)
        both, (gateup_total, out_total, down_total) = list(ready[:4]), ready[4:]
        moves = []
        for i in range(4):
            for j in range(n):
                for k in range(3 * heads):
                    at = (j, slice(None), slice(k * HD, (k + 1) * HD))
                    to = (k * n + j) * HD
                    moves.append((i, at, 0, (i, short, slice(to, to + HD))))
                at = (j, slice(None), slice(3 * heads * HD, None))
                moves.append((i, at, 1, (i, short, slice(j * HD, (j + 1) * HD))))
        shapes = [(4 * short, 3 * heads_all * HD), (4 * short, n * HD)]
        qkv_total, beta_total = finish(both, moves, shapes, "mixed_totals")
        beta_total = beta_total.reshape(4 * short, n, HD)[:, :, :heads]
        beta_total = jnp.transpose(beta_total, (0, 2, 1)).reshape(4 * short, heads_all)
    else:
        small_total = lax.psum(small, ("dp", "fsdp", "ctx"))
    gain_one, gain_two, gain_head, conv_total = jnp.split(small_total, cuts)
    return (
        output[None],
        grad_tokens[None],
        gain_one,
        qkv_total,
        beta_total,
        conv_total.reshape(conv_weight.shape),
        gain_head,
        out_total,
        gain_two,
        gateup_total,
        down_total,
    )


def solution(mesh):
    placed = (
        P(("dp", "fsdp"), "ctx", None),
        P(("dp", "fsdp")),
        P(("dp", "fsdp"), "ctx", None),
        P(),
        P("fsdp", None),
        P("fsdp", None),
        P(),
        P(),
        P("fsdp", None),
        P(),
        P("fsdp", None),
        P("fsdp", None),
    )
    return jax.shard_map(
        local,
        mesh=mesh,
        in_specs=placed,
        out_specs=(
            P(("dp", "fsdp"), "ctx", None),
            P(("dp", "fsdp"), "ctx", None),
            P(),
            P(("fsdp", "ctx"), None),
            P(("fsdp", "ctx"), None),
            P(),
            P(),
            P(("fsdp", "ctx"), None),
            P(),
            P(("fsdp", "ctx"), None),
            P(("fsdp", "ctx"), None),
        ),
        check_vma=False,
    )
```

```python
import functools
import jax, jax.numpy as jnp
from jax import lax
from jax.experimental import pallas as pl
from jax.experimental.pallas import tpu as pltpu
from jax.sharding import PartitionSpec as P

HD = 128
KERNEL = 4
CHUNK = 128
bf16 = jnp.bfloat16
f32 = jnp.float32

def dot(a, b):
    return jnp.dot(a, b, preferred_element_type=f32)

def dot_nt(a, b):
    return lax.dot_general(a, b, (((1,), (1,)), ((), ())), preferred_element_type=f32)

def dot_tn(a, b):
    return lax.dot_general(a, b, (((0,), (0,)), ((), ())), preferred_element_type=f32)

def halves(a):
    high = a.astype(bf16)
    return high, (a - high.astype(f32)).astype(bf16)

def fine_dot(a, b):
    n = b[0].shape[1]
    left = jnp.concatenate(a, 1)
    row = jnp.concatenate(b, 1)
    both = dot(left, jnp.concatenate([row, row], 0))
    return both[:, :n] + both[:, n:]

def unit_lower_inverses(lowers, size):
    rows = lax.broadcasted_iota(jnp.int32, (size, size), 0)
    cols = lax.broadcasted_iota(jnp.int32, (size, size), 1)
    eye = jnp.where(rows == cols, 1.0, 0.0)
    def joins(b):
        return (rows // (2 * b) == cols // (2 * b)) & ((rows // b) % 2 == 1) & ((cols // b) % 2 == 0)
    mask = joins(1)
    invs = [eye - jnp.where(mask, t, 0.0) for t in lowers]
    b = 2
    while b < size:
        mask = joins(b)
        parts = [halves(jnp.where(mask, t, 0.0)) for t in lowers]
        splits = [halves(t) for t in invs]
        inner = [halves(fine_dot(p, t)) for p, t in zip(parts, splits)]
        invs = [i - fine_dot(t, n) for i, t, n in zip(invs, splits, inner)]
        b *= 2
    return invs

def conv_rows(ref, weight, length):
    total = weight[0:1] * ref[pl.ds(5, length), :]
    for j in range(1, KERNEL):
        total = total + weight[j:j+1] * ref[pl.ds(5 + j, length), :]
    return total


def head_beta(logits, head, valid):
    lane = lax.broadcasted_iota(jnp.int32, logits.shape, 1)
    logit = jnp.sum(jnp.where(lane == head, logits, 0.0), -1, keepdims=True)
    return jnp.where(valid, jax.nn.sigmoid(logit), 0.0)


def mixer_forward_kernel(hb, nv_ref, pq, pk, pv, wq, wk, wv, bl, gain,
                         q_ref, k_ref, t_ref, e_ref, s_ref, o_ref, m_ref, ext):
    length = pq.shape[0]
    valid = lax.broadcasted_iota(jnp.int32, (length, 1), 0) < nv_ref[0]
    rows = lax.broadcasted_iota(jnp.int32, (CHUNK, CHUNK), 0)
    cols = lax.broadcasted_iota(jnp.int32, (CHUNK, CHUNK), 1)
    group = pl.program_id(0)
    acts = []
    for i, (p, w) in enumerate(((pq, wq), (pk, wk), (pv, wv))):
        ext[i, 0:8, :] = jnp.zeros((8, ext.shape[2]), f32)
        ext[i, 8:, :] = jnp.where(valid, p[...], 0.0)
        c = conv_rows(ext.at[i], w, length)
        acts.append(c * jax.nn.sigmoid(c))
    count = length // CHUNK
    spans = [slice(c * CHUNK, (c + 1) * CHUNK) for c in range(count)]
    heads = []
    for h in range(hb):
        lanes = slice(h * HD, (h + 1) * HD)
        a, b, v = (t[:, lanes] for t in acts)
        q = (a * (lax.rsqrt(jnp.sum(a * a, -1, keepdims=True) + 1e-6) * HD ** -0.5)).astype(bf16)
        k = (b * lax.rsqrt(jnp.sum(b * b, -1, keepdims=True) + 1e-6)).astype(bf16)
        beta = head_beta(bl[...], group * hb + h, valid)
        q_ref[:, lanes] = q
        k_ref[:, lanes] = k
        heads.append((q, k, (k.astype(f32) * beta).astype(bf16), (v * beta).astype(bf16)))
    cells = [(h, s) for h in range(hb) for s in spans]
    boths = [dot_nt(jnp.concatenate([heads[h][2][s], heads[h][0][s]], 0), heads[h][1][s]) for h, s in cells]
    invs = unit_lower_inverses([jnp.where(rows > cols, t[:CHUNK], 0.0) for t in boths], CHUNK)
    invs = [t.astype(bf16) for t in invs]
    blends = [dot(t, jnp.concatenate([heads[h][2][s], heads[h][3][s]], 1)) for t, (h, s) in zip(invs, cells)]
    states = [jnp.zeros((HD, HD), f32)] * hb
    for c, s in enumerate(spans):
        for h in range(hb):
            lanes = slice(h * HD, (h + 1) * HD)
            q, k = heads[h][:2]
            cell = h * count + c
            t_ref[h, c] = invs[cell]
            score = jnp.where(rows >= cols, boths[cell][CHUNK:], 0.0).astype(bf16)
            low = states[h].astype(bf16)
            s_ref[h, c] = low
            both = dot(jnp.concatenate([blends[cell][:, :HD].astype(bf16), q[s]], 0), low)
            err = (blends[cell][:, HD:] - both[:CHUNK]).astype(bf16)
            e_ref[s, lanes] = err
            states[h] = states[h] + dot_tn(k[s], err)
            out = both[CHUNK:] + dot(score, err)
            scale = lax.rsqrt(jnp.mean(out * out, -1, keepdims=True) + 1e-05)
            o_ref[s, lanes] = out.astype(bf16)
            m_ref[s, lanes] = (out * scale * gain[...]).astype(bf16)


def mixer_forward(projected, conv_w, gain, nv, heads):
    length = projected.shape[0]
    nc = length // CHUNK
    hb = 1
    groups = heads // hb
    w = hb * HD
    col = lambda off: (lambda i, *_: (0, i + off * groups))
    tok = pl.BlockSpec((length, w), lambda i, *_: (0, i))
    sq = pl.BlockSpec((hb, nc, HD, HD), lambda i, *_: (i, 0, 0, 0))
    in_specs = [pl.BlockSpec((length, w), col(o)) for o in range(3)]
    in_specs += [pl.BlockSpec((KERNEL, w), col(o)) for o in range(3)]
    in_specs += [pl.BlockSpec((length, HD), lambda i, *_: (0, 3 * heads)), pl.BlockSpec((1, HD), lambda i, *_: (0, 0))]
    flat = jax.ShapeDtypeStruct((length, heads * HD), bf16)
    square = jax.ShapeDtypeStruct((heads, nc, HD, HD), bf16)
    return pl.pallas_call(
        functools.partial(mixer_forward_kernel, hb),
        out_shape=(flat, flat, square, flat, square, flat, flat),
        grid_spec=pltpu.PrefetchScalarGridSpec(
            num_scalar_prefetch=1, grid=(groups,), in_specs=in_specs,
            out_specs=(tok, tok, sq, tok, sq, tok, tok),
            scratch_shapes=[pltpu.VMEM((3, length + 8, w), f32)]),
        name="mixer_forward",
    )(nv, projected, projected, projected, conv_w, conv_w, conv_w, projected, gain)


def mixer_backward_kernel(hb, heads_all, nv_ref, gm, o, q, k, t, e, s_c, bl, pq, pk, pv, wq, wk, wv, gain,
                          gp_ref, conv_ref, hg_ref, ext, gext):
    length = gm.shape[0]
    count = length // CHUNK
    group = pl.program_id(0)
    width = hb * HD
    valid = lax.broadcasted_iota(jnp.int32, (length, 1), 0) < nv_ref[0]
    rows = lax.broadcasted_iota(jnp.int32, (CHUNK, CHUNK), 0)
    cols = lax.broadcasted_iota(jnp.int32, (CHUNK, CHUNK), 1)
    spans = [slice(c * CHUNK, (c + 1) * CHUNK) for c in range(count)]
    logits_at = slice(3 * heads_all * HD, (3 * heads_all + 1) * HD)
    @pl.when(group == 0)
    def _():
        hg_ref[...] = jnp.zeros_like(hg_ref)
        rest = gp_ref.shape[1] - logits_at.start
        gp_ref[:, logits_at.start :] = jnp.zeros((length, rest), bf16)
    heads = []
    for h in range(hb):
        lanes = slice(h * HD, (h + 1) * HD)
        grad, out = gm[:, lanes].astype(f32), o[:, lanes].astype(f32)
        scale = lax.rsqrt(jnp.mean(out * out, -1, keepdims=True) + 1e-05)
        hg_ref[0:1, :] += jnp.sum(grad * out * scale, 0, keepdims=True)
        scaled = grad * gain[...]
        down = (scale * scaled - scale * scale * scale * out * jnp.mean(scaled * out, -1, keepdims=True)).astype(bf16)
        heads.append((q[:, lanes], k[:, lanes], down, head_beta(bl[...], group * hb + h, valid), e[:, lanes]))
    cells = [(h, c) for h in range(hb) for c in range(count)]
    scores = [jnp.where(rows >= cols, dot_nt(heads[h][0][spans[c]], heads[h][1][spans[c]]), 0.0).astype(bf16) for h, c in cells]
    errs = [dot_tn(m, heads[h][2][spans[c]]).astype(bf16) for m, (h, c) in zip(scores, cells)]
    firsts = [dot_tn(t[h, c], jnp.concatenate([r, heads[h][1][spans[c]]], 1)) for r, (h, c) in zip(errs, cells)]
    adds = [dot_tn(heads[h][0][spans[c]], heads[h][2][spans[c]]) for h, c in cells]
    states = [jnp.zeros((HD, HD), f32)] * hb
    backs, outs, gls = {}, {}, {}
    for c in reversed(range(count)):
        s = spans[c]
        for h in range(hb):
            cell = h * count + c
            low = states[h].astype(bf16)
            outs[h, c] = low
            full = firsts[cell][:, :HD] + dot(firsts[cell][:, HD:].astype(bf16), low)
            beta = heads[h][3][s]
            gls[h, c] = jnp.sum(full * heads[h][4][s].astype(f32), -1, keepdims=True) * (1.0 - beta)
            backs[h, c] = full * beta
            states[h] = states[h] + adds[cell] - dot_tn(heads[h][1][s], backs[h, c].astype(bf16))
    lane = lax.broadcasted_iota(jnp.int32, (length, HD), 1)
    total = jnp.zeros((length, HD), f32)
    grads = ([], [], [])
    for h in range(hb):
        gl = jnp.concatenate([gls[h, c] for c in range(count)], 0)
        total = jnp.where((lane == group * hb + h) & valid, gl, total)
        qh, kh, dh, _, err = heads[h]
        grads[2].append(jnp.concatenate([backs[h, c] for c in range(count)], 0))
        left = [jnp.concatenate([dh[s], (-backs[h, c]).astype(bf16)], 0) for c, s in enumerate(spans)]
        pairs = [dot_nt(p, err[s]) for p, s in zip(left, spans)]
        pairs = [jnp.concatenate([jnp.where(rows >= cols, p[:CHUNK], 0.0), jnp.where(rows > cols, p[CHUNK:], 0.0)], 0).astype(bf16) for p in pairs]
        first = [dot_nt(p, s_c[h, c]) for c, p in enumerate(left)]
        second = [dot(p, kh[s]) for p, s in zip(pairs, spans)]
        third = [dot_nt(err[s], outs[h, c]) for c, s in enumerate(spans)]
        fourth = [dot_tn(p, jnp.concatenate([qh[s], kh[s]], 0)) for p, s in zip(pairs, spans)]
        grads[0].append(jnp.concatenate([a[:CHUNK] + b[:CHUNK] for a, b in zip(first, second)], 0))
        grads[1].append(jnp.concatenate([a[CHUNK:] + b[CHUNK:] + x + y for a, b, x, y in zip(first, second, third, fourth)], 0))
    gp_ref[:, logits_at] = gp_ref[:, logits_at] + total.astype(bf16)
    for i, (p, w) in enumerate(((pq, wq), (pk, wk), (pv, wv))):
        ext[0:8, :] = jnp.zeros((8, width), f32)
        ext[8:, :] = jnp.where(valid, p[...], 0.0)
        pre = conv_rows(ext, w, length)
        sig = jax.nn.sigmoid(pre)
        pieces = []
        for h in range(hb):
            grad = grads[i][h]
            if i < 2:
                raw = (pre * sig)[:, h * HD:(h + 1) * HD]
                scale = lax.rsqrt(jnp.sum(raw * raw, -1, keepdims=True) + 1e-06)
                grad = scale * (grad - scale * scale * raw * jnp.sum(raw * grad, -1, keepdims=True))
                if i == 0:
                    grad = grad * HD ** -0.5
            pieces.append(grad)
        grad = jnp.concatenate(pieces, 1) if hb > 1 else pieces[0]
        grad = grad * sig * (1.0 + pre * (1.0 - sig))
        gext[0:length, :] = grad
        gext[length:, :] = jnp.zeros((8, width), f32)
        at = pl.ds(pl.multiple_of(i * heads_all * HD + group * width, HD), width)
        for j in range(KERNEL):
            conv_ref[j:j + 1, at] = jnp.sum(grad * ext[5 + j:5 + j + length, :], 0, keepdims=True)
        back = w[3:4] * grad
        for j in range(KERNEL - 1):
            back = back + w[j:j + 1] * gext[3 - j:3 - j + length, :]
        gp_ref[:, at] = jnp.where(valid, back, 0.0).astype(bf16)


def mixer_backward(gm, o, q, k, t, e, s_c, projected, conv_w, gain, nv):
    length = gm.shape[0]
    heads, nc = t.shape[:2]
    hb = 1
    groups = heads // hb
    w = hb * HD
    tok = pl.BlockSpec((length, w), lambda i, *_: (0, i))
    sq = pl.BlockSpec((hb, nc, HD, HD), lambda i, *_: (i, 0, 0, 0))
    col = lambda off: (lambda i, *_: (0, i + off * groups))
    fixed = lambda shape: pl.BlockSpec(shape, lambda i, *_: (0, 0))
    in_specs = [tok, tok, tok, tok, sq, tok, sq, pl.BlockSpec((length, HD), lambda i, *_: (0, 3 * heads))]
    in_specs += [pl.BlockSpec((length, w), col(n)) for n in range(3)]
    in_specs += [pl.BlockSpec((KERNEL, w), col(n)) for n in range(3)]
    in_specs += [fixed((1, HD))]
    wide = (length, pl.cdiv((3 * heads + 1) * HD, 256) * 256)
    return pl.pallas_call(
        functools.partial(mixer_backward_kernel, hb, heads),
        out_shape=(
            jax.ShapeDtypeStruct(wide, bf16),
            jax.ShapeDtypeStruct((KERNEL, 3 * heads * HD), f32),
            jax.ShapeDtypeStruct((8, HD), f32),
        ),
        grid_spec=pltpu.PrefetchScalarGridSpec(
            num_scalar_prefetch=1, grid=(groups,), in_specs=in_specs,
            out_specs=(fixed(wide), fixed((KERNEL, 3 * heads * HD)), fixed((8, HD))),
            scratch_shapes=[pltpu.VMEM((length + 8, w), f32), pltpu.VMEM((length + 8, w), f32)]),
        name="mixer_backward",
    )(nv, gm, o, q, k, t, e, s_c, projected, projected, projected, projected, conv_w, conv_w, conv_w, gain)


def xor(value, axis, step):
    return lax.ppermute(value, axis, [(i, i ^ step) for i in range(lax.axis_size(axis))])


def pick(tensor, index, axis=0):
    return lax.dynamic_index_in_dim(tensor, index, axis, keepdims=False)


def added(a, b):
    return (a.astype(f32) + b.astype(f32)).astype(bf16)


def direct():
    return (lax.axis_size("dp"), lax.axis_size("fsdp"), lax.axis_size("ctx")) == (4, 4, 2)


def mixer_columns(weight, heads):
    n = lax.axis_size("ctx")
    view = weight.reshape(weight.shape[0], 3, heads // n, n, HD)
    return pick(view, lax.axis_index("ctx"), 3).reshape(weight.shape[0], -1)


def beta_columns(weight, heads):
    n = lax.axis_size("ctx")
    view = weight.reshape(weight.shape[0], heads // n, n)
    return jnp.pad(pick(view, lax.axis_index("ctx"), 2), ((0, 0), (0, HD - heads // n)))


def feed_columns(weight):
    n = lax.axis_size("ctx")
    view = weight.reshape(weight.shape[0], 2, n, weight.shape[1] // (2 * n))
    return pick(view, lax.axis_index("ctx"), 2).reshape(weight.shape[0], -1)


def after(value, *others):
    return lax.optimization_barrier((value,) + others)


def start_pieces(tags, places, sources, outs, sems, z, d):
    copies = []
    for tag in tags:
        source, at_first, row_step, same, other = tag
        for at, index, row, col in places(tag, z ^ row_step, other if same else d ^ other):
            rows, width = (s.stop - s.start for s in at)
            target = outs[index].at[pl.ds(row, rows), pl.ds(col, width)]
            copy = pltpu.make_async_copy(
                sources[source].at[at_first + at], target, sems.at[len(copies)]
            )
            copy.start()
            copies.append(copy)
    return copies


def positions():
    return jnp.stack([lax.axis_index(a) for a in ("fsdp", "dp", "ctx")]).astype(jnp.int32)


def project_kernel(tags, places, count, where_ref, x_own, x_far, gain, *refs):
    sources = refs[:count]
    normed_ref, out_ref, full_ref, weight, sems, out_sem = refs[count:]
    step, steps = pl.program_id(0), pl.num_programs(0)
    z, d, c = where_ref[0], where_ref[1], where_ref[2]
    kept = pltpu.make_async_copy(weight, full_ref, out_sem)

    @pl.when(step == 0)
    def _():
        for copy in start_pieces(tags, places, sources, (weight,), sems, z, d):
            copy.wait()
        kept.start()

    x = jnp.where(step == c, x_own[...], x_far[...]).astype(f32)
    scale = lax.rsqrt(jnp.mean(x * x, -1, keepdims=True) + 1e-06)
    normed = (x * scale * gain[...]).astype(bf16)
    normed_ref[...] = normed
    out_ref[...] = dot(normed, weight[...])

    @pl.when(step == steps - 1)
    def _():
        kept.wait()


def project(x_own, x_far, gain, pieces, width):
    arrays, tags, places = pieces
    rows, depth = x_own.shape
    half = pl.BlockSpec((rows, depth), lambda i, *_: (0, 0))
    each = lambda w: pl.BlockSpec((rows, w), lambda i, *_: (i, 0))
    anywhere = pl.BlockSpec(memory_space=pl.ANY)
    return pl.pallas_call(
        functools.partial(project_kernel, tags, places, len(arrays)),
        out_shape=(
            jax.ShapeDtypeStruct((2 * rows, depth), bf16),
            jax.ShapeDtypeStruct((2 * rows, width), f32),
            jax.ShapeDtypeStruct((depth, width), bf16),
        ),
        grid_spec=pltpu.PrefetchScalarGridSpec(
            num_scalar_prefetch=1,
            grid=(2,),
            in_specs=[half, half, pl.BlockSpec((1, depth), lambda i, *_: (0, 0))]
            + [anywhere] * len(arrays),
            out_specs=(each(depth), each(width), anywhere),
            scratch_shapes=[
                pltpu.VMEM((depth, width), bf16),
                pltpu.SemaphoreType.DMA((len(tags),)),
                pltpu.SemaphoreType.DMA,
            ],
        ),
        name="projections",
    )(positions(), x_own, x_far, gain, *arrays)


def near_first(i, where):
    return ((where[2] + i) % 2, 0)


def attend_kernel(tags, places, count, where_ref, merged, *refs):
    sources = refs[:count]
    near, far, full_ref, weight, sems, out_sem = refs[count:]
    step, steps = pl.program_id(0), pl.num_programs(0)
    z, d = where_ref[0], where_ref[1]
    kept = pltpu.make_async_copy(weight, full_ref, out_sem)

    @pl.when(step == 0)
    def _():
        for copy in start_pieces(tags, places, sources, (weight,), sems, z, d):
            copy.wait()
        kept.start()

    total = dot(merged[...], weight[...])

    @pl.when(step == 0)
    def _():
        near[...] = total

    @pl.when(step == 1)
    def _():
        far[...] = total.astype(bf16)

    @pl.when(step == steps - 1)
    def _():
        kept.wait()


def near_spec(block, width):
    return pl.BlockSpec((block, width), lambda i, *_: (0, 0))


def far_spec(block, width):
    return pl.BlockSpec((block, width), lambda i, *_: (0, 0))


def attend(merged, pieces, width):
    arrays, tags, places = pieces
    rows, depth = merged.shape
    block = rows // 2
    anywhere = pl.BlockSpec(memory_space=pl.ANY)
    return pl.pallas_call(
        functools.partial(attend_kernel, tags, places, len(arrays)),
        out_shape=(
            jax.ShapeDtypeStruct((rows // 2, width), f32),
            jax.ShapeDtypeStruct((rows // 2, width), bf16),
            jax.ShapeDtypeStruct((depth, width), bf16),
        ),
        grid_spec=pltpu.PrefetchScalarGridSpec(
            num_scalar_prefetch=1,
            grid=(2,),
            in_specs=[pl.BlockSpec((block, depth), near_first)] + [anywhere] * len(arrays),
            out_specs=(near_spec(block, width), far_spec(block, width), anywhere),
            scratch_shapes=[
                pltpu.VMEM((depth, width), bf16),
                pltpu.SemaphoreType.DMA((2 * len(tags),)),
                pltpu.SemaphoreType.DMA,
            ],
        ),
        name="mixer_out",
    )(positions(), merged, *arrays)


def merged_grad_kernel(where_ref, own, far, weight, out):
    grad = jnp.where(pl.program_id(0) == 0, own[...], far[...])
    out[...] = dot_nt(grad, weight[...])


def merged_grad(own, far, weight):
    rows, width = own.shape
    depth = weight.shape[0]
    block = rows
    return pl.pallas_call(
        merged_grad_kernel,
        out_shape=jax.ShapeDtypeStruct((2 * rows, depth), f32),
        grid_spec=pltpu.PrefetchScalarGridSpec(
            num_scalar_prefetch=1,
            grid=(2,),
            in_specs=[
                near_spec(block, width),
                far_spec(block, width),
                pl.BlockSpec((depth, width), lambda i, *_: (0, 0)),
            ],
            out_specs=pl.BlockSpec((block, depth), near_first),
        ),
        name="merged_gradient",
    )(positions(), own, far, weight)


def normed_grad_kernel(where_ref, grad, weight, near, far):
    total = dot_nt(grad[...], weight[...])

    @pl.when(pl.program_id(0) == 0)
    def _():
        near[...] = total

    @pl.when(pl.program_id(0) == 1)
    def _():
        far[...] = total.astype(bf16)


def normed_grad(grad, weight):
    rows, (depth, width) = grad.shape[0], weight.shape
    block = rows // 2
    return pl.pallas_call(
        normed_grad_kernel,
        out_shape=(
            jax.ShapeDtypeStruct((rows // 2, depth), f32),
            jax.ShapeDtypeStruct((rows // 2, depth), bf16),
        ),
        grid_spec=pltpu.PrefetchScalarGridSpec(
            num_scalar_prefetch=1,
            grid=(2,),
            in_specs=[
                pl.BlockSpec((block, width), near_first),
                pl.BlockSpec((depth, width), lambda i, *_: (0, 0)),
            ],
            out_specs=(near_spec(block, depth), far_spec(block, depth)),
        ),
        name="normed_gradient",
    )(positions(), grad, weight)


def keep_and_send(total, where_ref, refs, col):
    low_keep, low_send, high_keep, high_send = refs
    first_low, first_high = where_ref[1] % 2 == 0, where_ref[1] // 2 == 0
    short = total.shape[0] // 32
    block = lambda i: total[i * short : (i + 1) * short]
    for z in range(2):
        for i in range(4):
            a, b = block(8 * z + 2 * i), block(8 * z + 2 * i + 1)
            low_keep[i % 2, z, i // 2, col, :] = jnp.where(first_low, a, b)
            low_send[i % 2, z, i // 2, col, :] = jnp.where(first_low, b, a)
            k = 16 + 8 * z + (i // 2) * 4 + i % 2
            a, b = block(k), block(k + 2)
            high_keep[i % 2, z, i // 2, col, :] = jnp.where(first_high, a, b)
            high_send[i % 2, z, i // 2, col, :] = jnp.where(first_high, b, a)


def weight_grad_kernel(parts, steps, where_ref, *refs):
    lefts, grad = refs[:parts], refs[parts]
    turned = refs[-1]
    step = pl.program_id(0)
    c = where_ref[2]

    @pl.when(step == 0)
    def _():
        at = 0
        for left in lefts:
            rows = left.shape[0]
            turned[:, at : at + rows] = left[...].T
            at += rows

    if len(refs) == parts + 6:
        every = slice(None)
        keep_and_send(dot(turned[...], grad[...]).astype(bf16), where_ref, refs[-5:-1], every)
        return

    merged, own, far = refs[parts + 1 : parts + 4]
    outs = refs[-5:-1]

    @pl.when(step < steps)
    def _():
        keep_and_send(dot(turned[...], grad[...]).astype(bf16), where_ref, outs, slice(None))

    @pl.when(step >= steps)
    def _():
        rows, half = own.shape[0], own.shape[1] // 2
        mine = merged[pl.ds(pl.multiple_of(c * rows, rows), rows), :]
        theirs = merged[pl.ds(pl.multiple_of((1 - c) * rows, rows), rows), :]
        width = outs[0].shape[-1]
        for k in range(2):
            at = pl.ds(pl.multiple_of(k * half + (step - steps) * width, width), width)
            part = (dot_tn(mine, own[:, at]) + dot_tn(theirs, far[:, at])).astype(bf16)
            lines = part.shape[0] // 32
            keep_and_send(part, where_ref, outs, slice(k * lines, (k + 1) * lines))


def weight_grad(lefts, grad, out=()):
    depth = lefts[0].shape[1]
    rows = sum(a.shape[0] for a in lefts)
    block = 256
    steps = pl.cdiv(grad.shape[1], block)
    more = out[1].shape[1] // 2 if out else 0
    shape = jax.ShapeDtypeStruct((2, 2, 2, depth // 32, grad.shape[1] + more), bf16)
    each = pl.BlockSpec((2, 2, 2, depth // 32, block), lambda i, *_: (0, 0, 0, 0, i))
    whole = lambda a: pl.BlockSpec(a.shape, lambda i, *_: (0, 0))
    specs = [whole(a) for a in lefts]
    specs += [pl.BlockSpec((rows, block), lambda i, *_: (0, jnp.minimum(i, steps - 1)))]
    specs += [whole(a) for a in out]
    return pl.pallas_call(
        functools.partial(weight_grad_kernel, len(lefts), steps),
        out_shape=(shape,) * 4,
        grid_spec=pltpu.PrefetchScalarGridSpec(
            num_scalar_prefetch=1,
            grid=(steps + more // block,),
            in_specs=specs,
            out_specs=(each,) * 4,
            scratch_shapes=[pltpu.VMEM((depth, rows), bf16)],
        ),
        name="weight_gradient",
    )(positions(), *lefts, grad, *out)


def down_grad_kernel(hidden, own, far, out, turned):
    rows = own.shape[0]

    @pl.when(pl.program_id(0) == 0)
    def _():
        turned[...] = hidden[...].T

    total = dot(turned[:, :rows], own[...]) + dot(turned[:, rows:], far[...])
    out[...] = total.astype(bf16)


def down_gradient(hidden, own, far):
    rows, width = own.shape
    half = hidden.shape[1]
    block = 256
    return pl.pallas_call(
        down_grad_kernel,
        out_shape=jax.ShapeDtypeStruct((half, width), bf16),
        grid=(width // block,),
        in_specs=[
            pl.BlockSpec((2 * rows, half), lambda i: (0, 0)),
            pl.BlockSpec((rows, block), lambda i: (0, i)),
            pl.BlockSpec((rows, block), lambda i: (0, i)),
        ],
        out_specs=pl.BlockSpec((half, block), lambda i: (0, i)),
        scratch_shapes=[pltpu.VMEM((half, 2 * rows), bf16)],
        name="down_gradient",
    )(hidden, own, far)


def whole_rows(weight):
    return lax.all_gather(weight, "fsdp", axis=0, tiled=True)


def exchange(blocks, axis):
    return lax.all_to_all(blocks, axis, 0, 0, tiled=True)


def to_all(piece, axis):
    return exchange(jnp.broadcast_to(piece, (lax.axis_size(axis),) + piece.shape), axis)


def bounds(total, step):
    return [slice(i, min(i + step, total)) for i in range(0, total, step)]


def feed_kernel(tags, places, count_down, own, where_ref, x_own, x_other, e_own, e_other, *refs):
    count = 1 + max(t[0] for t in tags)
    sources, downs = refs[:count], refs[count : count + count_down]
    hidden_ref, grad_ref, near_out, far_out, near_grad, far_grad = refs[count + count_down : -3]
    gateup, down, sems = refs[-3:]
    step = pl.program_id(0)
    z, d, c = where_ref[0], where_ref[1], where_ref[2]

    @pl.when(step == 0)
    def _():
        copies = start_pieces(tags, places, sources, (gateup,), sems, z, d)
        rows, cols = downs[1].shape[1:]
        for j in range(2):
            for source, at, first in ((downs[0], 2 * c + j, c), (downs[1], j, 1 - c)):
                col = pl.multiple_of(first * cols, HD)
                copy = pltpu.make_async_copy(
                    source.at[at],
                    down.at[pl.ds(j * rows, rows), pl.ds(col, cols)],
                    sems.at[len(copies)],
                )
                copy.start()
                copies.append(copy)
        for copy in copies:
            copy.wait()

    near = step < own
    x = jnp.where(near, x_own[...], x_other[...])
    e = jnp.where(near, e_own[...], e_other[...])
    half = down.shape[0]
    for j in bounds(half, 256):
        up_j = slice(half + j.start, half + j.stop)
        gate = dot(x, gateup[:, j])
        up = dot(x, gateup[:, up_j])
        grad = dot_nt(e, down[j, :])
        sig = jax.nn.sigmoid(gate)
        act = gate * sig
        hidden_ref[:, j] = (act * up).astype(bf16)
        grad_ref[:, j] = (grad * up * sig * (1.0 + gate * (1.0 - sig))).astype(bf16)
        grad_ref[:, up_j] = (grad * act).astype(bf16)
    out = dot(hidden_ref[...], down[...])
    back = dot_nt(grad_ref[...], gateup[...])

    @pl.when(near)
    def _():
        near_out[...] = out
        near_grad[...] = back

    @pl.when(jnp.logical_not(near))
    def _():
        far_out[...] = out.astype(bf16)
        far_grad[...] = back.astype(bf16)


def feed(x_own, x_other, e_own, e_other, wide, down):
    arrays, tags, places = wide
    rows, width = x_own.shape
    others = x_other.shape[0]
    half = 2 * down[1].shape[1]
    block = rows
    own, steps = rows // block, (rows + others) // block
    near = lambda w: pl.BlockSpec((block, w), lambda i, *_: (jnp.minimum(i, own - 1), 0))
    far = lambda w: pl.BlockSpec((block, w), lambda i, *_: (jnp.maximum(i - own, 0), 0))
    each = lambda w: pl.BlockSpec((block, w), lambda i, *_: (i, 0))
    anywhere = pl.BlockSpec(memory_space=pl.ANY)
    return pl.pallas_call(
        functools.partial(feed_kernel, tags, places, len(down), own),
        out_shape=(
            jax.ShapeDtypeStruct((rows + others, half), bf16),
            jax.ShapeDtypeStruct((rows + others, 2 * half), bf16),
            jax.ShapeDtypeStruct((rows, width), f32),
            jax.ShapeDtypeStruct((others, width), bf16),
            jax.ShapeDtypeStruct((rows, width), f32),
            jax.ShapeDtypeStruct((others, width), bf16),
        ),
        grid_spec=pltpu.PrefetchScalarGridSpec(
            num_scalar_prefetch=1,
            grid=(steps,),
            in_specs=[near(width), far(width), near(width), far(width)]
            + [anywhere] * (len(arrays) + len(down)),
            out_specs=(each(half), each(2 * half), near(width), far(width), near(width), far(width)),
            scratch_shapes=[
                pltpu.VMEM((width, 2 * half), bf16),
                pltpu.VMEM((half, width), bf16),
                pltpu.SemaphoreType.DMA((4 + len(tags),)),
            ],
        ),
        name="feed_forward",
    )(positions(), x_own, x_other, e_own, e_other, *arrays, *down)


def pack_kernel(heads, where_ref, qkv, beta, out, gateup, mixed_ref, wide_ref, every):
    rows = qkv.shape[0]
    strips = qkv.shape[1] // (2 * HD)
    mixed = (strips + 1) * HD
    width = gateup.shape[1] // 4
    half = out.shape[1] // 2
    short = out.shape[0]
    for c in range(2):

        @pl.when(where_ref[1] == c)
        def _():
            for i in range(strips):
                at = (2 * i + c) * HD
                mixed_ref[:, i * HD : (i + 1) * HD] = qkv[:, at : at + HD]
            source = lax.broadcasted_iota(jnp.int32, (heads, HD), 0)
            lane = lax.broadcasted_iota(jnp.int32, (heads, HD), 1)
            chosen = (source == 2 * lane + c).astype(f32).astype(bf16)
            every[...] = dot_tn(beta[...], chosen)
            here = pl.ds(pl.multiple_of(where_ref[0] * rows, rows), rows)
            mixed_ref[:, strips * HD : mixed] = every[here, :].astype(bf16)
            for i in range(2):
                at = (2 * i + c) * width
                wide_ref[0, :, i * width : (i + 1) * width] = gateup[:, at : at + width]

    wide_ref[0, :short, 2 * width :] = out[:, :half]
    wide_ref[0, short:, 2 * width :] = out[:, half:]
    for i in range(1, 4):
        wide_ref[i] = wide_ref[0]


def pack(w_qkv, w_beta, w_out, w_gateup):
    rows, short = w_qkv.shape[0] // 4, HD // 4
    heads = w_beta.shape[1]
    here = jnp.stack([lax.axis_index("dp"), lax.axis_index("ctx")]).astype(jnp.int32)
    mixed = w_qkv.shape[1] // 2 + HD
    wide = w_gateup.shape[1] // 2 + w_out.shape[1] // 2
    fixed = lambda *shape: pl.BlockSpec(shape, lambda i, *_: (0,) * len(shape))
    mine = lambda width: pl.BlockSpec((rows, width), lambda i, at: (at[0], 0))
    shapes = ((rows, mixed), (4, rows, wide))
    return pl.pallas_call(
        functools.partial(pack_kernel, heads),
        out_shape=tuple(jax.ShapeDtypeStruct(s, bf16) for s in shapes),
        grid_spec=pltpu.PrefetchScalarGridSpec(
            num_scalar_prefetch=1,
            grid=(1,),
            in_specs=[
                mine(w_qkv.shape[1]),
                pl.BlockSpec(w_beta.shape[::-1], lambda i, *_: (0, 0)),
                pl.BlockSpec((short, w_out.shape[1]), lambda i, at: (at[1] * 4 + at[0], 0)),
                mine(w_gateup.shape[1]),
            ],
            out_specs=tuple(fixed(*s) for s in shapes),
            scratch_shapes=[pltpu.VMEM((w_beta.shape[0], HD), f32)],
        ),
        name="weight_pieces",
    )(here, w_qkv, w_beta.T, w_out, w_gateup)


def gather_direct(mixed_piece, wide_piece, down_shard):
    z, c = lax.axis_index("fsdp"), lax.axis_index("ctx")
    own = [mixed_piece] + [xor(mixed_piece, "dp", k) for k in (1, 2, 3)]
    rows = [xor(mixed_piece, "fsdp", k) for k in (1, 2, 3)]
    wide_piece, *got = after(wide_piece, *own[1:], *rows)
    own[1:], rows = got[:3], got[3:]
    wide_own = [wide_piece[0]] + [xor(wide_piece[0], "dp", k) for k in (1, 2, 3)]
    wide_rows = exchange(wide_piece, "fsdp")
    rows, *wide_own[1:] = after(jnp.stack(rows), *wide_own[1:])
    rest = [rows] + [xor(rows, "dp", k) for k in (1, 2, 3)]
    half = down_shard.shape[1] // 2
    mine = lax.dynamic_slice_in_dim(down_shard, c * half, half, 1)
    tags = [(k, (), 0, False, k) for k in range(4)]
    tags += [(4 + i, (k - 1,), k, False, i) for i in range(4) for k in (1, 2, 3)]
    return own + rest, tags, wide_own, wide_rows, mine


def spread_first(own, wide_rows, mine):
    z = lax.axis_index("fsdp")
    half = wide_rows.shape[2] // 2
    low = jnp.stack([pick(wide_rows, z ^ k)[:, :half] for k in (1, 2, 3)])
    high = jnp.stack([pick(wide_rows, z ^ k)[:, half:] for k in (1, 2, 3)])
    low, high = [low, xor(low, "dp", 1)], [high, xor(high, "dp", 2)]
    mine, wide_rows = after(mine, wide_rows)
    return own, low, high, to_all(mine, "fsdp")


def spread_second(full, own, low, high):
    full, low[1], high[1] = after(full, low[1], high[1])
    low = low + [xor(low[0], "dp", 2), xor(low[1], "dp", 2)]
    high = [high[0], xor(high[0], "dp", 1), high[1], xor(high[1], "dp", 1)]
    tags = [(k, (), 0, False, k) for k in range(4)]
    tags += [(4 + i, (k - 1,), k, False, i) for i in range(4) for k in (1, 2, 3)]
    tags += [(8 + i, (k - 1,), k, False, i) for i in range(4) for k in (1, 2, 3)]
    return full, own + low + high, tags


def gather_weights(w_qkv, w_beta, w_out, w_gateup, w_down, heads):
    n, c = lax.axis_size("ctx"), lax.axis_index("ctx")
    if not direct():
        mixed = jnp.concatenate([mixer_columns(w_qkv, heads), beta_columns(w_beta, heads)], 1)
        out = whole_rows(w_out).reshape(heads // n, n, HD, -1)
        down = whole_rows(w_down)
        return (
            whole_rows(mixed),
            whole_rows(feed_columns(w_gateup)),
            pick(out, c, 1).reshape(-1, w_out.shape[1]),
            pick(down.reshape(n, -1, down.shape[1]), c),
        )
    rows, short = w_qkv.shape[0] // 4, HD // 4
    mixed_piece, wide_piece = pack(w_qkv, w_beta, w_out, w_gateup)
    mixed, width, half = mixed_piece.shape[1], w_gateup.shape[1] // 2, w_out.shape[1] // 2
    mixed_all, mixed_tags, own, wide_rows, mine = gather_direct(mixed_piece, wide_piece, w_down)
    cut = (width + half) // 2

    def mixed_places(tag, z, d):
        row = pl.multiple_of(z * (4 * rows) + d * rows, rows)
        return [((slice(0, rows), slice(0, mixed)), 0, row, 0)]

    def out_places(tag, z, d):
        row = pl.multiple_of(z * HD + d * short, short)
        first = width if tag[0] < 4 else width - cut
        at = slice(first, first + half)
        return [
            ((slice(0, short), at), 0, row, 0),
            ((slice(short, 2 * short), at), 0, row, half),
        ]

    def feed_places(tag, z, d):
        row = pl.multiple_of(z * (4 * rows) + d * rows, rows)
        if tag[0] < 4:
            at, col = slice(0, width), 0
        elif tag[0] < 8:
            at, col = slice(0, cut), 0
        else:
            at, col = slice(0, width - cut), cut
        return [((slice(0, rows), at), 0, row, col)]

    spread = spread_first(own, wide_rows, mine)

    def further(full):
        full, wide_all, wide_tags = spread_second(full, *spread[:3])
        out_tags = [t for t in wide_tags if not 4 <= t[0] < 8]
        wide = wide_all, wide_tags, feed_places
        return full, wide, (wide_all, out_tags, out_places), spread[3]

    return (mixed_all, mixed_tags, mixed_places), further


def feed_both(normed, grad_feed, gateup, down):
    if direct():
        normed_far, grad_far = xor(normed, "ctx", 1), xor(grad_feed, "ctx", 1)
        theirs = pick(down.reshape((2, 2) + down.shape[1:]), 1 - lax.axis_index("ctx"))
        down = [down, xor(theirs, "ctx", 1)]
        hidden, grad, out, out_far, back, back_far = feed(
            normed, normed_far, grad_feed, grad_far, gateup, down
        )
        out = out + xor(out_far, "ctx", 1).astype(f32)
        back = back + xor(back_far, "ctx", 1).astype(f32)
        return (normed, normed_far), (grad_feed, grad_far), hidden, grad, out, back
    normed, grad_feed = both_pieces(normed), both_pieces(grad_feed)
    gate_up = jnp.dot(normed, gateup, preferred_element_type=f32)
    ff_width = gate_up.shape[1] // 2
    gate_part = gate_up[:, :ff_width]
    up_part = gate_up[:, ff_width:]
    gate_sig = jax.nn.sigmoid(gate_part)
    hidden = (gate_part * gate_sig * up_part).astype(bf16)
    contract_cols = (((1,), (1,)), ((), ()))
    grad_hidden = lax.dot_general(grad_feed, down, contract_cols, preferred_element_type=f32)
    grad_gate = grad_hidden * up_part * gate_sig * (1.0 + gate_part * (1.0 - gate_sig))
    grad = jnp.concatenate([grad_gate, grad_hidden * gate_part * gate_sig], 1).astype(bf16)
    out = own_piece(jnp.dot(hidden, down, preferred_element_type=f32))
    back = own_piece(lax.dot_general(grad, gateup, contract_cols, preferred_element_type=f32))
    return normed, grad_feed, hidden, grad, out, back


def both_pieces(mine):
    n = lax.axis_size("ctx")
    if n != 2:
        return lax.all_gather(mine, "ctx", axis=0, tiled=True)
    other = xor(mine, "ctx", 1)
    first = lax.axis_index("ctx") == 0
    return jnp.concatenate([jnp.where(first, mine, other), jnp.where(first, other, mine)], 0)


def own_piece(partial):
    n = lax.axis_size("ctx")
    rows = partial.shape[0] // n
    if n != 2:
        return lax.psum_scatter(
            partial.astype(bf16), "ctx", scatter_dimension=0, tiled=True
        ).astype(f32)
    here = lax.axis_index("ctx")
    theirs = lax.dynamic_slice_in_dim(partial, (1 - here) * rows, rows, 0).astype(bf16)
    mine = lax.dynamic_slice_in_dim(partial, here * rows, rows, 0)
    return mine.astype(f32) + xor(theirs, "ctx", 1).astype(f32)


def replicas_first(part):
    d = lax.axis_index("dp")
    high, low = d // 2, d % 2
    a, b = part[:2], part[2:]
    got = xor(pick(a, 1 - low, 3), "dp", 1), xor(pick(b, 1 - high, 2), "dp", 2)
    return (pick(a, low, 3), pick(b, high, 2)), got


def halves_kernel(where_ref, *refs):
    for i in range(4):
        total = refs[2 * i][0].astype(f32) + refs[2 * i + 1][0].astype(f32)
        refs[8 + i][...] = total.astype(bf16)


def replicas_second(kept, got):
    shape = kept[0].shape[1:]
    block = (1, 1) + shape[1:]
    zeros = (0,) * (len(shape) - 1)
    high = lambda i, at: (at[1] // 2, i) + zeros
    not_high = lambda i, at: (1 - at[1] // 2, i) + zeros
    low = lambda i, at: (at[1] % 2, i) + zeros
    not_low = lambda i, at: (1 - at[1] % 2, i) + zeros
    specs, arrays = [], []
    for k, maps in ((0, (high, not_high)), (1, (low, not_low))):
        for chosen in maps:
            specs += [pl.BlockSpec(block, chosen)] * 2
            arrays += [kept[k], got[k]]
    outs = pl.pallas_call(
        halves_kernel,
        out_shape=(jax.ShapeDtypeStruct(shape, bf16),) * 4,
        grid_spec=pltpu.PrefetchScalarGridSpec(
            num_scalar_prefetch=1,
            grid=(2,),
            in_specs=specs,
            out_specs=(pl.BlockSpec((1,) + shape[1:], lambda i, *_: (i,) + zeros),) * 4,
        ),
        name="first_sums",
    )(positions(), *arrays)
    return (outs[0], outs[2]), (outs[1], outs[3])


def over_replicas(kept, got):
    return jnp.concatenate([added(kept[0], got[0]), added(kept[1], got[1])], 0)


def sent_kernel(where_ref, more, a_kept, a_got, b_kept, b_got, *outs):
    step = pl.program_id(0)
    a = a_kept[0].astype(f32) + a_got[0].astype(f32)
    b = b_kept[0].astype(f32) + b_got[0].astype(f32)
    total = jnp.where((where_ref[0] ^ step) < 2, a, b).astype(bf16)
    width = total.shape[2]
    for k in range(4):

        @pl.when(step == k)
        def _():
            outs[k][:, :, :width] = total
            outs[k][:, :, width:] = more[...]


def sent_rows(kept, got, more):
    shape = kept[0].shape[1:]
    zeros = (0,) * len(shape)
    a = pl.BlockSpec((1,) + shape, lambda i, at: (jnp.minimum(at[0] ^ i, 1),) + zeros)
    b = pl.BlockSpec((1,) + shape, lambda i, at: (jnp.maximum((at[0] ^ i) - 2, 0),) + zeros)
    wider = shape[:2] + (shape[2] + more.shape[2],)
    return pl.pallas_call(
        sent_kernel,
        out_shape=(jax.ShapeDtypeStruct(wider, bf16),) * 4,
        grid_spec=pltpu.PrefetchScalarGridSpec(
            num_scalar_prefetch=1,
            grid=(4,),
            in_specs=[pl.BlockSpec(more.shape, lambda i, *_: zeros), a, a, b, b],
            out_specs=(pl.BlockSpec(wider, lambda i, *_: zeros),) * 4,
        ),
        name="sums_sent",
    )(positions(), more, kept[0], got[0], kept[1], got[1])


def summed_pairs(own, got):
    own, *got = (part.astype(f32) for part in (own, *got))
    return (own + got[0]) + (got[1] + got[2])


def both_columns(part):
    c = lax.axis_index("ctx")
    other = xor(pick(part, 1 - c), "ctx", 1)
    mine = pick(part, c)
    first = c == 0
    return jnp.stack([jnp.where(first, mine, other), jnp.where(first, other, mine)])


def finish_kernel(moves, count, where_ref, *refs):
    sources, outs = refs[:count], refs[count:]
    d = where_ref[1]
    for source, at, index, to in moves:
        if len(to) == 4:
            row = pl.multiple_of((d ^ to[0]) * to[1] + to[2], to[1])
            to = (pl.ds(row, to[1]), to[3])
        elif len(to) == 3:
            if isinstance(to[0], int):
                to = (pl.ds(pl.multiple_of((d ^ to[0]) * to[1], to[1]), to[1]), to[2])
            else:
                to = (to[0], pl.ds(pl.multiple_of((d ^ to[1]) * to[2], HD), to[2]))
        outs[index][to] = sources[source][at].astype(f32)


def finish(sources, moves, shapes, name):
    whole = lambda shape: pl.BlockSpec(shape, lambda i, *_: (0,) * len(shape))
    return pl.pallas_call(
        functools.partial(finish_kernel, moves, len(sources)),
        out_shape=tuple(jax.ShapeDtypeStruct(s, f32) for s in shapes),
        grid_spec=pltpu.PrefetchScalarGridSpec(
            num_scalar_prefetch=1,
            grid=(1,),
            in_specs=[whole(s.shape) for s in sources],
            out_specs=tuple(whole(s) for s in shapes),
        ),
        name=name,
    )(positions(), *sources)


def blocks_of(grad, n, z):
    return grad.reshape(z, n, 2, 2, grad.shape[0] // (4 * z * n), grad.shape[1])


def scattered(full):
    share = lax.psum_scatter(full.astype(bf16), ("fsdp", "ctx"), scatter_dimension=0, tiled=True)
    return lax.psum(share, "dp").astype(f32)


def placed_at_ctx(part, axis):
    n = lax.axis_size("ctx")
    shape = [1] * (part.ndim + 1)
    shape[axis] = n
    here = (jnp.arange(n) == lax.axis_index("ctx")).reshape(shape)
    return jnp.where(here, jnp.expand_dims(part, axis), 0)


def sum_columns(grad, views, widths):
    outs, start = [], 0
    for shape, size in zip(views, widths):
        part = grad[:, start : start + size].reshape((grad.shape[0],) + shape)
        full = placed_at_ctx(part, part.ndim - 1)
        outs.append(scattered(full.reshape(grad.shape[0], -1)))
        start += size
    return outs


def added_up(parts):
    total = parts[0].astype(f32)
    for i in range(1, parts.shape[0]):
        total = total + parts[i].astype(f32)
    return total.astype(bf16)


def quarter(part, k):
    cols = part.shape[1] // 4
    return lax.dynamic_slice_in_dim(part, (lax.axis_index("dp") ^ k) * cols, cols, 1)


def down_to_owners(part):
    pairs = [(z * 2 + c, (2 * c + z // 2) * 2 + z % 2) for z in range(4) for c in range(2)]
    return lax.ppermute(part, ("fsdp", "ctx"), pairs)


def local(
    inputs,
    lengths,
    cotangent,
    norm_gain1,
    w_qkv,
    w_beta,
    conv_weight,
    head_gain,
    w_out,
    norm_gain2,
    w_gateup,
    w_down,
):
    n = lax.axis_size("ctx")
    heads_all = w_beta.shape[1]
    heads = heads_all // n
    tokens_in = inputs[0].astype(f32)
    piece_len, model_width = tokens_in.shape
    length = piece_len * n
    conv_mine = mixer_columns(conv_weight, heads_all)
    positions_here = jnp.arange(length, dtype=jnp.int32)
    start = lax.axis_index("ctx") * piece_len
    valid = ((start + positions_here[:piece_len]) < lengths[0]).astype(f32)[:, None]
    grad_feed = (cotangent[0].astype(f32) * valid).astype(bf16)
    if direct():
        pieces, further = gather_weights(w_qkv, w_beta, w_out, w_gateup, w_down, heads_all)
        far_rows = xor(inputs[0], "ctx", 1)
        normed_one, projected, mixed = project(
            inputs[0], far_rows, norm_gain1[None], pieces, (3 * heads + 1) * HD
        )
        projected, gateup, out, down = further(projected)
    else:
        mixed, gateup, out, down = gather_weights(
            w_qkv, w_beta, w_out, w_gateup, w_down, heads_all
        )
        tokens_all = both_pieces(inputs[0]).astype(f32)
        scale_all = lax.rsqrt(jnp.mean(tokens_all * tokens_all, -1, keepdims=True) + 1e-06)
        normed_one = (tokens_all * scale_all * norm_gain1).astype(bf16)
        projected = jnp.dot(normed_one, mixed, preferred_element_type=f32)
    queries, keys, inverse, errors, states, heads_out, merged = mixer_forward(
        projected, conv_mine, head_gain[None], lengths, heads
    )
    if direct():
        near, far, out = attend(merged, out, model_width)
        attention = near + xor(far, "ctx", 1).astype(f32)
    else:
        attention = own_piece(jnp.dot(merged, out, preferred_element_type=f32))
    middle = tokens_in + attention
    scale_two = lax.rsqrt(jnp.mean(middle * middle, -1, keepdims=True) + 1e-06)
    normed_two = (middle * scale_two * norm_gain2).astype(bf16)
    normed_two, feed_all, hidden, grad_gate_up, feed_out, grad_normed_two = feed_both(
        normed_two, grad_feed, gateup, down
    )
    output = (middle + feed_out).astype(bf16)
    contract_cols = (((1,), (1,)), ((), ()))
    contract_rows = (((0,), (0,)), ((), ()))
    ff_width = hidden.shape[1]
    if direct():
        down_grad = down_gradient(hidden, *feed_all)
        grad_gate_up, down_grad = after(grad_gate_up, down_grad)
        down_got = exchange(down_grad.reshape(4, down_grad.shape[0] // 4, -1), "fsdp")
        low_kept, low_sent, high_kept, high_sent = weight_grad(normed_two, grad_gate_up)
        wide_kept = low_kept, high_kept
        wide_got = xor(low_sent, "dp", 1), xor(high_sent, "dp", 2)
        grad_normed_two, low_sent = after(grad_normed_two, low_sent)
    else:
        down_grad = lax.dot_general(
            hidden, feed_all, contract_rows, preferred_element_type=f32
        ).astype(bf16)
        gateup_grad = lax.dot_general(
            normed_two, grad_gate_up, contract_rows, preferred_element_type=f32
        ).astype(bf16)
    gain_two_term = jnp.sum(grad_normed_two * middle * scale_two, 0)
    scaled_two = grad_normed_two * norm_gain2
    grad_middle = (
        grad_feed.astype(f32)
        + scale_two * scaled_two
        - scale_two
        * scale_two
        * scale_two
        * middle
        * jnp.mean(scaled_two * middle, -1, keepdims=True)
    )
    grad_attention = grad_middle.astype(bf16)
    if direct():
        grad_far = xor(grad_attention, "ctx", 1)
        grad_merged = merged_grad(grad_attention, grad_far, out)
    else:
        grad_attention = both_pieces(grad_attention)
        out_grad = lax.dot_general(
            merged, grad_attention, contract_rows, preferred_element_type=f32
        ).astype(bf16)
        grad_merged = lax.dot_general(
            grad_attention, out, contract_cols, preferred_element_type=f32
        )
    grad_mixed, conv_term, gain_rows = mixer_backward(
        grad_merged, heads_out, queries, keys, inverse, errors, states,
        projected, conv_mine, head_gain[None], lengths,
    )
    if direct():
        grad_mixed, *wide_got = after(grad_mixed, *wide_got)
        wide_kept, wide_sent = replicas_second(wide_kept, wide_got)
        grad_mixed, *wide_sent = after(grad_mixed, *wide_sent)
        wide_got = xor(wide_sent[0], "dp", 2), xor(wide_sent[1], "dp", 1)
        low_kept, low_sent, high_kept, high_sent = weight_grad(
            (normed_one,), grad_mixed, (merged, grad_attention, grad_far)
        )
        mixed_kept = low_kept, high_kept
        mixed_got = xor(low_sent, "dp", 1), xor(high_sent, "dp", 2)
        grad_mixed, low_kept = after(grad_mixed, mixed_kept[0])
        mixed_kept = low_kept, mixed_kept[1]
        near, far = normed_grad(grad_mixed, mixed)
        near, far, down_got, *wide_got = after(near, far, down_got, *wide_got)
        wide = exchange(over_replicas(wide_kept, wide_got), "fsdp")
        down_part = added_up(down_got)
        near, *mixed_got = after(near, *mixed_got)
        grad_normed_one = near + xor(far, "ctx", 1).astype(f32)
        mixed_kept, mixed_sent = replicas_second(mixed_kept, mixed_got)
        mixed_got = xor(mixed_sent[0], "dp", 2), xor(mixed_sent[1], "dp", 1)
    else:
        mixed_grad = lax.dot_general(
            normed_one, grad_mixed, contract_rows, preferred_element_type=f32
        ).astype(bf16)
        grad_normed_one = own_piece(
            lax.dot_general(grad_mixed, mixed, contract_cols, preferred_element_type=f32)
        )
        (gateup_total,) = sum_columns(gateup_grad, [(2, ff_width)], [2 * ff_width])
        down_total = scattered(placed_at_ctx(down_grad, 0).reshape(-1, model_width))
        view = placed_at_ctx(out_grad.reshape(heads, HD, model_width), 1)
        out_total = scattered(view.reshape(-1, model_width))
        views, widths = [(3, heads, HD), (1, heads, 1)], [3 * heads * HD, heads]
        qkv_total, beta_total = sum_columns(mixed_grad, views, widths)
    scale_one = lax.rsqrt(jnp.mean(tokens_in * tokens_in, -1, keepdims=True) + 1e-06)
    gain_one_term = jnp.sum(grad_normed_one * tokens_in * scale_one, 0)
    scaled_one = grad_normed_one * norm_gain1
    grad_tokens = (
        grad_middle
        + scale_one * scaled_one
        - scale_one
        * scale_one
        * scale_one
        * tokens_in
        * jnp.mean(scaled_one * tokens_in, -1, keepdims=True)
    ).astype(bf16)
    conv_term = placed_at_ctx(conv_term.reshape(KERNEL, 3, heads, HD), 3)
    small = jnp.concatenate([gain_one_term, gain_two_term, gain_rows[0], conv_term.reshape(-1)], 0)
    cuts = [model_width, 2 * model_width, 2 * model_width + HD]
    if direct():
        small = small + xor(small, "ctx", 1)
        size, lines, cols = small.shape[0], mixed_kept[0].shape[2], model_width // 4
        assert size <= n * lines * cols
        small = jnp.pad(small, (0, n * lines * cols - size)).reshape(n * lines, cols).astype(bf16)
        part = [jnp.concatenate([quarter(down_part, k), small], 0) for k in range(4)]
        down_got = [xor(part[k], "dp", k) for k in (1, 2, 3)]
        part, *got = after(part[0], *mixed_got, *down_got)
        mixed_got, down_got = got[:2], got[2:]
        part = summed_pairs(part, down_got).astype(bf16)
        down_mine, small = part[: -n * lines], part[-n * lines :]
        mixed_parts = sent_rows(mixed_kept, mixed_got, small.reshape(n, lines, cols))
        wide, down_mine, *mixed_parts = after(wide, down_mine, *mixed_parts)
        down_mine = down_to_owners(down_mine)
        mixed_got = [xor(mixed_parts[k], "fsdp", k) for k in (1, 2, 3)]
        wide = added_up(wide)
        feed_part = both_columns(wide)
        count = down_mine.shape[0] // lines
        each = pl.cdiv(count, n)
        down_part = jnp.pad(down_mine, ((0, (n * each - count) * lines), (0, 0)))
        down_part = jnp.transpose(down_part.reshape(n, each, lines, cols), (0, 2, 1, 3))
        down_part = down_part.reshape(n, lines, each * cols)
        wide = jnp.concatenate([feed_part, down_part], 2)
        wide = to_all(wide, "dp")
        mixed_mine, grad_tokens, *mixed_got = after(mixed_parts[0], grad_tokens, *mixed_got)
        total = summed_pairs(mixed_mine, mixed_got)
        strip, half = (3 * heads + 1) * HD, model_width // 2
        both = both_columns(total[..., :strip].astype(bf16))
        both = jnp.concatenate([both, total[..., -cols - half : -cols].astype(bf16)], 2)
        both = [both] + [xor(both, "dp", k) for k in (1, 2, 3)]
        small_total = total[..., -cols:].reshape(-1)[:size]
        short, rows = wide.shape[2], HD // (4 * n)
        moves = []
        for i in range(4):
            for j in range(n):
                lines = slice(i * short, (i + 1) * short)
                for k in range(2):
                    at = slice(k * ff_width, (k + 1) * ff_width)
                    to = (k * n + j) * ff_width
                    moves.append((0, (i, j, slice(None), at), 0, (lines, slice(to, to + ff_width))))
            first = 2 * ff_width
            for m in range(count):
                at = slice(first + (m % each) * cols, first + (m % each + 1) * cols)
                to = slice(m * short, (m + 1) * short), slice(i * cols, (i + 1) * cols)
                moves.append((0, (i, m // each, slice(None), at), 1, to))
        shapes = [(4 * short, 2 * n * ff_width), (down_mine.shape[0], 4 * cols)]
        gateup_total, down_total = finish([wide], moves, shapes, "wide_totals")
        moves = []
        for i in range(4):
            for j in range(n):
                for k in range(3 * heads):
                    at = (j, slice(None), slice(k * HD, (k + 1) * HD))
                    to = (k * n + j) * HD
                    moves.append((i, at, 0, (i, short, slice(to, to + HD))))
                at = (j, slice(None), slice(3 * heads * HD, strip))
                moves.append((i, at, 1, (i, short, slice(j * HD, (j + 1) * HD))))
                for k in range(2):
                    at = (j, slice(k * rows, (k + 1) * rows), slice(strip, None))
                    to = (i, rows, j * 4 * rows, slice(k * half, (k + 1) * half))
                    moves.append((i, at, 2, to))
        shapes = [(4 * short, 3 * heads_all * HD), (4 * short, n * HD)]
        shapes += [(4 * n * rows, model_width)]
        qkv_total, beta_total, out_total = finish(both, moves, shapes, "mixed_totals")
        beta_total = beta_total.reshape(4 * short, n, HD)[:, :, :heads]
        beta_total = jnp.transpose(beta_total, (0, 2, 1)).reshape(4 * short, heads_all)
    else:
        small_total = lax.psum(small, ("dp", "fsdp", "ctx"))
    gain_one, gain_two, gain_head, conv_total = jnp.split(small_total, cuts)
    return (
        output[None],
        grad_tokens[None],
        gain_one,
        qkv_total,
        beta_total,
        conv_total.reshape(conv_weight.shape),
        gain_head,
        out_total,
        gain_two,
        gateup_total,
        down_total,
    )


def solution(mesh):
    placed = (
        P(("dp", "fsdp"), "ctx", None),
        P(("dp", "fsdp")),
        P(("dp", "fsdp"), "ctx", None),
        P(),
        P("fsdp", None),
        P("fsdp", None),
        P(),
        P(),
        P("fsdp", None),
        P(),
        P("fsdp", None),
        P("fsdp", None),
    )
    return jax.shard_map(
        local,
        mesh=mesh,
        in_specs=placed,
        out_specs=(
            P(("dp", "fsdp"), "ctx", None),
            P(("dp", "fsdp"), "ctx", None),
            P(),
            P(("fsdp", "ctx"), None),
            P(("fsdp", "ctx"), None),
            P(),
            P(),
            P(("fsdp", "ctx"), None),
            P(),
            P(("fsdp", "ctx"), None),
            P(("fsdp", "ctx"), None),
        ),
        check_vma=False,
    )
```

```python
import functools
import jax, jax.numpy as jnp
from jax import lax
from jax.experimental import pallas as pl
from jax.experimental.pallas import tpu as pltpu
from jax.sharding import PartitionSpec as P

HD = 128
KERNEL = 4
CHUNK = 128
bf16 = jnp.bfloat16
f32 = jnp.float32

def dot(a, b):
    return jnp.dot(a, b, preferred_element_type=f32)

def dot_nt(a, b):
    return lax.dot_general(a, b, (((1,), (1,)), ((), ())), preferred_element_type=f32)

def dot_tn(a, b):
    return lax.dot_general(a, b, (((0,), (0,)), ((), ())), preferred_element_type=f32)

def halves(a):
    high = a.astype(bf16)
    return high, (a - high.astype(f32)).astype(bf16)

def fine_dot(a, b):
    n = b[0].shape[1]
    left = jnp.concatenate(a, 1)
    row = jnp.concatenate(b, 1)
    both = dot(left, jnp.concatenate([row, row], 0))
    return both[:, :n] + both[:, n:]

def unit_lower_inverses(lowers, size):
    rows = lax.broadcasted_iota(jnp.int32, (size, size), 0)
    cols = lax.broadcasted_iota(jnp.int32, (size, size), 1)
    eye = jnp.where(rows == cols, 1.0, 0.0)
    def joins(b):
        return (rows // (2 * b) == cols // (2 * b)) & ((rows // b) % 2 == 1) & ((cols // b) % 2 == 0)
    mask = joins(1)
    invs = [eye - jnp.where(mask, t, 0.0) for t in lowers]
    b = 2
    while b < size:
        mask = joins(b)
        parts = [halves(jnp.where(mask, t, 0.0)) for t in lowers]
        splits = [halves(t) for t in invs]
        inner = [halves(fine_dot(p, t)) for p, t in zip(parts, splits)]
        invs = [i - fine_dot(t, n) for i, t, n in zip(invs, splits, inner)]
        b *= 2
    return invs

def conv_rows(ref, weight, length):
    total = weight[0:1] * ref[pl.ds(5, length), :]
    for j in range(1, KERNEL):
        total = total + weight[j:j+1] * ref[pl.ds(5 + j, length), :]
    return total


def head_beta(logits, head, valid):
    lane = lax.broadcasted_iota(jnp.int32, logits.shape, 1)
    logit = jnp.sum(jnp.where(lane == head, logits, 0.0), -1, keepdims=True)
    return jnp.where(valid, jax.nn.sigmoid(logit), 0.0)


def mixer_forward_kernel(hb, nv_ref, pq, pk, pv, wq, wk, wv, bl, gain,
                         q_ref, k_ref, t_ref, e_ref, s_ref, o_ref, m_ref, ext):
    length = pq.shape[0]
    valid = lax.broadcasted_iota(jnp.int32, (length, 1), 0) < nv_ref[0]
    rows = lax.broadcasted_iota(jnp.int32, (CHUNK, CHUNK), 0)
    cols = lax.broadcasted_iota(jnp.int32, (CHUNK, CHUNK), 1)
    group = pl.program_id(0)
    acts = []
    for i, (p, w) in enumerate(((pq, wq), (pk, wk), (pv, wv))):
        ext[i, 0:8, :] = jnp.zeros((8, ext.shape[2]), f32)
        ext[i, 8:, :] = jnp.where(valid, p[...], 0.0)
        c = conv_rows(ext.at[i], w, length)
        acts.append(c * jax.nn.sigmoid(c))
    count = length // CHUNK
    spans = [slice(c * CHUNK, (c + 1) * CHUNK) for c in range(count)]
    heads = []
    for h in range(hb):
        lanes = slice(h * HD, (h + 1) * HD)
        a, b, v = (t[:, lanes] for t in acts)
        q = (a * (lax.rsqrt(jnp.sum(a * a, -1, keepdims=True) + 1e-6) * HD ** -0.5)).astype(bf16)
        k = (b * lax.rsqrt(jnp.sum(b * b, -1, keepdims=True) + 1e-6)).astype(bf16)
        beta = head_beta(bl[...], group * hb + h, valid)
        q_ref[:, lanes] = q
        k_ref[:, lanes] = k
        heads.append((q, k, (k.astype(f32) * beta).astype(bf16), (v * beta).astype(bf16)))
    cells = [(h, s) for h in range(hb) for s in spans]
    boths = [dot_nt(jnp.concatenate([heads[h][2][s], heads[h][0][s]], 0), heads[h][1][s]) for h, s in cells]
    invs = unit_lower_inverses([jnp.where(rows > cols, t[:CHUNK], 0.0) for t in boths], CHUNK)
    invs = [t.astype(bf16) for t in invs]
    blends = [dot(t, jnp.concatenate([heads[h][2][s], heads[h][3][s]], 1)) for t, (h, s) in zip(invs, cells)]
    states = [jnp.zeros((HD, HD), f32)] * hb
    for c, s in enumerate(spans):
        for h in range(hb):
            lanes = slice(h * HD, (h + 1) * HD)
            q, k = heads[h][:2]
            cell = h * count + c
            t_ref[h, c] = invs[cell]
            score = jnp.where(rows >= cols, boths[cell][CHUNK:], 0.0).astype(bf16)
            low = states[h].astype(bf16)
            s_ref[h, c] = low
            both = dot(jnp.concatenate([blends[cell][:, :HD].astype(bf16), q[s]], 0), low)
            err = (blends[cell][:, HD:] - both[:CHUNK]).astype(bf16)
            e_ref[s, lanes] = err
            states[h] = states[h] + dot_tn(k[s], err)
            out = both[CHUNK:] + dot(score, err)
            scale = lax.rsqrt(jnp.mean(out * out, -1, keepdims=True) + 1e-05)
            o_ref[s, lanes] = out.astype(bf16)
            m_ref[s, lanes] = (out * scale * gain[...]).astype(bf16)


def mixer_forward(projected, conv_w, gain, nv, heads):
    length = projected.shape[0]
    nc = length // CHUNK
    hb = 1
    groups = heads // hb
    w = hb * HD
    col = lambda off: (lambda i, *_: (0, i + off * groups))
    tok = pl.BlockSpec((length, w), lambda i, *_: (0, i))
    sq = pl.BlockSpec((hb, nc, HD, HD), lambda i, *_: (i, 0, 0, 0))
    in_specs = [pl.BlockSpec((length, w), col(o)) for o in range(3)]
    in_specs += [pl.BlockSpec((KERNEL, w), col(o)) for o in range(3)]
    in_specs += [pl.BlockSpec((length, HD), lambda i, *_: (0, 3 * heads)), pl.BlockSpec((1, HD), lambda i, *_: (0, 0))]
    flat = jax.ShapeDtypeStruct((length, heads * HD), bf16)
    square = jax.ShapeDtypeStruct((heads, nc, HD, HD), bf16)
    return pl.pallas_call(
        functools.partial(mixer_forward_kernel, hb),
        out_shape=(flat, flat, square, flat, square, flat, flat),
        grid_spec=pltpu.PrefetchScalarGridSpec(
            num_scalar_prefetch=1, grid=(groups,), in_specs=in_specs,
            out_specs=(tok, tok, sq, tok, sq, tok, tok),
            scratch_shapes=[pltpu.VMEM((3, length + 8, w), f32)]),
        name="mixer_forward",
    )(nv, projected, projected, projected, conv_w, conv_w, conv_w, projected, gain)


def mixer_backward_kernel(hb, heads_all, nv_ref, gm, o, q, k, t, e, s_c, bl, pq, pk, pv, wq, wk, wv, gain,
                          gp_ref, conv_ref, hg_ref, ext, gext):
    length = gm.shape[0]
    count = length // CHUNK
    group = pl.program_id(0)
    width = hb * HD
    valid = lax.broadcasted_iota(jnp.int32, (length, 1), 0) < nv_ref[0]
    rows = lax.broadcasted_iota(jnp.int32, (CHUNK, CHUNK), 0)
    cols = lax.broadcasted_iota(jnp.int32, (CHUNK, CHUNK), 1)
    spans = [slice(c * CHUNK, (c + 1) * CHUNK) for c in range(count)]
    logits_at = slice(3 * heads_all * HD, (3 * heads_all + 1) * HD)
    @pl.when(group == 0)
    def _():
        hg_ref[...] = jnp.zeros_like(hg_ref)
        rest = gp_ref.shape[1] - logits_at.start
        gp_ref[:, logits_at.start :] = jnp.zeros((length, rest), bf16)
    heads = []
    for h in range(hb):
        lanes = slice(h * HD, (h + 1) * HD)
        grad, out = gm[:, lanes].astype(f32), o[:, lanes].astype(f32)
        scale = lax.rsqrt(jnp.mean(out * out, -1, keepdims=True) + 1e-05)
        hg_ref[0:1, :] += jnp.sum(grad * out * scale, 0, keepdims=True)
        scaled = grad * gain[...]
        down = (scale * scaled - scale * scale * scale * out * jnp.mean(scaled * out, -1, keepdims=True)).astype(bf16)
        heads.append((q[:, lanes], k[:, lanes], down, head_beta(bl[...], group * hb + h, valid), e[:, lanes]))
    cells = [(h, c) for h in range(hb) for c in range(count)]
    scores = [jnp.where(rows >= cols, dot_nt(heads[h][0][spans[c]], heads[h][1][spans[c]]), 0.0).astype(bf16) for h, c in cells]
    errs = [dot_tn(m, heads[h][2][spans[c]]).astype(bf16) for m, (h, c) in zip(scores, cells)]
    firsts = [dot_tn(t[h, c], jnp.concatenate([r, heads[h][1][spans[c]]], 1)) for r, (h, c) in zip(errs, cells)]
    adds = [dot_tn(heads[h][0][spans[c]], heads[h][2][spans[c]]) for h, c in cells]
    states = [jnp.zeros((HD, HD), f32)] * hb
    backs, outs, gls = {}, {}, {}
    for c in reversed(range(count)):
        s = spans[c]
        for h in range(hb):
            cell = h * count + c
            low = states[h].astype(bf16)
            outs[h, c] = low
            full = firsts[cell][:, :HD] + dot(firsts[cell][:, HD:].astype(bf16), low)
            beta = heads[h][3][s]
            gls[h, c] = jnp.sum(full * heads[h][4][s].astype(f32), -1, keepdims=True) * (1.0 - beta)
            backs[h, c] = full * beta
            states[h] = states[h] + adds[cell] - dot_tn(heads[h][1][s], backs[h, c].astype(bf16))
    lane = lax.broadcasted_iota(jnp.int32, (length, HD), 1)
    total = jnp.zeros((length, HD), f32)
    grads = ([], [], [])
    for h in range(hb):
        gl = jnp.concatenate([gls[h, c] for c in range(count)], 0)
        total = jnp.where((lane == group * hb + h) & valid, gl, total)
        qh, kh, dh, _, err = heads[h]
        grads[2].append(jnp.concatenate([backs[h, c] for c in range(count)], 0))
        left = [jnp.concatenate([dh[s], (-backs[h, c]).astype(bf16)], 0) for c, s in enumerate(spans)]
        pairs = [dot_nt(p, err[s]) for p, s in zip(left, spans)]
        pairs = [jnp.concatenate([jnp.where(rows >= cols, p[:CHUNK], 0.0), jnp.where(rows > cols, p[CHUNK:], 0.0)], 0).astype(bf16) for p in pairs]
        first = [dot_nt(p, s_c[h, c]) for c, p in enumerate(left)]
        second = [dot(p, kh[s]) for p, s in zip(pairs, spans)]
        third = [dot_nt(err[s], outs[h, c]) for c, s in enumerate(spans)]
        fourth = [dot_tn(p, jnp.concatenate([qh[s], kh[s]], 0)) for p, s in zip(pairs, spans)]
        grads[0].append(jnp.concatenate([a[:CHUNK] + b[:CHUNK] for a, b in zip(first, second)], 0))
        grads[1].append(jnp.concatenate([a[CHUNK:] + b[CHUNK:] + x + y for a, b, x, y in zip(first, second, third, fourth)], 0))
    gp_ref[:, logits_at] = gp_ref[:, logits_at] + total.astype(bf16)
    for i, (p, w) in enumerate(((pq, wq), (pk, wk), (pv, wv))):
        ext[0:8, :] = jnp.zeros((8, width), f32)
        ext[8:, :] = jnp.where(valid, p[...], 0.0)
        pre = conv_rows(ext, w, length)
        sig = jax.nn.sigmoid(pre)
        pieces = []
        for h in range(hb):
            grad = grads[i][h]
            if i < 2:
                raw = (pre * sig)[:, h * HD:(h + 1) * HD]
                scale = lax.rsqrt(jnp.sum(raw * raw, -1, keepdims=True) + 1e-06)
                grad = scale * (grad - scale * scale * raw * jnp.sum(raw * grad, -1, keepdims=True))
                if i == 0:
                    grad = grad * HD ** -0.5
            pieces.append(grad)
        grad = jnp.concatenate(pieces, 1) if hb > 1 else pieces[0]
        grad = grad * sig * (1.0 + pre * (1.0 - sig))
        gext[0:length, :] = grad
        gext[length:, :] = jnp.zeros((8, width), f32)
        at = pl.ds(pl.multiple_of(i * heads_all * HD + group * width, HD), width)
        for j in range(KERNEL):
            conv_ref[j:j + 1, at] = jnp.sum(grad * ext[5 + j:5 + j + length, :], 0, keepdims=True)
        back = w[3:4] * grad
        for j in range(KERNEL - 1):
            back = back + w[j:j + 1] * gext[3 - j:3 - j + length, :]
        gp_ref[:, at] = jnp.where(valid, back, 0.0).astype(bf16)


def mixer_backward(gm, o, q, k, t, e, s_c, projected, conv_w, gain, nv):
    length = gm.shape[0]
    heads, nc = t.shape[:2]
    hb = 1
    groups = heads // hb
    w = hb * HD
    tok = pl.BlockSpec((length, w), lambda i, *_: (0, i))
    sq = pl.BlockSpec((hb, nc, HD, HD), lambda i, *_: (i, 0, 0, 0))
    col = lambda off: (lambda i, *_: (0, i + off * groups))
    fixed = lambda shape: pl.BlockSpec(shape, lambda i, *_: (0, 0))
    in_specs = [tok, tok, tok, tok, sq, tok, sq, pl.BlockSpec((length, HD), lambda i, *_: (0, 3 * heads))]
    in_specs += [pl.BlockSpec((length, w), col(n)) for n in range(3)]
    in_specs += [pl.BlockSpec((KERNEL, w), col(n)) for n in range(3)]
    in_specs += [fixed((1, HD))]
    wide = (length, pl.cdiv((3 * heads + 1) * HD, 256) * 256)
    return pl.pallas_call(
        functools.partial(mixer_backward_kernel, hb, heads),
        out_shape=(
            jax.ShapeDtypeStruct(wide, bf16),
            jax.ShapeDtypeStruct((KERNEL, 3 * heads * HD), f32),
            jax.ShapeDtypeStruct((8, HD), f32),
        ),
        grid_spec=pltpu.PrefetchScalarGridSpec(
            num_scalar_prefetch=1, grid=(groups,), in_specs=in_specs,
            out_specs=(fixed(wide), fixed((KERNEL, 3 * heads * HD)), fixed((8, HD))),
            scratch_shapes=[pltpu.VMEM((length + 8, w), f32), pltpu.VMEM((length + 8, w), f32)]),
        name="mixer_backward",
    )(nv, gm, o, q, k, t, e, s_c, projected, projected, projected, projected, conv_w, conv_w, conv_w, gain)


def xor(value, axis, step):
    return lax.ppermute(value, axis, [(i, i ^ step) for i in range(lax.axis_size(axis))])


def pick(tensor, index, axis=0):
    return lax.dynamic_index_in_dim(tensor, index, axis, keepdims=False)


def added(a, b):
    return (a.astype(f32) + b.astype(f32)).astype(bf16)


def direct():
    return (lax.axis_size("dp"), lax.axis_size("fsdp"), lax.axis_size("ctx")) == (4, 4, 2)


def mixer_columns(weight, heads):
    n = lax.axis_size("ctx")
    view = weight.reshape(weight.shape[0], 3, heads // n, n, HD)
    return pick(view, lax.axis_index("ctx"), 3).reshape(weight.shape[0], -1)


def beta_columns(weight, heads):
    n = lax.axis_size("ctx")
    view = weight.reshape(weight.shape[0], heads // n, n)
    return jnp.pad(pick(view, lax.axis_index("ctx"), 2), ((0, 0), (0, HD - heads // n)))


def feed_columns(weight):
    n = lax.axis_size("ctx")
    view = weight.reshape(weight.shape[0], 2, n, weight.shape[1] // (2 * n))
    return pick(view, lax.axis_index("ctx"), 2).reshape(weight.shape[0], -1)


def after(value, *others):
    return lax.optimization_barrier((value,) + others)


def start_pieces(tags, places, sources, outs, sems, z, d):
    copies = []
    for tag in tags:
        source, at_first, row_step, same, other = tag
        for at, index, row, col in places(tag, z ^ row_step, other if same else d ^ other):
            rows, width = (s.stop - s.start for s in at)
            target = outs[index].at[pl.ds(row, rows), pl.ds(col, width)]
            copy = pltpu.make_async_copy(
                sources[source].at[at_first + at], target, sems.at[len(copies)]
            )
            copy.start()
            copies.append(copy)
    return copies


def positions():
    return jnp.stack([lax.axis_index(a) for a in ("fsdp", "dp", "ctx")]).astype(jnp.int32)


def project_kernel(tags, places, count, where_ref, x_own, x_far, gain, *refs):
    sources = refs[:count]
    normed_ref, out_ref, full_ref, weight, sems, out_sem = refs[count:]
    step, steps = pl.program_id(0), pl.num_programs(0)
    z, d, c = where_ref[0], where_ref[1], where_ref[2]
    kept = pltpu.make_async_copy(weight, full_ref, out_sem)

    @pl.when(step == 0)
    def _():
        for copy in start_pieces(tags, places, sources, (weight,), sems, z, d):
            copy.wait()
        kept.start()

    x = jnp.where(step == c, x_own[...], x_far[...]).astype(f32)
    scale = lax.rsqrt(jnp.mean(x * x, -1, keepdims=True) + 1e-06)
    normed = (x * scale * gain[...]).astype(bf16)
    normed_ref[...] = normed
    out_ref[...] = dot(normed, weight[...])

    @pl.when(step == steps - 1)
    def _():
        kept.wait()


def project(x_own, x_far, gain, pieces, width):
    arrays, tags, places = pieces
    rows, depth = x_own.shape
    half = pl.BlockSpec((rows, depth), lambda i, *_: (0, 0))
    each = lambda w: pl.BlockSpec((rows, w), lambda i, *_: (i, 0))
    anywhere = pl.BlockSpec(memory_space=pl.ANY)
    return pl.pallas_call(
        functools.partial(project_kernel, tags, places, len(arrays)),
        out_shape=(
            jax.ShapeDtypeStruct((2 * rows, depth), bf16),
            jax.ShapeDtypeStruct((2 * rows, width), f32),
            jax.ShapeDtypeStruct((depth, width), bf16),
        ),
        grid_spec=pltpu.PrefetchScalarGridSpec(
            num_scalar_prefetch=1,
            grid=(2,),
            in_specs=[half, half, pl.BlockSpec((1, depth), lambda i, *_: (0, 0))]
            + [anywhere] * len(arrays),
            out_specs=(each(depth), each(width), anywhere),
            scratch_shapes=[
                pltpu.VMEM((depth, width), bf16),
                pltpu.SemaphoreType.DMA((len(tags),)),
                pltpu.SemaphoreType.DMA,
            ],
        ),
        name="projections",
    )(positions(), x_own, x_far, gain, *arrays)


def near_first(i, where):
    return ((where[2] + i) % 2, 0)


def attend_kernel(tags, places, count, where_ref, merged, *refs):
    sources = refs[:count]
    near, far, full_ref, weight, sems, out_sem = refs[count:]
    step, steps = pl.program_id(0), pl.num_programs(0)
    z, d = where_ref[0], where_ref[1]
    kept = pltpu.make_async_copy(weight, full_ref, out_sem)

    @pl.when(step == 0)
    def _():
        for copy in start_pieces(tags, places, sources, (weight,), sems, z, d):
            copy.wait()
        kept.start()

    total = dot(merged[...], weight[...])

    @pl.when(step == 0)
    def _():
        near[...] = total

    @pl.when(step == 1)
    def _():
        far[...] = total.astype(bf16)

    @pl.when(step == steps - 1)
    def _():
        kept.wait()


def near_spec(block, width):
    return pl.BlockSpec((block, width), lambda i, *_: (0, 0))


def far_spec(block, width):
    return pl.BlockSpec((block, width), lambda i, *_: (0, 0))


def attend(merged, pieces, width):
    arrays, tags, places = pieces
    rows, depth = merged.shape
    block = rows // 2
    anywhere = pl.BlockSpec(memory_space=pl.ANY)
    return pl.pallas_call(
        functools.partial(attend_kernel, tags, places, len(arrays)),
        out_shape=(
            jax.ShapeDtypeStruct((rows // 2, width), f32),
            jax.ShapeDtypeStruct((rows // 2, width), bf16),
            jax.ShapeDtypeStruct((depth, width), bf16),
        ),
        grid_spec=pltpu.PrefetchScalarGridSpec(
            num_scalar_prefetch=1,
            grid=(2,),
            in_specs=[pl.BlockSpec((block, depth), near_first)] + [anywhere] * len(arrays),
            out_specs=(near_spec(block, width), far_spec(block, width), anywhere),
            scratch_shapes=[
                pltpu.VMEM((depth, width), bf16),
                pltpu.SemaphoreType.DMA((2 * len(tags),)),
                pltpu.SemaphoreType.DMA,
            ],
        ),
        name="mixer_out",
    )(positions(), merged, *arrays)


def merged_grad_kernel(where_ref, own, far, weight, out):
    grad = jnp.where(pl.program_id(0) == 0, own[...], far[...])
    out[...] = dot_nt(grad, weight[...])


def merged_grad(own, far, weight):
    rows, width = own.shape
    depth = weight.shape[0]
    block = rows
    return pl.pallas_call(
        merged_grad_kernel,
        out_shape=jax.ShapeDtypeStruct((2 * rows, depth), f32),
        grid_spec=pltpu.PrefetchScalarGridSpec(
            num_scalar_prefetch=1,
            grid=(2,),
            in_specs=[
                near_spec(block, width),
                far_spec(block, width),
                pl.BlockSpec((depth, width), lambda i, *_: (0, 0)),
            ],
            out_specs=pl.BlockSpec((block, depth), near_first),
        ),
        name="merged_gradient",
    )(positions(), own, far, weight)


def normed_grad_kernel(where_ref, grad, weight, near, far):
    total = dot_nt(grad[...], weight[...])

    @pl.when(pl.program_id(0) == 0)
    def _():
        near[...] = total

    @pl.when(pl.program_id(0) == 1)
    def _():
        far[...] = total.astype(bf16)


def normed_grad(grad, weight):
    rows, (depth, width) = grad.shape[0], weight.shape
    block = rows // 2
    return pl.pallas_call(
        normed_grad_kernel,
        out_shape=(
            jax.ShapeDtypeStruct((rows // 2, depth), f32),
            jax.ShapeDtypeStruct((rows // 2, depth), bf16),
        ),
        grid_spec=pltpu.PrefetchScalarGridSpec(
            num_scalar_prefetch=1,
            grid=(2,),
            in_specs=[
                pl.BlockSpec((block, width), near_first),
                pl.BlockSpec((depth, width), lambda i, *_: (0, 0)),
            ],
            out_specs=(near_spec(block, depth), far_spec(block, depth)),
        ),
        name="normed_gradient",
    )(positions(), grad, weight)


def keep_and_send(total, where_ref, refs, col):
    low_keep, low_send, high_keep, high_send = refs
    first_low, first_high = where_ref[1] % 2 == 0, where_ref[1] // 2 == 0
    short = total.shape[0] // 32
    block = lambda i: total[i * short : (i + 1) * short]
    for z in range(2):
        for i in range(4):
            a, b = block(8 * z + 2 * i), block(8 * z + 2 * i + 1)
            low_keep[i % 2, z, i // 2, col, :] = jnp.where(first_low, a, b)
            low_send[i % 2, z, i // 2, col, :] = jnp.where(first_low, b, a)
            k = 16 + 8 * z + (i // 2) * 4 + i % 2
            a, b = block(k), block(k + 2)
            high_keep[i % 2, z, i // 2, col, :] = jnp.where(first_high, a, b)
            high_send[i % 2, z, i // 2, col, :] = jnp.where(first_high, b, a)


def weight_grad_kernel(parts, steps, where_ref, *refs):
    lefts, grad = refs[:parts], refs[parts]
    turned = refs[-1]
    step = pl.program_id(0)
    c = where_ref[2]

    @pl.when(step == 0)
    def _():
        at = 0
        for left in lefts:
            rows = left.shape[0]
            turned[:, at : at + rows] = left[...].T
            at += rows

    if len(refs) == parts + 6:
        every = slice(None)
        keep_and_send(dot(turned[...], grad[...]).astype(bf16), where_ref, refs[-5:-1], every)
        return

    merged, own, far = refs[parts + 1 : parts + 4]
    outs = refs[-5:-1]

    @pl.when(step < steps)
    def _():
        keep_and_send(dot(turned[...], grad[...]).astype(bf16), where_ref, outs, slice(None))

    @pl.when(step >= steps)
    def _():
        rows, half = own.shape[0], own.shape[1] // 2
        mine = merged[pl.ds(pl.multiple_of(c * rows, rows), rows), :]
        theirs = merged[pl.ds(pl.multiple_of((1 - c) * rows, rows), rows), :]
        width = outs[0].shape[-1]
        for k in range(2):
            at = pl.ds(pl.multiple_of(k * half + (step - steps) * width, width), width)
            part = (dot_tn(mine, own[:, at]) + dot_tn(theirs, far[:, at])).astype(bf16)
            lines = part.shape[0] // 32
            keep_and_send(part, where_ref, outs, slice(k * lines, (k + 1) * lines))


def weight_grad(lefts, grad, out=()):
    depth = lefts[0].shape[1]
    rows = sum(a.shape[0] for a in lefts)
    block = 256
    steps = pl.cdiv(grad.shape[1], block)
    more = out[1].shape[1] // 2 if out else 0
    shape = jax.ShapeDtypeStruct((2, 2, 2, depth // 32, grad.shape[1] + more), bf16)
    each = pl.BlockSpec((2, 2, 2, depth // 32, block), lambda i, *_: (0, 0, 0, 0, i))
    whole = lambda a: pl.BlockSpec(a.shape, lambda i, *_: (0, 0))
    specs = [whole(a) for a in lefts]
    specs += [pl.BlockSpec((rows, block), lambda i, *_: (0, jnp.minimum(i, steps - 1)))]
    specs += [whole(a) for a in out]
    return pl.pallas_call(
        functools.partial(weight_grad_kernel, len(lefts), steps),
        out_shape=(shape,) * 4,
        grid_spec=pltpu.PrefetchScalarGridSpec(
            num_scalar_prefetch=1,
            grid=(steps + more // block,),
            in_specs=specs,
            out_specs=(each,) * 4,
            scratch_shapes=[pltpu.VMEM((depth, rows), bf16)],
        ),
        name="weight_gradient",
    )(positions(), *lefts, grad, *out)


def down_grad_kernel(hidden, own, far, out, turned):
    rows = own.shape[0]

    @pl.when(pl.program_id(0) == 0)
    def _():
        turned[...] = hidden[...].T

    total = dot(turned[:, :rows], own[...]) + dot(turned[:, rows:], far[...])
    out[...] = total.astype(bf16)


def down_gradient(hidden, own, far):
    rows, width = own.shape
    half = hidden.shape[1]
    block = 256
    return pl.pallas_call(
        down_grad_kernel,
        out_shape=jax.ShapeDtypeStruct((half, width), bf16),
        grid=(width // block,),
        in_specs=[
            pl.BlockSpec((2 * rows, half), lambda i: (0, 0)),
            pl.BlockSpec((rows, block), lambda i: (0, i)),
            pl.BlockSpec((rows, block), lambda i: (0, i)),
        ],
        out_specs=pl.BlockSpec((half, block), lambda i: (0, i)),
        scratch_shapes=[pltpu.VMEM((half, 2 * rows), bf16)],
        name="down_gradient",
    )(hidden, own, far)


def whole_rows(weight):
    return lax.all_gather(weight, "fsdp", axis=0, tiled=True)


def exchange(blocks, axis):
    return lax.all_to_all(blocks, axis, 0, 0, tiled=True)


def to_all(piece, axis):
    return exchange(jnp.broadcast_to(piece, (lax.axis_size(axis),) + piece.shape), axis)


def bounds(total, step):
    return [slice(i, min(i + step, total)) for i in range(0, total, step)]


def feed_kernel(tags, places, count_down, own, where_ref, x_own, x_other, e_own, e_other, *refs):
    count = 1 + max(t[0] for t in tags)
    sources, downs = refs[:count], refs[count : count + count_down]
    hidden_ref, grad_ref, near_out, far_out, near_grad, far_grad = refs[count + count_down : -3]
    gateup, down, sems = refs[-3:]
    step = pl.program_id(0)
    z, d, c = where_ref[0], where_ref[1], where_ref[2]

    @pl.when(step == 0)
    def _():
        copies = start_pieces(tags, places, sources, (gateup,), sems, z, d)
        rows, cols = downs[1].shape[1:]
        for j in range(2):
            for source, at, first in ((downs[0], 2 * c + j, c), (downs[1], j, 1 - c)):
                col = pl.multiple_of(first * cols, HD)
                copy = pltpu.make_async_copy(
                    source.at[at],
                    down.at[pl.ds(j * rows, rows), pl.ds(col, cols)],
                    sems.at[len(copies)],
                )
                copy.start()
                copies.append(copy)
        for copy in copies:
            copy.wait()

    near = step < own
    x = jnp.where(near, x_own[...], x_other[...])
    e = jnp.where(near, e_own[...], e_other[...])
    half = down.shape[0]
    for j in bounds(half, 256):
        up_j = slice(half + j.start, half + j.stop)
        gate = dot(x, gateup[:, j])
        up = dot(x, gateup[:, up_j])
        grad = dot_nt(e, down[j, :])
        sig = jax.nn.sigmoid(gate)
        act = gate * sig
        hidden_ref[:, j] = (act * up).astype(bf16)
        grad_ref[:, j] = (grad * up * sig * (1.0 + gate * (1.0 - sig))).astype(bf16)
        grad_ref[:, up_j] = (grad * act).astype(bf16)
    out = dot(hidden_ref[...], down[...])
    back = dot_nt(grad_ref[...], gateup[...])

    @pl.when(near)
    def _():
        near_out[...] = out
        near_grad[...] = back

    @pl.when(jnp.logical_not(near))
    def _():
        far_out[...] = out.astype(bf16)
        far_grad[...] = back.astype(bf16)


def feed(x_own, x_other, e_own, e_other, wide, down):
    arrays, tags, places = wide
    rows, width = x_own.shape
    others = x_other.shape[0]
    half = 2 * down[1].shape[1]
    block = rows
    own, steps = rows // block, (rows + others) // block
    near = lambda w: pl.BlockSpec((block, w), lambda i, *_: (jnp.minimum(i, own - 1), 0))
    far = lambda w: pl.BlockSpec((block, w), lambda i, *_: (jnp.maximum(i - own, 0), 0))
    each = lambda w: pl.BlockSpec((block, w), lambda i, *_: (i, 0))
    anywhere = pl.BlockSpec(memory_space=pl.ANY)
    return pl.pallas_call(
        functools.partial(feed_kernel, tags, places, len(down), own),
        out_shape=(
            jax.ShapeDtypeStruct((rows + others, half), bf16),
            jax.ShapeDtypeStruct((rows + others, 2 * half), bf16),
            jax.ShapeDtypeStruct((rows, width), f32),
            jax.ShapeDtypeStruct((others, width), bf16),
            jax.ShapeDtypeStruct((rows, width), f32),
            jax.ShapeDtypeStruct((others, width), bf16),
        ),
        grid_spec=pltpu.PrefetchScalarGridSpec(
            num_scalar_prefetch=1,
            grid=(steps,),
            in_specs=[near(width), far(width), near(width), far(width)]
            + [anywhere] * (len(arrays) + len(down)),
            out_specs=(each(half), each(2 * half), near(width), far(width), near(width), far(width)),
            scratch_shapes=[
                pltpu.VMEM((width, 2 * half), bf16),
                pltpu.VMEM((half, width), bf16),
                pltpu.SemaphoreType.DMA((4 + len(tags),)),
            ],
        ),
        name="feed_forward",
    )(positions(), x_own, x_other, e_own, e_other, *arrays, *down)


def pack_kernel(heads, where_ref, qkv, beta, out, gateup, mixed_ref, wide_ref, every):
    rows = qkv.shape[0]
    strips = qkv.shape[1] // (2 * HD)
    mixed = (strips + 1) * HD
    width = gateup.shape[1] // 4
    half = out.shape[1] // 2
    short = out.shape[0]
    for c in range(2):

        @pl.when(where_ref[1] == c)
        def _():
            for i in range(strips):
                at = (2 * i + c) * HD
                mixed_ref[:, i * HD : (i + 1) * HD] = qkv[:, at : at + HD]
            source = lax.broadcasted_iota(jnp.int32, (heads, HD), 0)
            lane = lax.broadcasted_iota(jnp.int32, (heads, HD), 1)
            chosen = (source == 2 * lane + c).astype(f32).astype(bf16)
            every[...] = dot_tn(beta[...], chosen)
            here = pl.ds(pl.multiple_of(where_ref[0] * rows, rows), rows)
            mixed_ref[:, strips * HD : mixed] = every[here, :].astype(bf16)
            for i in range(2):
                at = (2 * i + c) * width
                wide_ref[0, :, i * width : (i + 1) * width] = gateup[:, at : at + width]

    wide_ref[0, :short, 2 * width :] = out[:, :half]
    wide_ref[0, short:, 2 * width :] = out[:, half:]
    for i in range(1, 4):
        wide_ref[i] = wide_ref[0]


def pack(w_qkv, w_beta, w_out, w_gateup):
    rows, short = w_qkv.shape[0] // 4, HD // 4
    heads = w_beta.shape[1]
    here = jnp.stack([lax.axis_index("dp"), lax.axis_index("ctx")]).astype(jnp.int32)
    mixed = w_qkv.shape[1] // 2 + HD
    wide = w_gateup.shape[1] // 2 + w_out.shape[1] // 2
    fixed = lambda *shape: pl.BlockSpec(shape, lambda i, *_: (0,) * len(shape))
    mine = lambda width: pl.BlockSpec((rows, width), lambda i, at: (at[0], 0))
    shapes = ((rows, mixed), (4, rows, wide))
    return pl.pallas_call(
        functools.partial(pack_kernel, heads),
        out_shape=tuple(jax.ShapeDtypeStruct(s, bf16) for s in shapes),
        grid_spec=pltpu.PrefetchScalarGridSpec(
            num_scalar_prefetch=1,
            grid=(1,),
            in_specs=[
                mine(w_qkv.shape[1]),
                pl.BlockSpec(w_beta.shape[::-1], lambda i, *_: (0, 0)),
                pl.BlockSpec((short, w_out.shape[1]), lambda i, at: (at[1] * 4 + at[0], 0)),
                mine(w_gateup.shape[1]),
            ],
            out_specs=tuple(fixed(*s) for s in shapes),
            scratch_shapes=[pltpu.VMEM((w_beta.shape[0], HD), f32)],
        ),
        name="weight_pieces",
    )(here, w_qkv, w_beta.T, w_out, w_gateup)


def gather_direct(mixed_piece, wide_piece, down_shard):
    z, c = lax.axis_index("fsdp"), lax.axis_index("ctx")
    own = [mixed_piece] + [xor(mixed_piece, "dp", k) for k in (1, 2, 3)]
    rows = [xor(mixed_piece, "fsdp", k) for k in (1, 2, 3)]
    wide_piece, *got = after(wide_piece, *own[1:], *rows)
    own[1:], rows = got[:3], got[3:]
    wide_own = [wide_piece[0]] + [xor(wide_piece[0], "dp", k) for k in (1, 2, 3)]
    wide_rows = exchange(wide_piece, "fsdp")
    rows, *wide_own[1:] = after(jnp.stack(rows), *wide_own[1:])
    rest = [rows] + [xor(rows, "dp", k) for k in (1, 2, 3)]
    half = down_shard.shape[1] // 2
    mine = lax.dynamic_slice_in_dim(down_shard, c * half, half, 1)
    tags = [(k, (), 0, False, k) for k in range(4)]
    tags += [(4 + i, (k - 1,), k, False, i) for i in range(4) for k in (1, 2, 3)]
    return own + rest, tags, wide_own, wide_rows, mine


def spread_first(own, wide_rows, mine):
    z = lax.axis_index("fsdp")
    half = wide_rows.shape[2] // 2
    low = jnp.stack([pick(wide_rows, z ^ k)[:, :half] for k in (1, 2, 3)])
    high = jnp.stack([pick(wide_rows, z ^ k)[:, half:] for k in (1, 2, 3)])
    low, high = [low, xor(low, "dp", 1)], [high, xor(high, "dp", 2)]
    mine, wide_rows = after(mine, wide_rows)
    return own, low, high, to_all(mine, "fsdp")


def spread_second(full, own, low, high):
    full, low[1], high[1] = after(full, low[1], high[1])
    low = low + [xor(low[0], "dp", 2), xor(low[1], "dp", 2)]
    high = [high[0], xor(high[0], "dp", 1), high[1], xor(high[1], "dp", 1)]
    tags = [(k, (), 0, False, k) for k in range(4)]
    tags += [(4 + i, (k - 1,), k, False, i) for i in range(4) for k in (1, 2, 3)]
    tags += [(8 + i, (k - 1,), k, False, i) for i in range(4) for k in (1, 2, 3)]
    return full, own + low + high, tags


def gather_weights(w_qkv, w_beta, w_out, w_gateup, w_down, heads):
    n, c = lax.axis_size("ctx"), lax.axis_index("ctx")
    if not direct():
        mixed = jnp.concatenate([mixer_columns(w_qkv, heads), beta_columns(w_beta, heads)], 1)
        out = whole_rows(w_out).reshape(heads // n, n, HD, -1)
        down = whole_rows(w_down)
        return (
            whole_rows(mixed),
            whole_rows(feed_columns(w_gateup)),
            pick(out, c, 1).reshape(-1, w_out.shape[1]),
            pick(down.reshape(n, -1, down.shape[1]), c),
        )
    rows, short = w_qkv.shape[0] // 4, HD // 4
    mixed_piece, wide_piece = pack(w_qkv, w_beta, w_out, w_gateup)
    mixed, width, half = mixed_piece.shape[1], w_gateup.shape[1] // 2, w_out.shape[1] // 2
    mixed_all, mixed_tags, own, wide_rows, mine = gather_direct(mixed_piece, wide_piece, w_down)
    cut = (width + half) // 2

    def mixed_places(tag, z, d):
        row = pl.multiple_of(z * (4 * rows) + d * rows, rows)
        return [((slice(0, rows), slice(0, mixed)), 0, row, 0)]

    def out_places(tag, z, d):
        row = pl.multiple_of(z * HD + d * short, short)
        first = width if tag[0] < 4 else width - cut
        at = slice(first, first + half)
        return [
            ((slice(0, short), at), 0, row, 0),
            ((slice(short, 2 * short), at), 0, row, half),
        ]

    def feed_places(tag, z, d):
        row = pl.multiple_of(z * (4 * rows) + d * rows, rows)
        if tag[0] < 4:
            at, col = slice(0, width), 0
        elif tag[0] < 8:
            at, col = slice(0, cut), 0
        else:
            at, col = slice(0, width - cut), cut
        return [((slice(0, rows), at), 0, row, col)]

    spread = spread_first(own, wide_rows, mine)

    def further(full):
        full, wide_all, wide_tags = spread_second(full, *spread[:3])
        out_tags = [t for t in wide_tags if not 4 <= t[0] < 8]
        wide = wide_all, wide_tags, feed_places
        return full, wide, (wide_all, out_tags, out_places), spread[3]

    return (mixed_all, mixed_tags, mixed_places), further


def feed_both(normed, grad_feed, gateup, down):
    if direct():
        normed_far, grad_far = xor(normed, "ctx", 1), xor(grad_feed, "ctx", 1)
        theirs = pick(down.reshape((2, 2) + down.shape[1:]), 1 - lax.axis_index("ctx"))
        down = [down, xor(theirs, "ctx", 1)]
        hidden, grad, out, out_far, back, back_far = feed(
            normed, normed_far, grad_feed, grad_far, gateup, down
        )
        out = out + xor(out_far, "ctx", 1).astype(f32)
        back = back + xor(back_far, "ctx", 1).astype(f32)
        return (normed, normed_far), (grad_feed, grad_far), hidden, grad, out, back
    normed, grad_feed = both_pieces(normed), both_pieces(grad_feed)
    gate_up = jnp.dot(normed, gateup, preferred_element_type=f32)
    ff_width = gate_up.shape[1] // 2
    gate_part = gate_up[:, :ff_width]
    up_part = gate_up[:, ff_width:]
    gate_sig = jax.nn.sigmoid(gate_part)
    hidden = (gate_part * gate_sig * up_part).astype(bf16)
    contract_cols = (((1,), (1,)), ((), ()))
    grad_hidden = lax.dot_general(grad_feed, down, contract_cols, preferred_element_type=f32)
    grad_gate = grad_hidden * up_part * gate_sig * (1.0 + gate_part * (1.0 - gate_sig))
    grad = jnp.concatenate([grad_gate, grad_hidden * gate_part * gate_sig], 1).astype(bf16)
    out = own_piece(jnp.dot(hidden, down, preferred_element_type=f32))
    back = own_piece(lax.dot_general(grad, gateup, contract_cols, preferred_element_type=f32))
    return normed, grad_feed, hidden, grad, out, back


def both_pieces(mine):
    n = lax.axis_size("ctx")
    if n != 2:
        return lax.all_gather(mine, "ctx", axis=0, tiled=True)
    other = xor(mine, "ctx", 1)
    first = lax.axis_index("ctx") == 0
    return jnp.concatenate([jnp.where(first, mine, other), jnp.where(first, other, mine)], 0)


def own_piece(partial):
    n = lax.axis_size("ctx")
    rows = partial.shape[0] // n
    if n != 2:
        return lax.psum_scatter(
            partial.astype(bf16), "ctx", scatter_dimension=0, tiled=True
        ).astype(f32)
    here = lax.axis_index("ctx")
    theirs = lax.dynamic_slice_in_dim(partial, (1 - here) * rows, rows, 0).astype(bf16)
    mine = lax.dynamic_slice_in_dim(partial, here * rows, rows, 0)
    return mine.astype(f32) + xor(theirs, "ctx", 1).astype(f32)


def replicas_first(part):
    d = lax.axis_index("dp")
    high, low = d // 2, d % 2
    a, b = part[:2], part[2:]
    got = xor(pick(a, 1 - low, 3), "dp", 1), xor(pick(b, 1 - high, 2), "dp", 2)
    return (pick(a, low, 3), pick(b, high, 2)), got


def halves_kernel(where_ref, *refs):
    for i in range(4):
        total = refs[2 * i][0].astype(f32) + refs[2 * i + 1][0].astype(f32)
        refs[8 + i][...] = total.astype(bf16)


def replicas_second(kept, got):
    shape = kept[0].shape[1:]
    block = (1, 1) + shape[1:]
    zeros = (0,) * (len(shape) - 1)
    high = lambda i, at: (at[1] // 2, i) + zeros
    not_high = lambda i, at: (1 - at[1] // 2, i) + zeros
    low = lambda i, at: (at[1] % 2, i) + zeros
    not_low = lambda i, at: (1 - at[1] % 2, i) + zeros
    specs, arrays = [], []
    for k, maps in ((0, (high, not_high)), (1, (low, not_low))):
        for chosen in maps:
            specs += [pl.BlockSpec(block, chosen)] * 2
            arrays += [kept[k], got[k]]
    outs = pl.pallas_call(
        halves_kernel,
        out_shape=(jax.ShapeDtypeStruct(shape, bf16),) * 4,
        grid_spec=pltpu.PrefetchScalarGridSpec(
            num_scalar_prefetch=1,
            grid=(2,),
            in_specs=specs,
            out_specs=(pl.BlockSpec((1,) + shape[1:], lambda i, *_: (i,) + zeros),) * 4,
        ),
        name="first_sums",
    )(positions(), *arrays)
    return (outs[0], outs[2]), (outs[1], outs[3])


def over_replicas(kept, got):
    return jnp.concatenate([added(kept[0], got[0]), added(kept[1], got[1])], 0)


def sent_kernel(where_ref, more, a_kept, a_got, b_kept, b_got, *outs):
    step = pl.program_id(0)
    a = a_kept[0].astype(f32) + a_got[0].astype(f32)
    b = b_kept[0].astype(f32) + b_got[0].astype(f32)
    total = jnp.where((where_ref[0] ^ step) < 2, a, b).astype(bf16)
    width = total.shape[2]
    for k in range(4):

        @pl.when(step == k)
        def _():
            outs[k][:, :, :width] = total
            outs[k][:, :, width:] = more[...]


def sent_rows(kept, got, more):
    shape = kept[0].shape[1:]
    zeros = (0,) * len(shape)
    a = pl.BlockSpec((1,) + shape, lambda i, at: (jnp.minimum(at[0] ^ i, 1),) + zeros)
    b = pl.BlockSpec((1,) + shape, lambda i, at: (jnp.maximum((at[0] ^ i) - 2, 0),) + zeros)
    wider = shape[:2] + (shape[2] + more.shape[2],)
    return pl.pallas_call(
        sent_kernel,
        out_shape=(jax.ShapeDtypeStruct(wider, bf16),) * 4,
        grid_spec=pltpu.PrefetchScalarGridSpec(
            num_scalar_prefetch=1,
            grid=(4,),
            in_specs=[pl.BlockSpec(more.shape, lambda i, *_: zeros), a, a, b, b],
            out_specs=(pl.BlockSpec(wider, lambda i, *_: zeros),) * 4,
        ),
        name="sums_sent",
    )(positions(), more, kept[0], got[0], kept[1], got[1])


def summed_pairs(own, got):
    own, *got = (part.astype(f32) for part in (own, *got))
    return (own + got[0]) + (got[1] + got[2])


def both_columns(part):
    c = lax.axis_index("ctx")
    other = xor(pick(part, 1 - c), "ctx", 1)
    mine = pick(part, c)
    first = c == 0
    return jnp.stack([jnp.where(first, mine, other), jnp.where(first, other, mine)])


def finish_kernel(moves, count, where_ref, *refs):
    sources, outs = refs[:count], refs[count:]
    d = where_ref[1]
    for source, at, index, to in moves:
        if len(to) == 4:
            row = pl.multiple_of((d ^ to[0]) * to[1] + to[2], to[1])
            to = (pl.ds(row, to[1]), to[3])
        elif len(to) == 3:
            if isinstance(to[0], int):
                to = (pl.ds(pl.multiple_of((d ^ to[0]) * to[1], to[1]), to[1]), to[2])
            else:
                to = (to[0], pl.ds(pl.multiple_of((d ^ to[1]) * to[2], HD), to[2]))
        outs[index][to] = sources[source][at].astype(f32)


def finish(sources, moves, shapes, name):
    whole = lambda shape: pl.BlockSpec(shape, lambda i, *_: (0,) * len(shape))
    return pl.pallas_call(
        functools.partial(finish_kernel, moves, len(sources)),
        out_shape=tuple(jax.ShapeDtypeStruct(s, f32) for s in shapes),
        grid_spec=pltpu.PrefetchScalarGridSpec(
            num_scalar_prefetch=1,
            grid=(1,),
            in_specs=[whole(s.shape) for s in sources],
            out_specs=tuple(whole(s) for s in shapes),
        ),
        name=name,
    )(positions(), *sources)


def blocks_of(grad, n, z):
    return grad.reshape(z, n, 2, 2, grad.shape[0] // (4 * z * n), grad.shape[1])


def scattered(full):
    share = lax.psum_scatter(full.astype(bf16), ("fsdp", "ctx"), scatter_dimension=0, tiled=True)
    return lax.psum(share, "dp").astype(f32)


def placed_at_ctx(part, axis):
    n = lax.axis_size("ctx")
    shape = [1] * (part.ndim + 1)
    shape[axis] = n
    here = (jnp.arange(n) == lax.axis_index("ctx")).reshape(shape)
    return jnp.where(here, jnp.expand_dims(part, axis), 0)


def sum_columns(grad, views, widths):
    outs, start = [], 0
    for shape, size in zip(views, widths):
        part = grad[:, start : start + size].reshape((grad.shape[0],) + shape)
        full = placed_at_ctx(part, part.ndim - 1)
        outs.append(scattered(full.reshape(grad.shape[0], -1)))
        start += size
    return outs


def added_up(parts):
    total = parts[0].astype(f32)
    for i in range(1, parts.shape[0]):
        total = total + parts[i].astype(f32)
    return total.astype(bf16)


def quarter(part, k):
    cols = part.shape[1] // 4
    return lax.dynamic_slice_in_dim(part, (lax.axis_index("dp") ^ k) * cols, cols, 1)


def down_to_owners(part):
    pairs = [(z * 2 + c, (2 * c + z // 2) * 2 + z % 2) for z in range(4) for c in range(2)]
    return lax.ppermute(part, ("fsdp", "ctx"), pairs)


def local(
    inputs,
    lengths,
    cotangent,
    norm_gain1,
    w_qkv,
    w_beta,
    conv_weight,
    head_gain,
    w_out,
    norm_gain2,
    w_gateup,
    w_down,
):
    n = lax.axis_size("ctx")
    heads_all = w_beta.shape[1]
    heads = heads_all // n
    tokens_in = inputs[0].astype(f32)
    piece_len, model_width = tokens_in.shape
    length = piece_len * n
    conv_mine = mixer_columns(conv_weight, heads_all)
    positions_here = jnp.arange(length, dtype=jnp.int32)
    start = lax.axis_index("ctx") * piece_len
    valid = ((start + positions_here[:piece_len]) < lengths[0]).astype(f32)[:, None]
    grad_feed = (cotangent[0].astype(f32) * valid).astype(bf16)
    if direct():
        pieces, further = gather_weights(w_qkv, w_beta, w_out, w_gateup, w_down, heads_all)
        far_rows = xor(inputs[0], "ctx", 1)
        normed_one, projected, mixed = project(
            inputs[0], far_rows, norm_gain1[None], pieces, (3 * heads + 1) * HD
        )
        projected, gateup, out, down = further(projected)
    else:
        mixed, gateup, out, down = gather_weights(
            w_qkv, w_beta, w_out, w_gateup, w_down, heads_all
        )
        tokens_all = both_pieces(inputs[0]).astype(f32)
        scale_all = lax.rsqrt(jnp.mean(tokens_all * tokens_all, -1, keepdims=True) + 1e-06)
        normed_one = (tokens_all * scale_all * norm_gain1).astype(bf16)
        projected = jnp.dot(normed_one, mixed, preferred_element_type=f32)
    queries, keys, inverse, errors, states, heads_out, merged = mixer_forward(
        projected, conv_mine, head_gain[None], lengths, heads
    )
    if direct():
        near, far, out = attend(merged, out, model_width)
        attention = near + xor(far, "ctx", 1).astype(f32)
    else:
        attention = own_piece(jnp.dot(merged, out, preferred_element_type=f32))
    middle = tokens_in + attention
    scale_two = lax.rsqrt(jnp.mean(middle * middle, -1, keepdims=True) + 1e-06)
    normed_two = (middle * scale_two * norm_gain2).astype(bf16)
    normed_two, feed_all, hidden, grad_gate_up, feed_out, grad_normed_two = feed_both(
        normed_two, grad_feed, gateup, down
    )
    output = (middle + feed_out).astype(bf16)
    contract_cols = (((1,), (1,)), ((), ()))
    contract_rows = (((0,), (0,)), ((), ()))
    ff_width = hidden.shape[1]
    if direct():
        down_grad = down_gradient(hidden, *feed_all)
        grad_gate_up, down_grad = after(grad_gate_up, down_grad)
        down_got = exchange(down_grad.reshape(4, down_grad.shape[0] // 4, -1), "fsdp")
        low_kept, low_sent, high_kept, high_sent = weight_grad(normed_two, grad_gate_up)
        wide_kept = low_kept, high_kept
        wide_got = xor(low_sent, "dp", 1), xor(high_sent, "dp", 2)
        grad_normed_two, low_sent = after(grad_normed_two, low_sent)
    else:
        down_grad = lax.dot_general(
            hidden, feed_all, contract_rows, preferred_element_type=f32
        ).astype(bf16)
        gateup_grad = lax.dot_general(
            normed_two, grad_gate_up, contract_rows, preferred_element_type=f32
        ).astype(bf16)
    gain_two_term = jnp.sum(grad_normed_two * middle * scale_two, 0)
    scaled_two = grad_normed_two * norm_gain2
    grad_middle = (
        grad_feed.astype(f32)
        + scale_two * scaled_two
        - scale_two
        * scale_two
        * scale_two
        * middle
        * jnp.mean(scaled_two * middle, -1, keepdims=True)
    )
    grad_attention = grad_middle.astype(bf16)
    if direct():
        grad_far = xor(grad_attention, "ctx", 1)
        grad_merged = merged_grad(grad_attention, grad_far, out)
    else:
        grad_attention = both_pieces(grad_attention)
        out_grad = lax.dot_general(
            merged, grad_attention, contract_rows, preferred_element_type=f32
        ).astype(bf16)
        grad_merged = lax.dot_general(
            grad_attention, out, contract_cols, preferred_element_type=f32
        )
    grad_mixed, conv_term, gain_rows = mixer_backward(
        grad_merged, heads_out, queries, keys, inverse, errors, states,
        projected, conv_mine, head_gain[None], lengths,
    )
    if direct():
        grad_mixed, *wide_got = after(grad_mixed, *wide_got)
        wide_kept, wide_sent = replicas_second(wide_kept, wide_got)
        grad_mixed, *wide_sent = after(grad_mixed, *wide_sent)
        wide_got = xor(wide_sent[0], "dp", 2), xor(wide_sent[1], "dp", 1)
        low_kept, low_sent, high_kept, high_sent = weight_grad(
            (normed_one,), grad_mixed, (merged, grad_attention, grad_far)
        )
        mixed_kept = low_kept, high_kept
        mixed_got = xor(low_sent, "dp", 1), xor(high_sent, "dp", 2)
        grad_mixed, low_kept = after(grad_mixed, mixed_kept[0])
        mixed_kept = low_kept, mixed_kept[1]
        near, far = normed_grad(grad_mixed, mixed)
        near, far, down_got, *wide_got = after(near, far, down_got, *wide_got)
        wide = exchange(over_replicas(wide_kept, wide_got), "fsdp")
        down_part = added_up(down_got)
        near, *mixed_got = after(near, *mixed_got)
        grad_normed_one = near + xor(far, "ctx", 1).astype(f32)
        mixed_kept, mixed_sent = replicas_second(mixed_kept, mixed_got)
        mixed_got = xor(mixed_sent[0], "dp", 2), xor(mixed_sent[1], "dp", 1)
    else:
        mixed_grad = lax.dot_general(
            normed_one, grad_mixed, contract_rows, preferred_element_type=f32
        ).astype(bf16)
        grad_normed_one = own_piece(
            lax.dot_general(grad_mixed, mixed, contract_cols, preferred_element_type=f32)
        )
        (gateup_total,) = sum_columns(gateup_grad, [(2, ff_width)], [2 * ff_width])
        down_total = scattered(placed_at_ctx(down_grad, 0).reshape(-1, model_width))
        view = placed_at_ctx(out_grad.reshape(heads, HD, model_width), 1)
        out_total = scattered(view.reshape(-1, model_width))
        views, widths = [(3, heads, HD), (1, heads, 1)], [3 * heads * HD, heads]
        qkv_total, beta_total = sum_columns(mixed_grad, views, widths)
    scale_one = lax.rsqrt(jnp.mean(tokens_in * tokens_in, -1, keepdims=True) + 1e-06)
    gain_one_term = jnp.sum(grad_normed_one * tokens_in * scale_one, 0)

    def input_gradient(grad_normed_one):
        scaled_one = grad_normed_one * norm_gain1
        total = (
            grad_middle
            + scale_one * scaled_one
            - scale_one
            * scale_one
            * scale_one
            * tokens_in
            * jnp.mean(scaled_one * tokens_in, -1, keepdims=True)
        )
        return total.astype(bf16)

    conv_term = placed_at_ctx(conv_term.reshape(KERNEL, 3, heads, HD), 3)
    small = jnp.concatenate([gain_one_term, gain_two_term, gain_rows[0], conv_term.reshape(-1)], 0)
    cuts = [model_width, 2 * model_width, 2 * model_width + HD]
    if direct():
        small = small + xor(small, "ctx", 1)
        size, lines, cols = small.shape[0], mixed_kept[0].shape[2], model_width // 4
        assert size <= n * lines * cols
        small = jnp.pad(small, (0, n * lines * cols - size)).reshape(n * lines, cols).astype(bf16)
        part = [jnp.concatenate([quarter(down_part, k), small], 0) for k in range(4)]
        down_got = [xor(part[k], "dp", k) for k in (1, 2, 3)]
        part, *got = after(part[0], *mixed_got, *down_got)
        mixed_got, down_got = got[:2], got[2:]
        part = summed_pairs(part, down_got).astype(bf16)
        down_mine, small = part[: -n * lines], part[-n * lines :]
        mixed_parts = sent_rows(mixed_kept, mixed_got, small.reshape(n, lines, cols))
        wide, down_mine, *mixed_parts = after(wide, down_mine, *mixed_parts)
        down_mine = down_to_owners(down_mine)
        mixed_got = [xor(mixed_parts[k], "fsdp", k) for k in (1, 2, 3)]
        wide = added_up(wide)
        feed_part = both_columns(wide)
        count = down_mine.shape[0] // lines
        each = pl.cdiv(count, n)
        down_part = jnp.pad(down_mine, ((0, (n * each - count) * lines), (0, 0)))
        down_part = jnp.transpose(down_part.reshape(n, each, lines, cols), (0, 2, 1, 3))
        down_part = down_part.reshape(n, lines, each * cols)
        wide = jnp.concatenate([feed_part, down_part], 2)
        wide = to_all(wide, "dp")
        ready = after(mixed_parts[0], grad_normed_one, *mixed_got)
        mixed_mine, grad_normed_one, *mixed_got = ready
        grad_tokens = input_gradient(grad_normed_one)
        total = summed_pairs(mixed_mine, mixed_got)
        strip, half = (3 * heads + 1) * HD, model_width // 2
        both = both_columns(total[..., :strip].astype(bf16))
        both = jnp.concatenate([both, total[..., -cols - half : -cols].astype(bf16)], 2)
        both = [both] + [xor(both, "dp", k) for k in (1, 2, 3)]
        small_total = total[..., -cols:].reshape(-1)[:size]
        short, rows = wide.shape[2], HD // (4 * n)
        moves = []
        for i in range(4):
            for j in range(n):
                lines = slice(i * short, (i + 1) * short)
                for k in range(2):
                    at = slice(k * ff_width, (k + 1) * ff_width)
                    to = (k * n + j) * ff_width
                    moves.append((0, (i, j, slice(None), at), 0, (lines, slice(to, to + ff_width))))
            first = 2 * ff_width
            for m in range(count):
                at = slice(first + (m % each) * cols, first + (m % each + 1) * cols)
                to = slice(m * short, (m + 1) * short), slice(i * cols, (i + 1) * cols)
                moves.append((0, (i, m // each, slice(None), at), 1, to))
        shapes = [(4 * short, 2 * n * ff_width), (down_mine.shape[0], 4 * cols)]
        gateup_total, down_total = finish([wide], moves, shapes, "wide_totals")
        ready = after(both[0], *both[1:], gateup_total, down_total)
        both, (gateup_total, down_total) = list(ready[:4]), ready[4:]
        moves = []
        for i in range(4):
            for j in range(n):
                for k in range(3 * heads):
                    at = (j, slice(None), slice(k * HD, (k + 1) * HD))
                    to = (k * n + j) * HD
                    moves.append((i, at, 0, (i, short, slice(to, to + HD))))
                at = (j, slice(None), slice(3 * heads * HD, strip))
                moves.append((i, at, 1, (i, short, slice(j * HD, (j + 1) * HD))))
                for k in range(2):
                    at = (j, slice(k * rows, (k + 1) * rows), slice(strip, None))
                    to = (i, rows, j * 4 * rows, slice(k * half, (k + 1) * half))
                    moves.append((i, at, 2, to))
        shapes = [(4 * short, 3 * heads_all * HD), (4 * short, n * HD)]
        shapes += [(4 * n * rows, model_width)]
        qkv_total, beta_total, out_total = finish(both, moves, shapes, "mixed_totals")
        beta_total = beta_total.reshape(4 * short, n, HD)[:, :, :heads]
        beta_total = jnp.transpose(beta_total, (0, 2, 1)).reshape(4 * short, heads_all)
    else:
        small_total = lax.psum(small, ("dp", "fsdp", "ctx"))
        grad_tokens = input_gradient(grad_normed_one)
    gain_one, gain_two, gain_head, conv_total = jnp.split(small_total, cuts)
    return (
        output[None],
        grad_tokens[None],
        gain_one,
        qkv_total,
        beta_total,
        conv_total.reshape(conv_weight.shape),
        gain_head,
        out_total,
        gain_two,
        gateup_total,
        down_total,
    )


def solution(mesh):
    placed = (
        P(("dp", "fsdp"), "ctx", None),
        P(("dp", "fsdp")),
        P(("dp", "fsdp"), "ctx", None),
        P(),
        P("fsdp", None),
        P("fsdp", None),
        P(),
        P(),
        P("fsdp", None),
        P(),
        P("fsdp", None),
        P("fsdp", None),
    )
    return jax.shard_map(
        local,
        mesh=mesh,
        in_specs=placed,
        out_specs=(
            P(("dp", "fsdp"), "ctx", None),
            P(("dp", "fsdp"), "ctx", None),
            P(),
            P(("fsdp", "ctx"), None),
            P(("fsdp", "ctx"), None),
            P(),
            P(),
            P(("fsdp", "ctx"), None),
            P(),
            P(("fsdp", "ctx"), None),
            P(("fsdp", "ctx"), None),
        ),
        check_vma=False,
    )
```

```python
import functools
import jax, jax.numpy as jnp
from jax import lax
from jax.experimental import pallas as pl
from jax.experimental.pallas import tpu as pltpu
from jax.sharding import PartitionSpec as P

HD = 128
KERNEL = 4
CHUNK = 128
bf16 = jnp.bfloat16
f32 = jnp.float32

def dot(a, b):
    return jnp.dot(a, b, preferred_element_type=f32)

def dot_nt(a, b):
    return lax.dot_general(a, b, (((1,), (1,)), ((), ())), preferred_element_type=f32)

def dot_tn(a, b):
    return lax.dot_general(a, b, (((0,), (0,)), ((), ())), preferred_element_type=f32)

def halves(a):
    high = a.astype(bf16)
    return high, (a - high.astype(f32)).astype(bf16)

def fine_dot(a, b):
    n = b[0].shape[1]
    left = jnp.concatenate(a, 1)
    row = jnp.concatenate(b, 1)
    both = dot(left, jnp.concatenate([row, row], 0))
    return both[:, :n] + both[:, n:]

def unit_lower_inverses(lowers, size):
    rows = lax.broadcasted_iota(jnp.int32, (size, size), 0)
    cols = lax.broadcasted_iota(jnp.int32, (size, size), 1)
    eye = jnp.where(rows == cols, 1.0, 0.0)
    def joins(b):
        return (rows // (2 * b) == cols // (2 * b)) & ((rows // b) % 2 == 1) & ((cols // b) % 2 == 0)
    mask = joins(1)
    invs = [eye - jnp.where(mask, t, 0.0) for t in lowers]
    b = 2
    while b < size:
        mask = joins(b)
        parts = [halves(jnp.where(mask, t, 0.0)) for t in lowers]
        splits = [halves(t) for t in invs]
        inner = [halves(fine_dot(p, t)) for p, t in zip(parts, splits)]
        invs = [i - fine_dot(t, n) for i, t, n in zip(invs, splits, inner)]
        b *= 2
    return invs

def conv_rows(ref, weight, length):
    total = weight[0:1] * ref[pl.ds(5, length), :]
    for j in range(1, KERNEL):
        total = total + weight[j:j+1] * ref[pl.ds(5 + j, length), :]
    return total


def head_beta(logits, head, valid):
    lane = lax.broadcasted_iota(jnp.int32, logits.shape, 1)
    logit = jnp.sum(jnp.where(lane == head, logits, 0.0), -1, keepdims=True)
    return jnp.where(valid, jax.nn.sigmoid(logit), 0.0)


def mixer_forward_kernel(hb, nv_ref, pq, pk, pv, wq, wk, wv, bl, gain,
                         q_ref, k_ref, t_ref, e_ref, s_ref, o_ref, m_ref, ext):
    length = pq.shape[0]
    valid = lax.broadcasted_iota(jnp.int32, (length, 1), 0) < nv_ref[0]
    rows = lax.broadcasted_iota(jnp.int32, (CHUNK, CHUNK), 0)
    cols = lax.broadcasted_iota(jnp.int32, (CHUNK, CHUNK), 1)
    group = pl.program_id(0)
    acts = []
    for i, (p, w) in enumerate(((pq, wq), (pk, wk), (pv, wv))):
        ext[i, 0:8, :] = jnp.zeros((8, ext.shape[2]), f32)
        ext[i, 8:, :] = jnp.where(valid, p[...], 0.0)
        c = conv_rows(ext.at[i], w, length)
        acts.append(c * jax.nn.sigmoid(c))
    count = length // CHUNK
    spans = [slice(c * CHUNK, (c + 1) * CHUNK) for c in range(count)]
    heads = []
    for h in range(hb):
        lanes = slice(h * HD, (h + 1) * HD)
        a, b, v = (t[:, lanes] for t in acts)
        q = (a * (lax.rsqrt(jnp.sum(a * a, -1, keepdims=True) + 1e-6) * HD ** -0.5)).astype(bf16)
        k = (b * lax.rsqrt(jnp.sum(b * b, -1, keepdims=True) + 1e-6)).astype(bf16)
        beta = head_beta(bl[...], group * hb + h, valid)
        q_ref[:, lanes] = q
        k_ref[:, lanes] = k
        heads.append((q, k, (k.astype(f32) * beta).astype(bf16), (v * beta).astype(bf16)))
    cells = [(h, s) for h in range(hb) for s in spans]
    boths = [dot_nt(jnp.concatenate([heads[h][2][s], heads[h][0][s]], 0), heads[h][1][s]) for h, s in cells]
    invs = unit_lower_inverses([jnp.where(rows > cols, t[:CHUNK], 0.0) for t in boths], CHUNK)
    invs = [t.astype(bf16) for t in invs]
    blends = [dot(t, jnp.concatenate([heads[h][2][s], heads[h][3][s]], 1)) for t, (h, s) in zip(invs, cells)]
    states = [jnp.zeros((HD, HD), f32)] * hb
    for c, s in enumerate(spans):
        for h in range(hb):
            lanes = slice(h * HD, (h + 1) * HD)
            q, k = heads[h][:2]
            cell = h * count + c
            t_ref[h, c] = invs[cell]
            score = jnp.where(rows >= cols, boths[cell][CHUNK:], 0.0).astype(bf16)
            low = states[h].astype(bf16)
            s_ref[h, c] = low
            both = dot(jnp.concatenate([blends[cell][:, :HD].astype(bf16), q[s]], 0), low)
            err = (blends[cell][:, HD:] - both[:CHUNK]).astype(bf16)
            e_ref[s, lanes] = err
            states[h] = states[h] + dot_tn(k[s], err)
            out = both[CHUNK:] + dot(score, err)
            scale = lax.rsqrt(jnp.mean(out * out, -1, keepdims=True) + 1e-05)
            o_ref[s, lanes] = out.astype(bf16)
            m_ref[s, lanes] = (out * scale * gain[...]).astype(bf16)


def mixer_forward(projected, conv_w, gain, nv, heads):
    length = projected.shape[0]
    nc = length // CHUNK
    hb = 1
    groups = heads // hb
    w = hb * HD
    col = lambda off: (lambda i, *_: (0, i + off * groups))
    tok = pl.BlockSpec((length, w), lambda i, *_: (0, i))
    sq = pl.BlockSpec((hb, nc, HD, HD), lambda i, *_: (i, 0, 0, 0))
    in_specs = [pl.BlockSpec((length, w), col(o)) for o in range(3)]
    in_specs += [pl.BlockSpec((KERNEL, w), col(o)) for o in range(3)]
    in_specs += [pl.BlockSpec((length, HD), lambda i, *_: (0, 3 * heads)), pl.BlockSpec((1, HD), lambda i, *_: (0, 0))]
    flat = jax.ShapeDtypeStruct((length, heads * HD), bf16)
    square = jax.ShapeDtypeStruct((heads, nc, HD, HD), bf16)
    return pl.pallas_call(
        functools.partial(mixer_forward_kernel, hb),
        out_shape=(flat, flat, square, flat, square, flat, flat),
        grid_spec=pltpu.PrefetchScalarGridSpec(
            num_scalar_prefetch=1, grid=(groups,), in_specs=in_specs,
            out_specs=(tok, tok, sq, tok, sq, tok, tok),
            scratch_shapes=[pltpu.VMEM((3, length + 8, w), f32)]),
        name="mixer_forward",
    )(nv, projected, projected, projected, conv_w, conv_w, conv_w, projected, gain)


def mixer_backward_kernel(hb, heads_all, nv_ref, gm, o, q, k, t, e, s_c, bl, pq, pk, pv, wq, wk, wv, gain,
                          gp_ref, conv_ref, hg_ref, ext, gext):
    length = gm.shape[0]
    count = length // CHUNK
    group = pl.program_id(0)
    width = hb * HD
    valid = lax.broadcasted_iota(jnp.int32, (length, 1), 0) < nv_ref[0]
    rows = lax.broadcasted_iota(jnp.int32, (CHUNK, CHUNK), 0)
    cols = lax.broadcasted_iota(jnp.int32, (CHUNK, CHUNK), 1)
    spans = [slice(c * CHUNK, (c + 1) * CHUNK) for c in range(count)]
    logits_at = slice(3 * heads_all * HD, (3 * heads_all + 1) * HD)
    @pl.when(group == 0)
    def _():
        hg_ref[...] = jnp.zeros_like(hg_ref)
        rest = gp_ref.shape[1] - logits_at.start
        gp_ref[:, logits_at.start :] = jnp.zeros((length, rest), bf16)
    heads = []
    for h in range(hb):
        lanes = slice(h * HD, (h + 1) * HD)
        grad, out = gm[:, lanes].astype(f32), o[:, lanes].astype(f32)
        scale = lax.rsqrt(jnp.mean(out * out, -1, keepdims=True) + 1e-05)
        hg_ref[0:1, :] += jnp.sum(grad * out * scale, 0, keepdims=True)
        scaled = grad * gain[...]
        down = (scale * scaled - scale * scale * scale * out * jnp.mean(scaled * out, -1, keepdims=True)).astype(bf16)
        heads.append((q[:, lanes], k[:, lanes], down, head_beta(bl[...], group * hb + h, valid), e[:, lanes]))
    cells = [(h, c) for h in range(hb) for c in range(count)]
    scores = [jnp.where(rows >= cols, dot_nt(heads[h][0][spans[c]], heads[h][1][spans[c]]), 0.0).astype(bf16) for h, c in cells]
    errs = [dot_tn(m, heads[h][2][spans[c]]).astype(bf16) for m, (h, c) in zip(scores, cells)]
    firsts = [dot_tn(t[h, c], jnp.concatenate([r, heads[h][1][spans[c]]], 1)) for r, (h, c) in zip(errs, cells)]
    adds = [dot_tn(heads[h][0][spans[c]], heads[h][2][spans[c]]) for h, c in cells]
    states = [jnp.zeros((HD, HD), f32)] * hb
    backs, outs, gls = {}, {}, {}
    for c in reversed(range(count)):
        s = spans[c]
        for h in range(hb):
            cell = h * count + c
            low = states[h].astype(bf16)
            outs[h, c] = low
            full = firsts[cell][:, :HD] + dot(firsts[cell][:, HD:].astype(bf16), low)
            beta = heads[h][3][s]
            gls[h, c] = jnp.sum(full * heads[h][4][s].astype(f32), -1, keepdims=True) * (1.0 - beta)
            backs[h, c] = full * beta
            states[h] = states[h] + adds[cell] - dot_tn(heads[h][1][s], backs[h, c].astype(bf16))
    lane = lax.broadcasted_iota(jnp.int32, (length, HD), 1)
    total = jnp.zeros((length, HD), f32)
    grads = ([], [], [])
    for h in range(hb):
        gl = jnp.concatenate([gls[h, c] for c in range(count)], 0)
        total = jnp.where((lane == group * hb + h) & valid, gl, total)
        qh, kh, dh, _, err = heads[h]
        grads[2].append(jnp.concatenate([backs[h, c] for c in range(count)], 0))
        left = [jnp.concatenate([dh[s], (-backs[h, c]).astype(bf16)], 0) for c, s in enumerate(spans)]
        pairs = [dot_nt(p, err[s]) for p, s in zip(left, spans)]
        pairs = [jnp.concatenate([jnp.where(rows >= cols, p[:CHUNK], 0.0), jnp.where(rows > cols, p[CHUNK:], 0.0)], 0).astype(bf16) for p in pairs]
        first = [dot_nt(p, s_c[h, c]) for c, p in enumerate(left)]
        second = [dot(p, kh[s]) for p, s in zip(pairs, spans)]
        third = [dot_nt(err[s], outs[h, c]) for c, s in enumerate(spans)]
        fourth = [dot_tn(p, jnp.concatenate([qh[s], kh[s]], 0)) for p, s in zip(pairs, spans)]
        grads[0].append(jnp.concatenate([a[:CHUNK] + b[:CHUNK] for a, b in zip(first, second)], 0))
        grads[1].append(jnp.concatenate([a[CHUNK:] + b[CHUNK:] + x + y for a, b, x, y in zip(first, second, third, fourth)], 0))
    gp_ref[:, logits_at] = gp_ref[:, logits_at] + total.astype(bf16)
    for i, (p, w) in enumerate(((pq, wq), (pk, wk), (pv, wv))):
        ext[0:8, :] = jnp.zeros((8, width), f32)
        ext[8:, :] = jnp.where(valid, p[...], 0.0)
        pre = conv_rows(ext, w, length)
        sig = jax.nn.sigmoid(pre)
        pieces = []
        for h in range(hb):
            grad = grads[i][h]
            if i < 2:
                raw = (pre * sig)[:, h * HD:(h + 1) * HD]
                scale = lax.rsqrt(jnp.sum(raw * raw, -1, keepdims=True) + 1e-06)
                grad = scale * (grad - scale * scale * raw * jnp.sum(raw * grad, -1, keepdims=True))
                if i == 0:
                    grad = grad * HD ** -0.5
            pieces.append(grad)
        grad = jnp.concatenate(pieces, 1) if hb > 1 else pieces[0]
        grad = grad * sig * (1.0 + pre * (1.0 - sig))
        gext[0:length, :] = grad
        gext[length:, :] = jnp.zeros((8, width), f32)
        at = pl.ds(pl.multiple_of(i * heads_all * HD + group * width, HD), width)
        for j in range(KERNEL):
            conv_ref[j:j + 1, at] = jnp.sum(grad * ext[5 + j:5 + j + length, :], 0, keepdims=True)
        back = w[3:4] * grad
        for j in range(KERNEL - 1):
            back = back + w[j:j + 1] * gext[3 - j:3 - j + length, :]
        gp_ref[:, at] = jnp.where(valid, back, 0.0).astype(bf16)


def mixer_backward(gm, o, q, k, t, e, s_c, projected, conv_w, gain, nv):
    length = gm.shape[0]
    heads, nc = t.shape[:2]
    hb = 1
    groups = heads // hb
    w = hb * HD
    tok = pl.BlockSpec((length, w), lambda i, *_: (0, i))
    sq = pl.BlockSpec((hb, nc, HD, HD), lambda i, *_: (i, 0, 0, 0))
    col = lambda off: (lambda i, *_: (0, i + off * groups))
    fixed = lambda shape: pl.BlockSpec(shape, lambda i, *_: (0, 0))
    in_specs = [tok, tok, tok, tok, sq, tok, sq, pl.BlockSpec((length, HD), lambda i, *_: (0, 3 * heads))]
    in_specs += [pl.BlockSpec((length, w), col(n)) for n in range(3)]
    in_specs += [pl.BlockSpec((KERNEL, w), col(n)) for n in range(3)]
    in_specs += [fixed((1, HD))]
    wide = (length, pl.cdiv((3 * heads + 1) * HD, 256) * 256)
    return pl.pallas_call(
        functools.partial(mixer_backward_kernel, hb, heads),
        out_shape=(
            jax.ShapeDtypeStruct(wide, bf16),
            jax.ShapeDtypeStruct((KERNEL, 3 * heads * HD), f32),
            jax.ShapeDtypeStruct((8, HD), f32),
        ),
        grid_spec=pltpu.PrefetchScalarGridSpec(
            num_scalar_prefetch=1, grid=(groups,), in_specs=in_specs,
            out_specs=(fixed(wide), fixed((KERNEL, 3 * heads * HD)), fixed((8, HD))),
            scratch_shapes=[pltpu.VMEM((length + 8, w), f32), pltpu.VMEM((length + 8, w), f32)]),
        name="mixer_backward",
    )(nv, gm, o, q, k, t, e, s_c, projected, projected, projected, projected, conv_w, conv_w, conv_w, gain)


def xor(value, axis, step):
    return lax.ppermute(value, axis, [(i, i ^ step) for i in range(lax.axis_size(axis))])


def pick(tensor, index, axis=0):
    return lax.dynamic_index_in_dim(tensor, index, axis, keepdims=False)


def added(a, b):
    return (a.astype(f32) + b.astype(f32)).astype(bf16)


def direct():
    return (lax.axis_size("dp"), lax.axis_size("fsdp"), lax.axis_size("ctx")) == (4, 4, 2)


def mixer_columns(weight, heads):
    n = lax.axis_size("ctx")
    view = weight.reshape(weight.shape[0], 3, heads // n, n, HD)
    return pick(view, lax.axis_index("ctx"), 3).reshape(weight.shape[0], -1)


def beta_columns(weight, heads):
    n = lax.axis_size("ctx")
    view = weight.reshape(weight.shape[0], heads // n, n)
    return jnp.pad(pick(view, lax.axis_index("ctx"), 2), ((0, 0), (0, HD - heads // n)))


def feed_columns(weight):
    n = lax.axis_size("ctx")
    view = weight.reshape(weight.shape[0], 2, n, weight.shape[1] // (2 * n))
    return pick(view, lax.axis_index("ctx"), 2).reshape(weight.shape[0], -1)


def after(value, *others):
    return lax.optimization_barrier((value,) + others)


def start_pieces(tags, places, sources, outs, sems, z, d):
    copies = []
    for tag in tags:
        source, at_first, row_step, same, other = tag
        for at, index, row, col in places(tag, z ^ row_step, other if same else d ^ other):
            rows, width = (s.stop - s.start for s in at)
            target = outs[index].at[pl.ds(row, rows), pl.ds(col, width)]
            copy = pltpu.make_async_copy(
                sources[source].at[at_first + at], target, sems.at[len(copies)]
            )
            copy.start()
            copies.append(copy)
    return copies


def positions():
    return jnp.stack([lax.axis_index(a) for a in ("fsdp", "dp", "ctx")]).astype(jnp.int32)


def project_kernel(tags, places, count, where_ref, x_own, x_far, gain, *refs):
    sources = refs[:count]
    normed_ref, out_ref, full_ref, weight, sems, out_sem = refs[count:]
    step, steps = pl.program_id(0), pl.num_programs(0)
    z, d, c = where_ref[0], where_ref[1], where_ref[2]
    kept = pltpu.make_async_copy(weight, full_ref, out_sem)

    @pl.when(step == 0)
    def _():
        for copy in start_pieces(tags, places, sources, (weight,), sems, z, d):
            copy.wait()
        kept.start()

    x = jnp.where(step == c, x_own[...], x_far[...]).astype(f32)
    scale = lax.rsqrt(jnp.mean(x * x, -1, keepdims=True) + 1e-06)
    normed = (x * scale * gain[...]).astype(bf16)
    normed_ref[...] = normed
    out_ref[...] = dot(normed, weight[...])

    @pl.when(step == steps - 1)
    def _():
        kept.wait()


def project(x_own, x_far, gain, pieces, width):
    arrays, tags, places = pieces
    rows, depth = x_own.shape
    half = pl.BlockSpec((rows, depth), lambda i, *_: (0, 0))
    each = lambda w: pl.BlockSpec((rows, w), lambda i, *_: (i, 0))
    anywhere = pl.BlockSpec(memory_space=pl.ANY)
    return pl.pallas_call(
        functools.partial(project_kernel, tags, places, len(arrays)),
        out_shape=(
            jax.ShapeDtypeStruct((2 * rows, depth), bf16),
            jax.ShapeDtypeStruct((2 * rows, width), f32),
            jax.ShapeDtypeStruct((depth, width), bf16),
        ),
        grid_spec=pltpu.PrefetchScalarGridSpec(
            num_scalar_prefetch=1,
            grid=(2,),
            in_specs=[half, half, pl.BlockSpec((1, depth), lambda i, *_: (0, 0))]
            + [anywhere] * len(arrays),
            out_specs=(each(depth), each(width), anywhere),
            scratch_shapes=[
                pltpu.VMEM((depth, width), bf16),
                pltpu.SemaphoreType.DMA((len(tags),)),
                pltpu.SemaphoreType.DMA,
            ],
        ),
        name="projections",
    )(positions(), x_own, x_far, gain, *arrays)


def near_first(i, where):
    return ((where[2] + i) % 2, 0)


def attend_kernel(tags, places, count, where_ref, merged, *refs):
    sources = refs[:count]
    near, far, full_ref, weight, sems, out_sem = refs[count:]
    step, steps = pl.program_id(0), pl.num_programs(0)
    z, d = where_ref[0], where_ref[1]
    kept = pltpu.make_async_copy(weight, full_ref, out_sem)

    @pl.when(step == 0)
    def _():
        for copy in start_pieces(tags, places, sources, (weight,), sems, z, d):
            copy.wait()
        kept.start()

    total = dot(merged[...], weight[...])

    @pl.when(step == 0)
    def _():
        near[...] = total

    @pl.when(step == 1)
    def _():
        far[...] = total.astype(bf16)

    @pl.when(step == steps - 1)
    def _():
        kept.wait()


def near_spec(block, width):
    return pl.BlockSpec((block, width), lambda i, *_: (0, 0))


def far_spec(block, width):
    return pl.BlockSpec((block, width), lambda i, *_: (0, 0))


def attend(merged, pieces, width):
    arrays, tags, places = pieces
    rows, depth = merged.shape
    block = rows // 2
    anywhere = pl.BlockSpec(memory_space=pl.ANY)
    return pl.pallas_call(
        functools.partial(attend_kernel, tags, places, len(arrays)),
        out_shape=(
            jax.ShapeDtypeStruct((rows // 2, width), f32),
            jax.ShapeDtypeStruct((rows // 2, width), bf16),
            jax.ShapeDtypeStruct((depth, width), bf16),
        ),
        grid_spec=pltpu.PrefetchScalarGridSpec(
            num_scalar_prefetch=1,
            grid=(2,),
            in_specs=[pl.BlockSpec((block, depth), near_first)] + [anywhere] * len(arrays),
            out_specs=(near_spec(block, width), far_spec(block, width), anywhere),
            scratch_shapes=[
                pltpu.VMEM((depth, width), bf16),
                pltpu.SemaphoreType.DMA((2 * len(tags),)),
                pltpu.SemaphoreType.DMA,
            ],
        ),
        name="mixer_out",
    )(positions(), merged, *arrays)


def merged_grad_kernel(where_ref, own, far, weight, out):
    grad = jnp.where(pl.program_id(0) == 0, own[...], far[...])
    out[...] = dot_nt(grad, weight[...])


def merged_grad(own, far, weight):
    rows, width = own.shape
    depth = weight.shape[0]
    block = rows
    return pl.pallas_call(
        merged_grad_kernel,
        out_shape=jax.ShapeDtypeStruct((2 * rows, depth), f32),
        grid_spec=pltpu.PrefetchScalarGridSpec(
            num_scalar_prefetch=1,
            grid=(2,),
            in_specs=[
                near_spec(block, width),
                far_spec(block, width),
                pl.BlockSpec((depth, width), lambda i, *_: (0, 0)),
            ],
            out_specs=pl.BlockSpec((block, depth), near_first),
        ),
        name="merged_gradient",
    )(positions(), own, far, weight)


def normed_grad_kernel(where_ref, grad, weight, near, far):
    total = dot_nt(grad[...], weight[...])

    @pl.when(pl.program_id(0) == 0)
    def _():
        near[...] = total

    @pl.when(pl.program_id(0) == 1)
    def _():
        far[...] = total.astype(bf16)


def normed_grad(grad, weight):
    rows, (depth, width) = grad.shape[0], weight.shape
    block = rows // 2
    return pl.pallas_call(
        normed_grad_kernel,
        out_shape=(
            jax.ShapeDtypeStruct((rows // 2, depth), f32),
            jax.ShapeDtypeStruct((rows // 2, depth), bf16),
        ),
        grid_spec=pltpu.PrefetchScalarGridSpec(
            num_scalar_prefetch=1,
            grid=(2,),
            in_specs=[
                pl.BlockSpec((block, width), near_first),
                pl.BlockSpec((depth, width), lambda i, *_: (0, 0)),
            ],
            out_specs=(near_spec(block, depth), far_spec(block, depth)),
        ),
        name="normed_gradient",
    )(positions(), grad, weight)


def keep_and_send(total, where_ref, refs, col):
    low_keep, low_send, high_keep, high_send = refs
    first_low, first_high = where_ref[1] % 2 == 0, where_ref[1] // 2 == 0
    short = total.shape[0] // 32
    block = lambda i: total[i * short : (i + 1) * short]
    for z in range(2):
        for i in range(4):
            a, b = block(8 * z + 2 * i), block(8 * z + 2 * i + 1)
            low_keep[i % 2, z, i // 2, col, :] = jnp.where(first_low, a, b)
            low_send[i % 2, z, i // 2, col, :] = jnp.where(first_low, b, a)
            k = 16 + 8 * z + (i // 2) * 4 + i % 2
            a, b = block(k), block(k + 2)
            high_keep[i % 2, z, i // 2, col, :] = jnp.where(first_high, a, b)
            high_send[i % 2, z, i // 2, col, :] = jnp.where(first_high, b, a)


def weight_grad_kernel(parts, steps, where_ref, *refs):
    lefts, grad = refs[:parts], refs[parts]
    turned = refs[-1]
    step = pl.program_id(0)
    c = where_ref[2]

    @pl.when(step == 0)
    def _():
        at = 0
        for left in lefts:
            rows = left.shape[0]
            turned[:, at : at + rows] = left[...].T
            at += rows

    if len(refs) == parts + 6:
        every = slice(None)
        keep_and_send(dot(turned[...], grad[...]).astype(bf16), where_ref, refs[-5:-1], every)
        return

    merged, own, far = refs[parts + 1 : parts + 4]
    outs = refs[-5:-1]

    @pl.when(step < steps)
    def _():
        keep_and_send(dot(turned[...], grad[...]).astype(bf16), where_ref, outs, slice(None))

    @pl.when(step >= steps)
    def _():
        rows, half = own.shape[0], own.shape[1] // 2
        mine = merged[pl.ds(pl.multiple_of(c * rows, rows), rows), :]
        theirs = merged[pl.ds(pl.multiple_of((1 - c) * rows, rows), rows), :]
        width = outs[0].shape[-1]
        for k in range(2):
            at = pl.ds(pl.multiple_of(k * half + (step - steps) * width, width), width)
            part = (dot_tn(mine, own[:, at]) + dot_tn(theirs, far[:, at])).astype(bf16)
            lines = part.shape[0] // 32
            keep_and_send(part, where_ref, outs, slice(k * lines, (k + 1) * lines))


def weight_grad(lefts, grad, out=()):
    depth = lefts[0].shape[1]
    rows = sum(a.shape[0] for a in lefts)
    block = 256
    steps = pl.cdiv(grad.shape[1], block)
    more = out[1].shape[1] // 2 if out else 0
    shape = jax.ShapeDtypeStruct((2, 2, 2, depth // 32, grad.shape[1] + more), bf16)
    each = pl.BlockSpec((2, 2, 2, depth // 32, block), lambda i, *_: (0, 0, 0, 0, i))
    whole = lambda a: pl.BlockSpec(a.shape, lambda i, *_: (0, 0))
    specs = [whole(a) for a in lefts]
    specs += [pl.BlockSpec((rows, block), lambda i, *_: (0, jnp.minimum(i, steps - 1)))]
    specs += [whole(a) for a in out]
    return pl.pallas_call(
        functools.partial(weight_grad_kernel, len(lefts), steps),
        out_shape=(shape,) * 4,
        grid_spec=pltpu.PrefetchScalarGridSpec(
            num_scalar_prefetch=1,
            grid=(steps + more // block,),
            in_specs=specs,
            out_specs=(each,) * 4,
            scratch_shapes=[pltpu.VMEM((depth, rows), bf16)],
        ),
        name="weight_gradient",
    )(positions(), *lefts, grad, *out)


def down_grad_kernel(hidden, own, far, out, turned):
    rows = own.shape[0]

    @pl.when(pl.program_id(0) == 0)
    def _():
        turned[...] = hidden[...].T

    total = dot(turned[:, :rows], own[...]) + dot(turned[:, rows:], far[...])
    out[...] = total.astype(bf16)


def down_gradient(hidden, own, far):
    rows, width = own.shape
    half = hidden.shape[1]
    block = 256
    return pl.pallas_call(
        down_grad_kernel,
        out_shape=jax.ShapeDtypeStruct((half, width), bf16),
        grid=(width // block,),
        in_specs=[
            pl.BlockSpec((2 * rows, half), lambda i: (0, 0)),
            pl.BlockSpec((rows, block), lambda i: (0, i)),
            pl.BlockSpec((rows, block), lambda i: (0, i)),
        ],
        out_specs=pl.BlockSpec((half, block), lambda i: (0, i)),
        scratch_shapes=[pltpu.VMEM((half, 2 * rows), bf16)],
        name="down_gradient",
    )(hidden, own, far)


def whole_rows(weight):
    return lax.all_gather(weight, "fsdp", axis=0, tiled=True)


def exchange(blocks, axis):
    return lax.all_to_all(blocks, axis, 0, 0, tiled=True)


def to_all(piece, axis):
    return exchange(jnp.broadcast_to(piece, (lax.axis_size(axis),) + piece.shape), axis)


def bounds(total, step):
    return [slice(i, min(i + step, total)) for i in range(0, total, step)]


def feed_kernel(tags, places, count_down, own, where_ref, x_own, x_other, e_own, e_other, *refs):
    count = 1 + max(t[0] for t in tags)
    sources, downs = refs[:count], refs[count : count + count_down]
    hidden_ref, grad_ref, near_out, far_out, near_grad, far_grad = refs[count + count_down : -3]
    gateup, down, sems = refs[-3:]
    step = pl.program_id(0)
    z, d, c = where_ref[0], where_ref[1], where_ref[2]

    @pl.when(step == 0)
    def _():
        copies = start_pieces(tags, places, sources, (gateup,), sems, z, d)
        rows, cols = downs[1].shape[1:]
        for j in range(2):
            for source, at, first in ((downs[0], 2 * c + j, c), (downs[1], j, 1 - c)):
                col = pl.multiple_of(first * cols, HD)
                copy = pltpu.make_async_copy(
                    source.at[at],
                    down.at[pl.ds(j * rows, rows), pl.ds(col, cols)],
                    sems.at[len(copies)],
                )
                copy.start()
                copies.append(copy)
        for copy in copies:
            copy.wait()

    near = step < own
    x = jnp.where(near, x_own[...], x_other[...])
    e = jnp.where(near, e_own[...], e_other[...])
    half = down.shape[0]
    for j in bounds(half, 256):
        up_j = slice(half + j.start, half + j.stop)
        gate = dot(x, gateup[:, j])
        up = dot(x, gateup[:, up_j])
        grad = dot_nt(e, down[j, :])
        sig = jax.nn.sigmoid(gate)
        act = gate * sig
        hidden_ref[:, j] = (act * up).astype(bf16)
        grad_ref[:, j] = (grad * up * sig * (1.0 + gate * (1.0 - sig))).astype(bf16)
        grad_ref[:, up_j] = (grad * act).astype(bf16)
    out = dot(hidden_ref[...], down[...])
    back = dot_nt(grad_ref[...], gateup[...])

    @pl.when(near)
    def _():
        near_out[...] = out
        near_grad[...] = back

    @pl.when(jnp.logical_not(near))
    def _():
        far_out[...] = out.astype(bf16)
        far_grad[...] = back.astype(bf16)


def feed(x_own, x_other, e_own, e_other, wide, down):
    arrays, tags, places = wide
    rows, width = x_own.shape
    others = x_other.shape[0]
    half = 2 * down[1].shape[1]
    block = min(256, rows)
    own, steps = rows // block, (rows + others) // block
    near = lambda w: pl.BlockSpec((block, w), lambda i, *_: (jnp.minimum(i, own - 1), 0))
    far = lambda w: pl.BlockSpec((block, w), lambda i, *_: (jnp.maximum(i - own, 0), 0))
    each = lambda w: pl.BlockSpec((block, w), lambda i, *_: (i, 0))
    anywhere = pl.BlockSpec(memory_space=pl.ANY)
    return pl.pallas_call(
        functools.partial(feed_kernel, tags, places, len(down), own),
        out_shape=(
            jax.ShapeDtypeStruct((rows + others, half), bf16),
            jax.ShapeDtypeStruct((rows + others, 2 * half), bf16),
            jax.ShapeDtypeStruct((rows, width), f32),
            jax.ShapeDtypeStruct((others, width), bf16),
            jax.ShapeDtypeStruct((rows, width), f32),
            jax.ShapeDtypeStruct((others, width), bf16),
        ),
        grid_spec=pltpu.PrefetchScalarGridSpec(
            num_scalar_prefetch=1,
            grid=(steps,),
            in_specs=[near(width), far(width), near(width), far(width)]
            + [anywhere] * (len(arrays) + len(down)),
            out_specs=(each(half), each(2 * half), near(width), far(width), near(width), far(width)),
            scratch_shapes=[
                pltpu.VMEM((width, 2 * half), bf16),
                pltpu.VMEM((half, width), bf16),
                pltpu.SemaphoreType.DMA((4 + len(tags),)),
            ],
        ),
        name="feed_forward",
    )(positions(), x_own, x_other, e_own, e_other, *arrays, *down)


def pack_kernel(heads, where_ref, qkv, beta, out, gateup, mixed_ref, wide_ref, every):
    rows = qkv.shape[0]
    strips = qkv.shape[1] // (2 * HD)
    mixed = (strips + 1) * HD
    width = gateup.shape[1] // 4
    half = out.shape[1] // 2
    short = out.shape[0]
    for c in range(2):

        @pl.when(where_ref[1] == c)
        def _():
            for i in range(strips):
                at = (2 * i + c) * HD
                mixed_ref[:, i * HD : (i + 1) * HD] = qkv[:, at : at + HD]
            source = lax.broadcasted_iota(jnp.int32, (heads, HD), 0)
            lane = lax.broadcasted_iota(jnp.int32, (heads, HD), 1)
            chosen = (source == 2 * lane + c).astype(f32).astype(bf16)
            every[...] = dot_tn(beta[...], chosen)
            here = pl.ds(pl.multiple_of(where_ref[0] * rows, rows), rows)
            mixed_ref[:, strips * HD : mixed] = every[here, :].astype(bf16)
            for i in range(2):
                at = (2 * i + c) * width
                wide_ref[0, :, i * width : (i + 1) * width] = gateup[:, at : at + width]

    wide_ref[0, :short, 2 * width :] = out[:, :half]
    wide_ref[0, short:, 2 * width :] = out[:, half:]
    for i in range(1, 4):
        wide_ref[i] = wide_ref[0]


def pack(w_qkv, w_beta, w_out, w_gateup):
    rows, short = w_qkv.shape[0] // 4, HD // 4
    heads = w_beta.shape[1]
    here = jnp.stack([lax.axis_index("dp"), lax.axis_index("ctx")]).astype(jnp.int32)
    mixed = w_qkv.shape[1] // 2 + HD
    wide = w_gateup.shape[1] // 2 + w_out.shape[1] // 2
    fixed = lambda *shape: pl.BlockSpec(shape, lambda i, *_: (0,) * len(shape))
    mine = lambda width: pl.BlockSpec((rows, width), lambda i, at: (at[0], 0))
    shapes = ((rows, mixed), (4, rows, wide))
    return pl.pallas_call(
        functools.partial(pack_kernel, heads),
        out_shape=tuple(jax.ShapeDtypeStruct(s, bf16) for s in shapes),
        grid_spec=pltpu.PrefetchScalarGridSpec(
            num_scalar_prefetch=1,
            grid=(1,),
            in_specs=[
                mine(w_qkv.shape[1]),
                pl.BlockSpec(w_beta.shape[::-1], lambda i, *_: (0, 0)),
                pl.BlockSpec((short, w_out.shape[1]), lambda i, at: (at[1] * 4 + at[0], 0)),
                mine(w_gateup.shape[1]),
            ],
            out_specs=tuple(fixed(*s) for s in shapes),
            scratch_shapes=[pltpu.VMEM((w_beta.shape[0], HD), f32)],
        ),
        name="weight_pieces",
    )(here, w_qkv, w_beta.T, w_out, w_gateup)


def gather_direct(mixed_piece, wide_piece, down_shard):
    z, c = lax.axis_index("fsdp"), lax.axis_index("ctx")
    own = [mixed_piece] + [xor(mixed_piece, "dp", k) for k in (1, 2, 3)]
    rows = [xor(mixed_piece, "fsdp", k) for k in (1, 2, 3)]
    wide_piece, *got = after(wide_piece, *own[1:], *rows)
    own[1:], rows = got[:3], got[3:]
    wide_own = [wide_piece[0]] + [xor(wide_piece[0], "dp", k) for k in (1, 2, 3)]
    wide_rows = exchange(wide_piece, "fsdp")
    rows, *wide_own[1:] = after(jnp.stack(rows), *wide_own[1:])
    rest = [rows] + [xor(rows, "dp", k) for k in (1, 2, 3)]
    half = down_shard.shape[1] // 2
    mine = lax.dynamic_slice_in_dim(down_shard, c * half, half, 1)
    tags = [(k, (), 0, False, k) for k in range(4)]
    tags += [(4 + i, (k - 1,), k, False, i) for i in range(4) for k in (1, 2, 3)]
    return own + rest, tags, wide_own, wide_rows, mine


def spread_first(own, wide_rows, mine):
    z = lax.axis_index("fsdp")
    half = wide_rows.shape[2] // 2
    low = jnp.stack([pick(wide_rows, z ^ k)[:, :half] for k in (1, 2, 3)])
    high = jnp.stack([pick(wide_rows, z ^ k)[:, half:] for k in (1, 2, 3)])
    low, high = [low, xor(low, "dp", 1)], [high, xor(high, "dp", 2)]
    mine, wide_rows = after(mine, wide_rows)
    return own, low, high, to_all(mine, "fsdp")


def spread_second(full, own, low, high):
    full, low[1], high[1] = after(full, low[1], high[1])
    low = low + [xor(low[0], "dp", 2), xor(low[1], "dp", 2)]
    high = [high[0], xor(high[0], "dp", 1), high[1], xor(high[1], "dp", 1)]
    tags = [(k, (), 0, False, k) for k in range(4)]
    tags += [(4 + i, (k - 1,), k, False, i) for i in range(4) for k in (1, 2, 3)]
    tags += [(8 + i, (k - 1,), k, False, i) for i in range(4) for k in (1, 2, 3)]
    return full, own + low + high, tags


def gather_weights(w_qkv, w_beta, w_out, w_gateup, w_down, heads):
    n, c = lax.axis_size("ctx"), lax.axis_index("ctx")
    if not direct():
        mixed = jnp.concatenate([mixer_columns(w_qkv, heads), beta_columns(w_beta, heads)], 1)
        out = whole_rows(w_out).reshape(heads // n, n, HD, -1)
        down = whole_rows(w_down)
        return (
            whole_rows(mixed),
            whole_rows(feed_columns(w_gateup)),
            pick(out, c, 1).reshape(-1, w_out.shape[1]),
            pick(down.reshape(n, -1, down.shape[1]), c),
        )
    rows, short = w_qkv.shape[0] // 4, HD // 4
    mixed_piece, wide_piece = pack(w_qkv, w_beta, w_out, w_gateup)
    mixed, width, half = mixed_piece.shape[1], w_gateup.shape[1] // 2, w_out.shape[1] // 2
    mixed_all, mixed_tags, own, wide_rows, mine = gather_direct(mixed_piece, wide_piece, w_down)
    cut = (width + half) // 2

    def mixed_places(tag, z, d):
        row = pl.multiple_of(z * (4 * rows) + d * rows, rows)
        return [((slice(0, rows), slice(0, mixed)), 0, row, 0)]

    def out_places(tag, z, d):
        row = pl.multiple_of(z * HD + d * short, short)
        first = width if tag[0] < 4 else width - cut
        at = slice(first, first + half)
        return [
            ((slice(0, short), at), 0, row, 0),
            ((slice(short, 2 * short), at), 0, row, half),
        ]

    def feed_places(tag, z, d):
        row = pl.multiple_of(z * (4 * rows) + d * rows, rows)
        if tag[0] < 4:
            at, col = slice(0, width), 0
        elif tag[0] < 8:
            at, col = slice(0, cut), 0
        else:
            at, col = slice(0, width - cut), cut
        return [((slice(0, rows), at), 0, row, col)]

    spread = spread_first(own, wide_rows, mine)

    def further(full):
        full, wide_all, wide_tags = spread_second(full, *spread[:3])
        out_tags = [t for t in wide_tags if not 4 <= t[0] < 8]
        wide = wide_all, wide_tags, feed_places
        return full, wide, (wide_all, out_tags, out_places), spread[3]

    return (mixed_all, mixed_tags, mixed_places), further


def feed_both(normed, grad_feed, gateup, down):
    if direct():
        normed_far, grad_far = xor(normed, "ctx", 1), xor(grad_feed, "ctx", 1)
        theirs = pick(down.reshape((2, 2) + down.shape[1:]), 1 - lax.axis_index("ctx"))
        down = [down, xor(theirs, "ctx", 1)]
        hidden, grad, out, out_far, back, back_far = feed(
            normed, normed_far, grad_feed, grad_far, gateup, down
        )
        out = out + xor(out_far, "ctx", 1).astype(f32)
        back = back + xor(back_far, "ctx", 1).astype(f32)
        return (normed, normed_far), (grad_feed, grad_far), hidden, grad, out, back
    normed, grad_feed = both_pieces(normed), both_pieces(grad_feed)
    gate_up = jnp.dot(normed, gateup, preferred_element_type=f32)
    ff_width = gate_up.shape[1] // 2
    gate_part = gate_up[:, :ff_width]
    up_part = gate_up[:, ff_width:]
    gate_sig = jax.nn.sigmoid(gate_part)
    hidden = (gate_part * gate_sig * up_part).astype(bf16)
    contract_cols = (((1,), (1,)), ((), ()))
    grad_hidden = lax.dot_general(grad_feed, down, contract_cols, preferred_element_type=f32)
    grad_gate = grad_hidden * up_part * gate_sig * (1.0 + gate_part * (1.0 - gate_sig))
    grad = jnp.concatenate([grad_gate, grad_hidden * gate_part * gate_sig], 1).astype(bf16)
    out = own_piece(jnp.dot(hidden, down, preferred_element_type=f32))
    back = own_piece(lax.dot_general(grad, gateup, contract_cols, preferred_element_type=f32))
    return normed, grad_feed, hidden, grad, out, back


def both_pieces(mine):
    n = lax.axis_size("ctx")
    if n != 2:
        return lax.all_gather(mine, "ctx", axis=0, tiled=True)
    other = xor(mine, "ctx", 1)
    first = lax.axis_index("ctx") == 0
    return jnp.concatenate([jnp.where(first, mine, other), jnp.where(first, other, mine)], 0)


def own_piece(partial):
    n = lax.axis_size("ctx")
    rows = partial.shape[0] // n
    if n != 2:
        return lax.psum_scatter(
            partial.astype(bf16), "ctx", scatter_dimension=0, tiled=True
        ).astype(f32)
    here = lax.axis_index("ctx")
    theirs = lax.dynamic_slice_in_dim(partial, (1 - here) * rows, rows, 0).astype(bf16)
    mine = lax.dynamic_slice_in_dim(partial, here * rows, rows, 0)
    return mine.astype(f32) + xor(theirs, "ctx", 1).astype(f32)


def replicas_first(part):
    d = lax.axis_index("dp")
    high, low = d // 2, d % 2
    a, b = part[:2], part[2:]
    got = xor(pick(a, 1 - low, 3), "dp", 1), xor(pick(b, 1 - high, 2), "dp", 2)
    return (pick(a, low, 3), pick(b, high, 2)), got


def halves_kernel(where_ref, *refs):
    for i in range(4):
        total = refs[2 * i][0].astype(f32) + refs[2 * i + 1][0].astype(f32)
        refs[8 + i][...] = total.astype(bf16)


def replicas_second(kept, got):
    shape = kept[0].shape[1:]
    block = (1, 1) + shape[1:]
    zeros = (0,) * (len(shape) - 1)
    high = lambda i, at: (at[1] // 2, i) + zeros
    not_high = lambda i, at: (1 - at[1] // 2, i) + zeros
    low = lambda i, at: (at[1] % 2, i) + zeros
    not_low = lambda i, at: (1 - at[1] % 2, i) + zeros
    specs, arrays = [], []
    for k, maps in ((0, (high, not_high)), (1, (low, not_low))):
        for chosen in maps:
            specs += [pl.BlockSpec(block, chosen)] * 2
            arrays += [kept[k], got[k]]
    outs = pl.pallas_call(
        halves_kernel,
        out_shape=(jax.ShapeDtypeStruct(shape, bf16),) * 4,
        grid_spec=pltpu.PrefetchScalarGridSpec(
            num_scalar_prefetch=1,
            grid=(2,),
            in_specs=specs,
            out_specs=(pl.BlockSpec((1,) + shape[1:], lambda i, *_: (i,) + zeros),) * 4,
        ),
        name="first_sums",
    )(positions(), *arrays)
    return (outs[0], outs[2]), (outs[1], outs[3])


def over_replicas(kept, got):
    return jnp.concatenate([added(kept[0], got[0]), added(kept[1], got[1])], 0)


def sent_kernel(where_ref, more, a_kept, a_got, b_kept, b_got, *outs):
    step = pl.program_id(0)
    a = a_kept[0].astype(f32) + a_got[0].astype(f32)
    b = b_kept[0].astype(f32) + b_got[0].astype(f32)
    total = jnp.where((where_ref[0] ^ step) < 2, a, b).astype(bf16)
    width = total.shape[2]
    for k in range(4):

        @pl.when(step == k)
        def _():
            outs[k][:, :, :width] = total
            outs[k][:, :, width:] = more[...]


def sent_rows(kept, got, more):
    shape = kept[0].shape[1:]
    zeros = (0,) * len(shape)
    a = pl.BlockSpec((1,) + shape, lambda i, at: (jnp.minimum(at[0] ^ i, 1),) + zeros)
    b = pl.BlockSpec((1,) + shape, lambda i, at: (jnp.maximum((at[0] ^ i) - 2, 0),) + zeros)
    wider = shape[:2] + (shape[2] + more.shape[2],)
    return pl.pallas_call(
        sent_kernel,
        out_shape=(jax.ShapeDtypeStruct(wider, bf16),) * 4,
        grid_spec=pltpu.PrefetchScalarGridSpec(
            num_scalar_prefetch=1,
            grid=(4,),
            in_specs=[pl.BlockSpec(more.shape, lambda i, *_: zeros), a, a, b, b],
            out_specs=(pl.BlockSpec(wider, lambda i, *_: zeros),) * 4,
        ),
        name="sums_sent",
    )(positions(), more, kept[0], got[0], kept[1], got[1])


def summed_pairs(own, got):
    own, *got = (part.astype(f32) for part in (own, *got))
    return (own + got[0]) + (got[1] + got[2])


def both_columns(part):
    c = lax.axis_index("ctx")
    other = xor(pick(part, 1 - c), "ctx", 1)
    mine = pick(part, c)
    first = c == 0
    return jnp.stack([jnp.where(first, mine, other), jnp.where(first, other, mine)])


def finish_kernel(moves, count, where_ref, *refs):
    sources, outs = refs[:count], refs[count:]
    d = where_ref[1]
    for source, at, index, to in moves:
        if len(to) == 4:
            row = pl.multiple_of((d ^ to[0]) * to[1] + to[2], to[1])
            to = (pl.ds(row, to[1]), to[3])
        elif len(to) == 3:
            if isinstance(to[0], int):
                to = (pl.ds(pl.multiple_of((d ^ to[0]) * to[1], to[1]), to[1]), to[2])
            else:
                to = (to[0], pl.ds(pl.multiple_of((d ^ to[1]) * to[2], HD), to[2]))
        outs[index][to] = sources[source][at].astype(f32)


def finish(sources, moves, shapes, name):
    whole = lambda shape: pl.BlockSpec(shape, lambda i, *_: (0,) * len(shape))
    return pl.pallas_call(
        functools.partial(finish_kernel, moves, len(sources)),
        out_shape=tuple(jax.ShapeDtypeStruct(s, f32) for s in shapes),
        grid_spec=pltpu.PrefetchScalarGridSpec(
            num_scalar_prefetch=1,
            grid=(1,),
            in_specs=[whole(s.shape) for s in sources],
            out_specs=tuple(whole(s) for s in shapes),
        ),
        name=name,
    )(positions(), *sources)


def blocks_of(grad, n, z):
    return grad.reshape(z, n, 2, 2, grad.shape[0] // (4 * z * n), grad.shape[1])


def scattered(full):
    share = lax.psum_scatter(full.astype(bf16), ("fsdp", "ctx"), scatter_dimension=0, tiled=True)
    return lax.psum(share, "dp").astype(f32)


def placed_at_ctx(part, axis):
    n = lax.axis_size("ctx")
    shape = [1] * (part.ndim + 1)
    shape[axis] = n
    here = (jnp.arange(n) == lax.axis_index("ctx")).reshape(shape)
    return jnp.where(here, jnp.expand_dims(part, axis), 0)


def sum_columns(grad, views, widths):
    outs, start = [], 0
    for shape, size in zip(views, widths):
        part = grad[:, start : start + size].reshape((grad.shape[0],) + shape)
        full = placed_at_ctx(part, part.ndim - 1)
        outs.append(scattered(full.reshape(grad.shape[0], -1)))
        start += size
    return outs


def added_up(parts):
    total = parts[0].astype(f32)
    for i in range(1, parts.shape[0]):
        total = total + parts[i].astype(f32)
    return total.astype(bf16)


def quarter(part, k):
    cols = part.shape[1] // 4
    return lax.dynamic_slice_in_dim(part, (lax.axis_index("dp") ^ k) * cols, cols, 1)


def down_to_owners(part):
    pairs = [(z * 2 + c, (2 * c + z // 2) * 2 + z % 2) for z in range(4) for c in range(2)]
    return lax.ppermute(part, ("fsdp", "ctx"), pairs)


def local(
    inputs,
    lengths,
    cotangent,
    norm_gain1,
    w_qkv,
    w_beta,
    conv_weight,
    head_gain,
    w_out,
    norm_gain2,
    w_gateup,
    w_down,
):
    n = lax.axis_size("ctx")
    heads_all = w_beta.shape[1]
    heads = heads_all // n
    tokens_in = inputs[0].astype(f32)
    piece_len, model_width = tokens_in.shape
    length = piece_len * n
    conv_mine = mixer_columns(conv_weight, heads_all)
    positions_here = jnp.arange(length, dtype=jnp.int32)
    start = lax.axis_index("ctx") * piece_len
    valid = ((start + positions_here[:piece_len]) < lengths[0]).astype(f32)[:, None]
    grad_feed = (cotangent[0].astype(f32) * valid).astype(bf16)
    if direct():
        pieces, further = gather_weights(w_qkv, w_beta, w_out, w_gateup, w_down, heads_all)
        far_rows = xor(inputs[0], "ctx", 1)
        normed_one, projected, mixed = project(
            inputs[0], far_rows, norm_gain1[None], pieces, (3 * heads + 1) * HD
        )
        projected, gateup, out, down = further(projected)
    else:
        mixed, gateup, out, down = gather_weights(
            w_qkv, w_beta, w_out, w_gateup, w_down, heads_all
        )
        tokens_all = both_pieces(inputs[0]).astype(f32)
        scale_all = lax.rsqrt(jnp.mean(tokens_all * tokens_all, -1, keepdims=True) + 1e-06)
        normed_one = (tokens_all * scale_all * norm_gain1).astype(bf16)
        projected = jnp.dot(normed_one, mixed, preferred_element_type=f32)
    queries, keys, inverse, errors, states, heads_out, merged = mixer_forward(
        projected, conv_mine, head_gain[None], lengths, heads
    )
    if direct():
        near, far, out = attend(merged, out, model_width)
        attention = near + xor(far, "ctx", 1).astype(f32)
    else:
        attention = own_piece(jnp.dot(merged, out, preferred_element_type=f32))
    middle = tokens_in + attention
    scale_two = lax.rsqrt(jnp.mean(middle * middle, -1, keepdims=True) + 1e-06)
    normed_two = (middle * scale_two * norm_gain2).astype(bf16)
    normed_two, feed_all, hidden, grad_gate_up, feed_out, grad_normed_two = feed_both(
        normed_two, grad_feed, gateup, down
    )
    output = (middle + feed_out).astype(bf16)
    contract_cols = (((1,), (1,)), ((), ()))
    contract_rows = (((0,), (0,)), ((), ()))
    ff_width = hidden.shape[1]
    if direct():
        down_grad = down_gradient(hidden, *feed_all)
        grad_gate_up, down_grad = after(grad_gate_up, down_grad)
        down_got = exchange(down_grad.reshape(4, down_grad.shape[0] // 4, -1), "fsdp")
        low_kept, low_sent, high_kept, high_sent = weight_grad(normed_two, grad_gate_up)
        wide_kept = low_kept, high_kept
        wide_got = xor(low_sent, "dp", 1), xor(high_sent, "dp", 2)
        grad_normed_two, low_sent = after(grad_normed_two, low_sent)
    else:
        down_grad = lax.dot_general(
            hidden, feed_all, contract_rows, preferred_element_type=f32
        ).astype(bf16)
        gateup_grad = lax.dot_general(
            normed_two, grad_gate_up, contract_rows, preferred_element_type=f32
        ).astype(bf16)
    gain_two_term = jnp.sum(grad_normed_two * middle * scale_two, 0)
    scaled_two = grad_normed_two * norm_gain2
    grad_middle = (
        grad_feed.astype(f32)
        + scale_two * scaled_two
        - scale_two
        * scale_two
        * scale_two
        * middle
        * jnp.mean(scaled_two * middle, -1, keepdims=True)
    )
    grad_attention = grad_middle.astype(bf16)
    if direct():
        grad_far = xor(grad_attention, "ctx", 1)
        grad_merged = merged_grad(grad_attention, grad_far, out)
    else:
        grad_attention = both_pieces(grad_attention)
        out_grad = lax.dot_general(
            merged, grad_attention, contract_rows, preferred_element_type=f32
        ).astype(bf16)
        grad_merged = lax.dot_general(
            grad_attention, out, contract_cols, preferred_element_type=f32
        )
    grad_mixed, conv_term, gain_rows = mixer_backward(
        grad_merged, heads_out, queries, keys, inverse, errors, states,
        projected, conv_mine, head_gain[None], lengths,
    )
    if direct():
        grad_mixed, *wide_got = after(grad_mixed, *wide_got)
        wide_kept, wide_sent = replicas_second(wide_kept, wide_got)
        grad_mixed, *wide_sent = after(grad_mixed, *wide_sent)
        wide_got = xor(wide_sent[0], "dp", 2), xor(wide_sent[1], "dp", 1)
        low_kept, low_sent, high_kept, high_sent = weight_grad(
            (normed_one,), grad_mixed, (merged, grad_attention, grad_far)
        )
        mixed_kept = low_kept, high_kept
        mixed_got = xor(low_sent, "dp", 1), xor(high_sent, "dp", 2)
        grad_mixed, low_kept = after(grad_mixed, mixed_kept[0])
        mixed_kept = low_kept, mixed_kept[1]
        near, far = normed_grad(grad_mixed, mixed)
        near, far, down_got, *wide_got = after(near, far, down_got, *wide_got)
        wide = exchange(over_replicas(wide_kept, wide_got), "fsdp")
        down_part = added_up(down_got)
        near, *mixed_got = after(near, *mixed_got)
        grad_normed_one = near + xor(far, "ctx", 1).astype(f32)
        mixed_kept, mixed_sent = replicas_second(mixed_kept, mixed_got)
        mixed_got = xor(mixed_sent[0], "dp", 2), xor(mixed_sent[1], "dp", 1)
    else:
        mixed_grad = lax.dot_general(
            normed_one, grad_mixed, contract_rows, preferred_element_type=f32
        ).astype(bf16)
        grad_normed_one = own_piece(
            lax.dot_general(grad_mixed, mixed, contract_cols, preferred_element_type=f32)
        )
        (gateup_total,) = sum_columns(gateup_grad, [(2, ff_width)], [2 * ff_width])
        down_total = scattered(placed_at_ctx(down_grad, 0).reshape(-1, model_width))
        view = placed_at_ctx(out_grad.reshape(heads, HD, model_width), 1)
        out_total = scattered(view.reshape(-1, model_width))
        views, widths = [(3, heads, HD), (1, heads, 1)], [3 * heads * HD, heads]
        qkv_total, beta_total = sum_columns(mixed_grad, views, widths)
    scale_one = lax.rsqrt(jnp.mean(tokens_in * tokens_in, -1, keepdims=True) + 1e-06)
    gain_one_term = jnp.sum(grad_normed_one * tokens_in * scale_one, 0)

    def input_gradient(grad_normed_one):
        scaled_one = grad_normed_one * norm_gain1
        total = (
            grad_middle
            + scale_one * scaled_one
            - scale_one
            * scale_one
            * scale_one
            * tokens_in
            * jnp.mean(scaled_one * tokens_in, -1, keepdims=True)
        )
        return total.astype(bf16)

    conv_term = placed_at_ctx(conv_term.reshape(KERNEL, 3, heads, HD), 3)
    small = jnp.concatenate([gain_one_term, gain_two_term, gain_rows[0], conv_term.reshape(-1)], 0)
    cuts = [model_width, 2 * model_width, 2 * model_width + HD]
    if direct():
        small = small + xor(small, "ctx", 1)
        size, lines, cols = small.shape[0], mixed_kept[0].shape[2], model_width // 4
        assert size <= n * lines * cols
        small = jnp.pad(small, (0, n * lines * cols - size)).reshape(n * lines, cols).astype(bf16)
        part = [jnp.concatenate([quarter(down_part, k), small], 0) for k in range(4)]
        down_got = [xor(part[k], "dp", k) for k in (1, 2, 3)]
        part, *got = after(part[0], *mixed_got, *down_got)
        mixed_got, down_got = got[:2], got[2:]
        part = summed_pairs(part, down_got).astype(bf16)
        down_mine, small = part[: -n * lines], part[-n * lines :]
        mixed_parts = sent_rows(mixed_kept, mixed_got, small.reshape(n, lines, cols))
        wide, down_mine, *mixed_parts = after(wide, down_mine, *mixed_parts)
        down_mine = down_to_owners(down_mine)
        mixed_got = [xor(mixed_parts[k], "fsdp", k) for k in (1, 2, 3)]
        wide = added_up(wide)
        feed_part = both_columns(wide)
        count = down_mine.shape[0] // lines
        each = pl.cdiv(count, n)
        down_part = jnp.pad(down_mine, ((0, (n * each - count) * lines), (0, 0)))
        down_part = jnp.transpose(down_part.reshape(n, each, lines, cols), (0, 2, 1, 3))
        down_part = down_part.reshape(n, lines, each * cols)
        wide = jnp.concatenate([feed_part, down_part], 2)
        wide = to_all(wide, "dp")
        ready = after(mixed_parts[0], grad_normed_one, *mixed_got)
        mixed_mine, grad_normed_one, *mixed_got = ready
        grad_tokens = input_gradient(grad_normed_one)
        total = summed_pairs(mixed_mine, mixed_got)
        strip, half = (3 * heads + 1) * HD, model_width // 2
        both = both_columns(total[..., :strip].astype(bf16))
        both = jnp.concatenate([both, total[..., -cols - half : -cols].astype(bf16)], 2)
        both = [both] + [xor(both, "dp", k) for k in (1, 2, 3)]
        small_total = total[..., -cols:].reshape(-1)[:size]
        short, rows = wide.shape[2], HD // (4 * n)
        moves = []
        for i in range(4):
            for j in range(n):
                lines = slice(i * short, (i + 1) * short)
                for k in range(2):
                    at = slice(k * ff_width, (k + 1) * ff_width)
                    to = (k * n + j) * ff_width
                    moves.append((0, (i, j, slice(None), at), 0, (lines, slice(to, to + ff_width))))
            first = 2 * ff_width
            for m in range(count):
                at = slice(first + (m % each) * cols, first + (m % each + 1) * cols)
                to = slice(m * short, (m + 1) * short), slice(i * cols, (i + 1) * cols)
                moves.append((0, (i, m // each, slice(None), at), 1, to))
        shapes = [(4 * short, 2 * n * ff_width), (down_mine.shape[0], 4 * cols)]
        gateup_total, down_total = finish([wide], moves, shapes, "wide_totals")
        ready = after(both[0], *both[1:], gateup_total, down_total)
        both, (gateup_total, down_total) = list(ready[:4]), ready[4:]
        moves = []
        for i in range(4):
            for j in range(n):
                for k in range(3 * heads):
                    at = (j, slice(None), slice(k * HD, (k + 1) * HD))
                    to = (k * n + j) * HD
                    moves.append((i, at, 0, (i, short, slice(to, to + HD))))
                at = (j, slice(None), slice(3 * heads * HD, strip))
                moves.append((i, at, 1, (i, short, slice(j * HD, (j + 1) * HD))))
                for k in range(2):
                    at = (j, slice(k * rows, (k + 1) * rows), slice(strip, None))
                    to = (i, rows, j * 4 * rows, slice(k * half, (k + 1) * half))
                    moves.append((i, at, 2, to))
        shapes = [(4 * short, 3 * heads_all * HD), (4 * short, n * HD)]
        shapes += [(4 * n * rows, model_width)]
        qkv_total, beta_total, out_total = finish(both, moves, shapes, "mixed_totals")
        beta_total = beta_total.reshape(4 * short, n, HD)[:, :, :heads]
        beta_total = jnp.transpose(beta_total, (0, 2, 1)).reshape(4 * short, heads_all)
    else:
        small_total = lax.psum(small, ("dp", "fsdp", "ctx"))
        grad_tokens = input_gradient(grad_normed_one)
    gain_one, gain_two, gain_head, conv_total = jnp.split(small_total, cuts)
    return (
        output[None],
        grad_tokens[None],
        gain_one,
        qkv_total,
        beta_total,
        conv_total.reshape(conv_weight.shape),
        gain_head,
        out_total,
        gain_two,
        gateup_total,
        down_total,
    )


def solution(mesh):
    placed = (
        P(("dp", "fsdp"), "ctx", None),
        P(("dp", "fsdp")),
        P(("dp", "fsdp"), "ctx", None),
        P(),
        P("fsdp", None),
        P("fsdp", None),
        P(),
        P(),
        P("fsdp", None),
        P(),
        P("fsdp", None),
        P("fsdp", None),
    )
    return jax.shard_map(
        local,
        mesh=mesh,
        in_specs=placed,
        out_specs=(
            P(("dp", "fsdp"), "ctx", None),
            P(("dp", "fsdp"), "ctx", None),
            P(),
            P(("fsdp", "ctx"), None),
            P(("fsdp", "ctx"), None),
            P(),
            P(),
            P(("fsdp", "ctx"), None),
            P(),
            P(("fsdp", "ctx"), None),
            P(("fsdp", "ctx"), None),
        ),
        check_vma=False,
    )
```
